256 devices in a mesh: dp: 4 (over y), seq: 64 (over z, x, core).
Axes of the slice: x: 4, y: 4, z: 8, core: 2. Of those that a mesh axis runs over, the one named last changes fastest.
Arguments:
- queries: bfloat16 [4, 8192, 1024], P('dp', 'seq'), may hold values from -6 to 6
- keys: bfloat16 [4, 8192, 1024], P('dp', 'seq'), may hold values from -6 to 6
- values: bfloat16 [4, 8192, 1024], P('dp', 'seq'), may hold values from -6 to 6
- gates: bfloat16 [4, 8192, 1024], P('dp', 'seq'), may hold values from -6 to 6
- cotangent: bfloat16 [4, 8192, 1024], P('dp', 'seq'), may hold values from -16 to 16
- segment: int32 [4, 8192], P('dp'), may hold values from 0 to 31, never falling along the last dimension, each value on 1 to 1024 neighbouring positions
- w_out: bfloat16 [1024, 1024], replicated, may hold values from -0.1875 to 0.1875
Outputs:
- output: bfloat16 [4, 8192, 1024], P('dp', 'seq')
- grad_queries: bfloat16 [4, 8192, 1024], P('dp', 'seq')
- grad_keys: bfloat16 [4, 8192, 1024], P('dp', 'seq')
- grad_values: bfloat16 [4, 8192, 1024], P('dp', 'seq')
- grad_gates: bfloat16 [4, 8192, 1024], P('dp', 'seq')
- grad_w_out: float32 [1024, 1024], P(('dp', 'seq'))
The draws below stay inside these ranges and needn't reach their ends.
Inputs may be any that keep to these rules, and one draw needn't show every extreme that they name: `segment`: within each replica the user numbers never fall along the tokens; every user has 1 to 1024 tokens, and one user has exactly 1024.
All inputs are finite; a program needn't handle non-finite values.
Results may differ from the reference program's by a relative error of at most 0.0058.
Values may be sent and summed in bfloat16 or wider, within the bound.
No kernel may reach another device: no remote copies, remote signals or barrier semaphores. Data moves between devices by JAX's collectives and lax.ppermute only.
A program may use at most 128 MiB of HBM per device.

```python
import math
import jax
import jax.numpy as jnp
import numpy as np
from jax import lax

HEADS = 8
WIDTH = 1024
TOK_DEV = 128
LMAX = 1024
HOPS = 8
COUNT = 32
SEQ_TOKENS = 8192
N_DP = 4


def spiked(values, rng, source, target, shards_of, factor):
    owner, partner = [(jnp.arange(values.shape[position]) // (values.shape[position] // shards_of)).reshape([-1 if axis == position else 1 for axis in range(values.ndim)]) for position in (source, target)]
    chosen = jax.random.permutation(rng, shards_of)[partner]
    strong = (owner == chosen) | (owner == (partner + shards_of // 2) % shards_of)
    return jnp.where(strong, factor * values, values)


def levels(stream_key, extent, pieces, least, top_value):
    def one(dim, parts):
        draws = jax.random.uniform(jax.random.fold_in(jax.random.fold_in(stream_key, 6), dim), (parts,), jnp.float32, least / len(pieces), top_value / len(pieces))
        return jnp.repeat(jnp.exp(draws), extent[dim] // parts).reshape((-1,) + (1,) * (len(extent) - dim - 1))

    level = one(*pieces[0])
    for cut in pieces[1:]:
        level = level * one(*cut)
    return level


def length_profile(number_of, total, most, slope):
    portions = [(1 << 20) // math.isqrt(rank ** slope) + 1 for rank in range(2, number_of + 1)]
    rest, holding = total - most - (number_of - 1), [1] * (number_of - 1)
    while rest > 0:
        movable = [i for i in range(number_of - 1) if holding[i] < most]
        mass, remaining = sum([portions[i] for i in movable]), rest
        for i in movable:
            extra = min(most - holding[i], max(1, remaining * portions[i] // mass), rest)
            holding[i] = holding[i] + extra
            rest = rest - extra
    return np.array([most] + holding)


def uneven_parts(rng, number_of, total, most, skew):
    if number_of == 2:
        one = jax.random.randint(rng, (), max(1, total - most), min(most, total - 1) + 1)
        return jnp.stack([one, total - one])
    tallies = jnp.asarray(length_profile(number_of, total, most, skew), jnp.int32)
    couples = (number_of - 1) // 2
    donor, receiver = tallies[1:1 + 2 * couples:2], tallies[2:2 + 2 * couples:2]
    room = jnp.minimum(donor - 1, most - receiver)
    moved = jax.random.randint(jax.random.fold_in(rng, 1), (couples,), 0, 1 << 20) % (room + 1)
    tallies = tallies.at[1:1 + 2 * couples:2].set(donor - moved).at[2:2 + 2 * couples:2].set(receiver + moved)
    return tallies[jax.random.permutation(jax.random.fold_in(rng, 2), number_of)]


def bell_draw(rng, dims, deviation, bound, pieces=(), held_as=jnp.bfloat16):
    array = jax.random.normal(rng, dims, jnp.float32) * deviation
    if len(pieces) > 0:
        array = levels(rng, dims, pieces, -0.22, 0.18) * array
    return jnp.clip(array, min=-bound, max=bound).astype(held_as)


def heavy_noise(rng, extent, scale, reach, pieces, heavy, held_as=jnp.bfloat16):
    values = scale * jax.random.normal(rng, extent, jnp.float32)
    if pieces:
        values = values * levels(rng, extent, pieces, -0.22, 0.18)
    return jnp.clip(spiked(values, jax.random.fold_in(rng, 3), *heavy), -reach, reach).astype(held_as)


def setup_inputs(seed: int = 0) -> dict:
    key_list = jax.random.split(jax.random.key(seed), 8)
    queries = bell_draw(key_list[0], (N_DP, SEQ_TOKENS, WIDTH), 1.0, 6.0, ((0, 4), (1, 64)))
    keys = bell_draw(key_list[1], (N_DP, SEQ_TOKENS, WIDTH), 1.0, 6.0, ((0, 4), (1, 64)))
    values = bell_draw(key_list[2], (N_DP, SEQ_TOKENS, WIDTH), 1.0, 6.0, ((0, 4), (1, 64)))
    gates = bell_draw(key_list[3], (N_DP, SEQ_TOKENS, WIDTH), 1.0, 6.0, ((0, 4), (1, 64)))
    cotangent = heavy_noise(key_list[4], (N_DP, SEQ_TOKENS, WIDTH), 1.0, 16.0, ((0, 4), (1, 64)), (1, 2, 64, 4.0))
    segment = jax.vmap(lambda own: jnp.searchsorted(jnp.cumsum(uneven_parts(own, COUNT, SEQ_TOKENS, LMAX, 2)), jnp.arange(SEQ_TOKENS), side="right"))(jax.random.split(key_list[5], N_DP)).reshape((N_DP, SEQ_TOKENS)).astype(jnp.int32)
    w_out = bell_draw(key_list[6], (WIDTH, WIDTH), WIDTH ** -0.5, 0.1875)
    return dict(queries=queries, keys=keys, values=values, gates=gates, cotangent=cotangent, segment=segment, w_out=w_out)


EPS = 1e-05

def silu_slope(scores):
    sigmoid_value = jax.nn.sigmoid(scores)
    return sigmoid_value * (1.0 + scores * (1.0 - sigmoid_value))

def block_pass(query_rows, gate_rows, cotan_rows, w_out, key_rows, value_rows, allowed):
    row_count, features = query_rows.shape
    head_size = features // HEADS
    score_scale = 1.0 / math.sqrt(head_size)
    query_heads = query_rows.astype(jnp.float32).reshape(row_count, HEADS, head_size)
    key_heads = key_rows.astype(jnp.float32).reshape(-1, HEADS, head_size)
    value_heads = value_rows.astype(jnp.float32).reshape(-1, HEADS, head_size)
    scores = jnp.einsum('qhd,khd->hqk', query_heads, key_heads) * score_scale
    weights = jnp.where(allowed[None], jax.nn.silu(scores), 0.0).astype(jnp.bfloat16)
    mixed = jnp.einsum('hqk,khd->qhd', weights.astype(jnp.float32), value_heads).reshape(row_count, features)
    row_mean = lax.optimization_barrier(jnp.mean(mixed, axis=-1, keepdims=True))
    centred = mixed - row_mean
    inverse = lax.rsqrt(lax.optimization_barrier(jnp.mean(centred * centred, axis=-1, keepdims=True)) + EPS)
    normed = centred * inverse
    gate_float = gate_rows.astype(jnp.float32)
    gated = (normed * gate_float).astype(jnp.bfloat16)
    output_rows = jnp.dot(gated, w_out, preferred_element_type=jnp.float32).astype(jnp.bfloat16)
    dgated = jnp.dot(cotan_rows, w_out.T, preferred_element_type=jnp.float32)
    grad_gate_rows = (dgated * normed).astype(jnp.bfloat16)
    dnormed = dgated * gate_float
    dmixed = inverse * (dnormed - lax.optimization_barrier(jnp.mean(dnormed, axis=-1, keepdims=True)) - normed * lax.optimization_barrier(jnp.mean(dnormed * normed, axis=-1, keepdims=True)))
    dmixed = dmixed.astype(jnp.bfloat16)
    dmixed_heads = dmixed.astype(jnp.float32).reshape(row_count, HEADS, head_size)
    dweights = jnp.einsum('qhd,khd->hqk', dmixed_heads, value_heads)
    dscores = jnp.where(allowed[None], dweights * silu_slope(scores) * score_scale, 0.0).astype(jnp.bfloat16)
    dvalue_rows = jnp.einsum('hqk,qhd->khd', weights.astype(jnp.float32), dmixed_heads).reshape(-1, features)
    dquery_rows = jnp.einsum('hqk,khd->qhd', dscores.astype(jnp.float32), key_heads).reshape(row_count, features)
    dkey_rows = jnp.einsum('hqk,qhd->khd', dscores.astype(jnp.float32), query_heads).reshape(-1, features)
    weight_part = jnp.dot(gated.T, cotan_rows, preferred_element_type=jnp.float32)
    return (output_rows, dquery_rows.astype(jnp.bfloat16), grad_gate_rows, dkey_rows, dvalue_rows, weight_part)

def reference(queries, keys, values, gates, cotangent, segment, w_out):
    groups, total_rows, features = queries.shape
    reach_rows = HOPS * TOK_DEV
    key_count = reach_rows + TOK_DEV
    block_total = total_rows // TOK_DEV

    def one_group(arrays):
        query_all, key_all, value_all, gate_all, cotan_all, segment_ids = arrays
        keys_padded = jnp.concatenate([jnp.zeros((reach_rows, features), jnp.bfloat16), key_all])
        values_padded = jnp.concatenate([jnp.zeros((reach_rows, features), jnp.bfloat16), value_all])
        segment_padded = jnp.concatenate([jnp.full((reach_rows,), -1, jnp.int32), segment_ids])

        def block_step(running, block_index):
            dkey_acc, dvalue_acc, weight_acc = running
            block_start = (block_index * TOK_DEV).astype(jnp.int32)
            query_rows = lax.dynamic_slice_in_dim(query_all, block_start, TOK_DEV)
            gate_rows = lax.dynamic_slice_in_dim(gate_all, block_start, TOK_DEV)
            cotan_rows = lax.dynamic_slice_in_dim(cotan_all, block_start, TOK_DEV)
            key_rows = lax.dynamic_slice_in_dim(keys_padded, block_start, key_count)
            value_rows = lax.dynamic_slice_in_dim(values_padded, block_start, key_count)
            key_segment = lax.dynamic_slice_in_dim(segment_padded, block_start, key_count)
            query_segment = lax.dynamic_slice_in_dim(segment_ids, block_start, TOK_DEV)
            query_place = block_start + jnp.arange(TOK_DEV, dtype=jnp.int32)
            key_place = block_start - reach_rows + jnp.arange(key_count, dtype=jnp.int32)
            allowed = (query_segment[:, None] == key_segment[None, :]) & (key_place[None, :] <= query_place[:, None])
            output_rows, dquery_rows, grad_gate_rows, dkey_rows, dvalue_rows, weight_part = block_pass(query_rows, gate_rows, cotan_rows, w_out, key_rows, value_rows, allowed)
            dkey_acc = lax.dynamic_update_slice_in_dim(dkey_acc, lax.dynamic_slice_in_dim(dkey_acc, block_start, key_count) + dkey_rows, block_start, 0)
            dvalue_acc = lax.dynamic_update_slice_in_dim(dvalue_acc, lax.dynamic_slice_in_dim(dvalue_acc, block_start, key_count) + dvalue_rows, block_start, 0)
            return ((dkey_acc, dvalue_acc, weight_acc + weight_part), (output_rows, dquery_rows, grad_gate_rows))
        start_state = (jnp.zeros((total_rows + reach_rows, features), jnp.float32), jnp.zeros((total_rows + reach_rows, features), jnp.float32), jnp.zeros((features, features), jnp.float32))
        final_state, stacked = lax.scan(block_step, start_state, jnp.arange(block_total, dtype=jnp.int32))
        dkey_acc, dvalue_acc, weight_acc = final_state
        output_all = stacked[0].reshape(total_rows, features)
        dquery_all = stacked[1].reshape(total_rows, features)
        dgate_all = stacked[2].reshape(total_rows, features)
        return (output_all, dquery_all, dkey_acc[reach_rows:].astype(jnp.bfloat16), dvalue_acc[reach_rows:].astype(jnp.bfloat16), dgate_all, weight_acc)
    results = lax.map(one_group, (queries, keys, values, gates, cotangent, segment))
    return (results[0], results[1], results[2], results[3], results[4], lax.optimization_barrier(jnp.sum(results[5], axis=0)))
```

```python
import functools
import math

import jax
import jax.numpy as jnp
from jax import lax
from jax.experimental import pallas as pl
from jax.experimental.pallas import tpu as pltpu
from jax.sharding import Mesh
from jax.sharding import PartitionSpec as P

HEADS = 8
EPS = 1e-05
USERS = 32
TOK = 128
PLANE = 1024
TILE = 256
TILES = PLANE // TILE
SCALE = 1.0 / math.sqrt(128.0)
F32 = jnp.float32
BF16 = jnp.bfloat16
PLANE_AXES = ("x", "c")
VMEM_LIMIT = 48 * 1024 * 1024

NN = (((1,), (0,)), ((), ()))
NT = (((1,), (1,)), ((), ()))
TN = (((0,), (0,)), ((), ()))


def dot(a, b, dims=NN):
    return lax.dot_general(a, b, dims, preferred_element_type=F32)


def flip(block):
    return block.astype(F32).T.astype(BF16)


def call(body, outs, flops, moved, scratch=(), smem=0, ins=0):
    vmem = pl.BlockSpec(memory_space=pltpu.VMEM)
    specs = [pl.BlockSpec(memory_space=pltpu.SMEM)] * smem + [vmem] * (ins - smem)
    many = isinstance(outs, (list, tuple))
    return pl.pallas_call(
        body,
        out_shape=outs,
        in_specs=specs,
        out_specs=[vmem] * len(outs) if many else vmem,
        scratch_shapes=list(scratch),
        compiler_params=pltpu.CompilerParams(vmem_limit_bytes=VMEM_LIMIT),
        cost_estimate=pl.CostEstimate(flops=flops, bytes_accessed=moved, transcendentals=0),
    )


def shape(dims, dtype):
    return jax.ShapeDtypeStruct(dims, dtype)


def pack_body(q_ref, k_ref, v_ref, out_ref):
    for h in range(HEADS):
        cols = slice(h * TOK, (h + 1) * TOK)
        out_ref[h, 0:128, :] = q_ref[:, cols]
        out_ref[h, 128:256, :] = k_ref[:, cols]
        out_ref[h, 256:384, :] = v_ref[:, cols]


def dgated_body(cot_ref, gate_ref, w_ref, out_ref):
    cot = cot_ref[...]
    for h in range(HEADS):
        cols = slice(h * TOK, (h + 1) * TOK)
        out_ref[h, 0:128, :] = flip(gate_ref[:, cols])
        out_ref[h, 128:256, :] = dot(w_ref[cols, :], cot, NT).astype(BF16)


def tile_of(ref, j, rows):
    return ref[pl.ds(2 * j, 2), rows, :].reshape(TILE, 128)


def tile_mask(start_ref, i, first_key):
    start = jnp.concatenate([start_ref[2 * i : 2 * i + 1, :], start_ref[2 * i + 1 : 2 * i + 2, :]], axis=1)
    key_place = first_key + lax.broadcasted_iota(jnp.int32, (TILE, TILE), 0)
    query_place = i * TILE + lax.broadcasted_iota(jnp.int32, (TILE, TILE), 1)
    return (key_place >= start) & (key_place <= query_place)


def sigmoid(s):
    return 1.0 / (1.0 + jnp.exp(-s))


def forward_tiles(i, low, high, first, keys_ref, key_rows, start_ref, qt, vt_ref, total):
    def step(j, acc):
        s = dot(tile_of(keys_ref, j, key_rows), qt) * SCALE
        mask = tile_mask(start_ref, i, first + j * TILE)
        w = jnp.where(mask, s * sigmoid(s), 0.0).astype(BF16)
        return acc + dot(vt_ref[j], w)

    return lax.fori_loop(low, high, step, total)


def fwd_own_body(low_ref, recv_ref, start_ref, mixt_ref, qt_ref, vt_ref):
    for t in range(HEADS):
        qt_ref[:, t * TOK : (t + 1) * TOK] = flip(recv_ref[t, 0:128, :])
        vt_ref[t // 2, :, (t % 2) * TOK : (t % 2 + 1) * TOK] = flip(recv_ref[t, 256:384, :])
    for i in range(TILES):
        cols = slice(i * TILE, (i + 1) * TILE)
        low = jnp.maximum(low_ref[i] - TILES, 0)
        mixt_ref[:, cols] = forward_tiles(
            i, low, i + 1, 0, recv_ref, slice(128, 256), start_ref, qt_ref[:, cols], vt_ref, jnp.zeros((128, TILE), F32)
        )


def fwd_halo_body(low_ref, halo_ref, start_ref, qt_ref, part_ref, gd_ref, mixt_ref, stats_ref, vt_ref):
    for t in range(HEADS):
        vt_ref[t // 2, :, (t % 2) * TOK : (t % 2 + 1) * TOK] = flip(halo_ref[t, 128:256, :])
    for i in range(TILES):
        cols = slice(i * TILE, (i + 1) * TILE)
        mixt_ref[:, cols] = forward_tiles(
            i, low_ref[i], TILES, -PLANE, halo_ref, slice(0, 128), start_ref, qt_ref[:, cols], vt_ref, part_ref[:, cols]
        )
    for b in range(HEADS):
        mix = mixt_ref[:, b * TOK : (b + 1) * TOK]
        dn = gd_ref[b, 0:128, :].astype(F32) * gd_ref[b, 128:256, :].astype(F32)
        mean = jnp.sum(mix, axis=0, keepdims=True) * (1.0 / 128.0)
        centred = mix - mean
        rows = (
            mean,
            jnp.sum(centred * centred, axis=0, keepdims=True),
            jnp.sum(dn, axis=0, keepdims=True),
            jnp.sum(dn * centred, axis=0, keepdims=True),
        )
        for k, row in enumerate(rows):
            stats_ref[0, 8 * k + b : 8 * k + b + 1, :] = row
    for d in range(1, HEADS):
        stats_ref[d] = stats_ref[0]


def finish_body(mixt_ref, gd_ref, stats_ref, gated_ref, gg_ref, dmix_ref):
    means = [stats_ref[h, 0:8, :] for h in range(HEADS)]
    mean = sum(means) * (1.0 / HEADS)
    square = sum(stats_ref[h, 8:16, :] for h in range(HEADS))
    square = square + 128.0 * sum((m - mean) * (m - mean) for m in means)
    inverse = lax.rsqrt(square * (1.0 / 1024.0) + EPS)
    dmean = sum(stats_ref[h, 16:24, :] for h in range(HEADS)) * (1.0 / 1024.0)
    cross = sum(stats_ref[h, 24:32, :] + (means[h] - mean) * stats_ref[h, 16:24, :] for h in range(HEADS))
    dcross = cross * inverse * (1.0 / 1024.0)
    for b in range(HEADS):
        cols = slice(b * TOK, (b + 1) * TOK)
        one = slice(b, b + 1)
        inv = inverse[one, :]
        normed = (mixt_ref[:, cols] - mean[one, :]) * inv
        gate = gd_ref[b, 0:128, :].astype(F32)
        dgated = gd_ref[b, 128:256, :].astype(F32)
        gated_ref[:, cols] = (normed * gate).astype(BF16)
        gg_ref[:, cols] = (normed * dgated).astype(BF16)
        dmix_ref[:, cols] = (inv * (dgated * gate - dmean[one, :] - normed * dcross[one, :])).astype(BF16)


def weight_body(gated_ref, cot_ref, out_ref):
    total = dot(gated_ref[:, 0:TOK], cot_ref[0])
    for b in range(1, HEADS):
        total = total + dot(gated_ref[:, b * TOK : (b + 1) * TOK], cot_ref[b])
    out_ref[...] = total.astype(BF16)


def backward_tiles(i, low, high, first, keys_ref, key_rows, value_rows, start_ref, qt, q, dmt, kt_ref, dk_ref, dv_ref, total):
    def step(j, acc):
        s = dot(tile_of(keys_ref, j, key_rows), qt) * SCALE
        mask = tile_mask(start_ref, i, first + j * TILE)
        sig = sigmoid(s)
        w = jnp.where(mask, s * sig, 0.0).astype(BF16)
        dw = dot(tile_of(keys_ref, j, value_rows), dmt)
        ds = jnp.where(mask, dw * (sig * (1.0 + s * (1.0 - sig))) * SCALE, 0.0).astype(BF16)
        dv_ref[j] += dot(w, dmt, NT)
        dk_ref[j] += dot(ds, q)
        return acc + dot(kt_ref[j], ds)

    return lax.fori_loop(low, high, step, total)


def bwd_halo_body(low_ref, halo_ref, recv_ref, start_ref, qt_ref, dmix_ref, dqt_ref, out_ref, kt_ref, dk_ref, dv_ref):
    for t in range(HEADS):
        kt_ref[t // 2, :, (t % 2) * TOK : (t % 2 + 1) * TOK] = flip(halo_ref[t, 0:128, :])
    dk_ref[...] = jnp.zeros_like(dk_ref)
    dv_ref[...] = jnp.zeros_like(dv_ref)
    for i in range(TILES):
        cols = slice(i * TILE, (i + 1) * TILE)
        dqt_ref[:, cols] = backward_tiles(
            i, low_ref[i], TILES, -PLANE, halo_ref, slice(0, 128), slice(128, 256), start_ref, qt_ref[:, cols],
            tile_of(recv_ref, i, slice(0, 128)), dmix_ref[:, cols], kt_ref, dk_ref, dv_ref, jnp.zeros((128, TILE), F32),
        )
    for j in range(TILES):
        out_ref[2 * j : 2 * j + 2, 0:128, :] = dk_ref[j].astype(BF16).reshape(2, 128, 128)
        out_ref[2 * j : 2 * j + 2, 128:256, :] = dv_ref[j].astype(BF16).reshape(2, 128, 128)


def bwd_own_body(low_ref, recv_ref, start_ref, qt_ref, dmix_ref, part_ref, dq_ref, dk_ref, dv_ref, kt_ref):
    for t in range(HEADS):
        kt_ref[t // 2, :, (t % 2) * TOK : (t % 2 + 1) * TOK] = flip(recv_ref[t, 128:256, :])
    dk_ref[...] = jnp.zeros_like(dk_ref)
    dv_ref[...] = jnp.zeros_like(dv_ref)
    for i in range(TILES):
        cols = slice(i * TILE, (i + 1) * TILE)
        low = jnp.maximum(low_ref[i] - TILES, 0)
        dqt = backward_tiles(
            i, low, i + 1, 0, recv_ref, slice(128, 256), slice(256, 384), start_ref, qt_ref[:, cols],
            tile_of(recv_ref, i, slice(0, 128)), dmix_ref[:, cols], kt_ref, dk_ref, dv_ref, part_ref[:, cols],
        )
        dq_ref[i] = dqt.T.astype(BF16)


def gather_body(gated_ref, gg_ref, dq_ref, dk_ref, dv_ref, next_ref, out_ref):
    for b in range(HEADS):
        cols = slice(b * TOK, (b + 1) * TOK)
        rows = slice((b % 2) * TOK, (b % 2 + 1) * TOK)
        out_ref[b, 0:128, :] = gated_ref[:, cols]
        out_ref[b, 128:256, :] = gg_ref[:, cols]
        out_ref[b, 256:384, :] = dq_ref[b // 2, rows, :]
        out_ref[b, 384:512, :] = (dk_ref[b // 2, rows, :] + next_ref[b, 0:128, :].astype(F32)).astype(BF16)
        out_ref[b, 512:640, :] = (dv_ref[b // 2, rows, :] + next_ref[b, 128:256, :].astype(F32)).astype(BF16)


def final_body(recv_ref, w_ref, out_ref, dq_ref, dk_ref, dv_ref, gg_ref):
    total = jnp.zeros((TOK, 1024), F32)
    for h in range(HEADS):
        cols = slice(h * TOK, (h + 1) * TOK)
        total = total + dot(flip(recv_ref[h, 0:128, :]), w_ref[cols, :])
        gg_ref[:, cols] = flip(recv_ref[h, 128:256, :])
        dq_ref[:, cols] = recv_ref[h, 256:384, :]
        dk_ref[:, cols] = recv_ref[h, 384:512, :]
        dv_ref[:, cols] = recv_ref[h, 512:640, :]
    out_ref[...] = total.astype(BF16)


def plane_exchange(blocks):
    return lax.all_to_all(blocks, PLANE_AXES, 0, 0, tiled=True)


def shards(sizes, queries, keys, values, gates, cotangent, segment, w_out):
    dp, planes = sizes
    q, k, v, gate, cot, seg = (a[0] for a in (queries, keys, values, gates, cotangent, segment))
    cot_plane = lax.all_gather(cot, PLANE_AXES)

    packed = call(pack_body, shape((8, 384, 128), BF16), 1 << 16, 3 << 19, ins=3)(q, k, v)
    recv = plane_exchange(packed)

    place = lax.axis_index("z") * PLANE
    users = jnp.arange(USERS, dtype=jnp.int32)[:, None]
    first = jnp.sum((seg[None, :] < users).astype(jnp.int32), axis=1)
    mine = lax.dynamic_slice_in_dim(seg, place, PLANE)
    start = jnp.sum(jnp.where(mine[None, :] == users, first[:, None], 0), axis=0) - place
    low = (start[::TILE] + PLANE) // TILE
    start = start.reshape(8, 128)

    gd = call(dgated_body, shape((8, 256, 128), BF16), 1 << 28, 3 << 20, ins=3)(cot, gate, w_out)
    gd_recv = plane_exchange(gd)

    halo = lax.ppermute(recv[:, 128:384], "z", [(i, i + 1) for i in range(planes - 1)])
    vt = pltpu.VMEM((TILES, 128, TILE), BF16)
    acc = pltpu.VMEM((TILES, TILE, 128), F32)
    part, qt = call(
        fwd_own_body, [shape((128, PLANE), F32), shape((128, PLANE), BF16)], 1 << 29, 1 << 21, [vt], smem=1, ins=3
    )(low, recv, start)
    mixt, stats = call(
        fwd_halo_body, [shape((128, PLANE), F32), shape((8, 32, 128), F32)], 1 << 28, 1 << 21, [vt], smem=1, ins=6
    )(low, halo, start, qt, part, gd_recv)
    stats = plane_exchange(stats)
    gated, gg, dmix = call(finish_body, [shape((128, PLANE), BF16)] * 3, 1 << 22, 1 << 21, ins=3)(mixt, gd_recv, stats)

    partial = call(weight_body, shape((128, 1024), BF16), 1 << 28, 5 << 19, ins=2)(gated, cot_plane)
    shares = lax.all_to_all(partial, ("dp", "z"), 0, 0, tiled=True).reshape(dp * planes, 4, 1024)
    summed = jnp.sum(shares.astype(F32), axis=0)
    route = []
    for d in range(dp):
        for z in range(planes):
            for r in range(8):
                rows = 128 * r + 4 * (d * planes + z)
                route.append(((d * planes + z) * 8 + r, rows // 4))
    weight_grad = lax.ppermute(summed, ("dp", "z", "x", "c"), route)

    dqt, back = call(
        bwd_halo_body, [shape((128, PLANE), F32), shape((8, 256, 128), BF16)], 1 << 29, 1 << 21, [vt, acc, acc], smem=1, ins=6
    )(low, halo, recv, start, qt, dmix)
    back = lax.ppermute(back, "z", [(i, i - 1) for i in range(1, planes)])
    dq, dk, dv = call(
        bwd_own_body,
        [shape((TILES, TILE, 128), BF16), shape((TILES, TILE, 128), F32), shape((TILES, TILE, 128), F32)],
        1 << 30, 1 << 22, [vt], smem=1, ins=6,
    )(low, recv, start, qt, dmix, dqt)
    sent = call(gather_body, shape((8, 640, 128), BF16), 1 << 20, 1 << 22, ins=6)(gated, gg, dq, dk, dv, back)
    got = plane_exchange(sent)
    rows = shape((TOK, 1024), BF16)
    out, dq, dk, dv, gg = call(final_body, [rows] * 5, 1 << 28, 5 << 20, ins=2)(got, w_out)
    return out[None], dq[None], dk[None], dv[None], gg[None], weight_grad


def solution(mesh):
    dp, seq = mesh.shape["dp"], mesh.shape["seq"]
    planes = seq // 8
    grid = Mesh(mesh.devices.reshape(dp, planes, 4, 2), ("dp", "z", "x", "c"))
    tokens = P("dp", ("z", "x", "c"), None)
    return jax.shard_map(
        functools.partial(shards, (dp, planes)),
        mesh=grid,
        in_specs=(tokens,) * 5 + (P("dp", None), P()),
        out_specs=(tokens,) * 5 + (P(("dp", "z", "x", "c"), None),),
        check_vma=False,
    )
```

```python
import functools
import math

import jax
import jax.numpy as jnp
from jax import lax
from jax.experimental import pallas as pl
from jax.experimental.pallas import tpu as pltpu
from jax.sharding import Mesh
from jax.sharding import PartitionSpec as P

HEADS = 8
EPS = 1e-05
USERS = 32
TOK = 128
PLANE = 1024
TILE = 256
TILES = PLANE // TILE
SCALE = 1.0 / math.sqrt(128.0)
F32 = jnp.float32
BF16 = jnp.bfloat16
PLANE_AXES = ("x", "c")
VMEM_LIMIT = 60 * 1024 * 1024
ROOM = 62_300_000

NN = (((1,), (0,)), ((), ()))
NT = (((1,), (1,)), ((), ()))
TN = (((0,), (0,)), ((), ()))


def dot(a, b, dims=NN):
    return lax.dot_general(a, b, dims, preferred_element_type=F32)


def flip(block):
    return block.astype(F32).T.astype(BF16)


def call(body, places, outs, flops, scratch=(), limit=VMEM_LIMIT):
    many = isinstance(outs, (list, tuple))
    outs = list(outs) if many else [outs]
    spaces = {"s": pltpu.SMEM, "v": pltpu.VMEM, "h": pltpu.HBM, "l": pltpu.HBM}

    def build(*args):
        staged = [n for n, place in enumerate(places) if place in "hl"]

        def whole(*refs):
            refs = list(refs)
            given, refs = refs[: len(args)], refs[len(args) :]
            results, refs = refs[: len(outs)], refs[len(outs) :]
            held, refs = refs[: len(staged)], refs[len(staged) :]
            made, refs = refs[: len(outs)], refs[len(outs) :]
            sems, out_sems, extra = refs[0], refs[1], refs[2:]
            now = []
            for m, n in enumerate(staged):
                copy = pltpu.make_async_copy(given[n], held[m], sems.at[m])
                copy.start()
                given[n] = held[m]
                if places[n] == "l":
                    given[n] = (held[m], copy)
                else:
                    now.append(copy)
            for copy in now:
                copy.wait()
            body(*given, *made, *extra)
            back = [pltpu.make_async_copy(src, dst, out_sems.at[m]) for m, (src, dst) in enumerate(zip(made, results))]
            for copy in back:
                copy.start()
            for copy in back:
                copy.wait()

        moved = sum(a.size * a.dtype.itemsize for a in args) + sum(o.size * o.dtype.itemsize for o in outs)
        got = pl.pallas_call(
            whole,
            out_shape=outs,
            in_specs=[pl.BlockSpec(memory_space=spaces[place]) for place in places],
            out_specs=[pl.BlockSpec(memory_space=pltpu.HBM)] * len(outs),
            scratch_shapes=[pltpu.VMEM(args[n].shape, args[n].dtype) for n in staged]
            + [pltpu.VMEM(o.shape, o.dtype) for o in outs]
            + [pltpu.SemaphoreType.DMA((max(len(staged), 1),)), pltpu.SemaphoreType.DMA((len(outs),))]
            + list(scratch),
            compiler_params=pltpu.CompilerParams(vmem_limit_bytes=limit),
            cost_estimate=pl.CostEstimate(flops=flops, bytes_accessed=moved, transcendentals=0),
        )(*args)
        return got if many else got[0]

    return build


def shape(dims, dtype):
    return jax.ShapeDtypeStruct(dims, dtype)


def pack_body(q_ref, k_ref, v_ref, out_ref, sems):
    copies = []
    for h in range(HEADS):
        for n, ref in enumerate((q_ref, k_ref, v_ref)):
            src = ref.at[:, h * TOK : (h + 1) * TOK]
            copies.append(pltpu.make_async_copy(src, out_ref.at[h, n * TOK : (n + 1) * TOK, :], sems.at[n, h]))
    for copy in copies:
        copy.start()
    for copy in copies:
        copy.wait()


def dgated_body(cot_ref, gate_ref, w_ref, out_ref):
    cot = cot_ref[...]
    for h in range(HEADS):
        cols = slice(h * TOK, (h + 1) * TOK)
        out_ref[h, 0:128, :] = flip(gate_ref[:, cols])
        out_ref[h, 128:256, :] = dot(w_ref[cols, :], cot, NT).astype(BF16)


def tile_of(ref, j, rows):
    return ref[pl.ds(2 * j, 2), rows, :].reshape(TILE, 128)


def tile_mask(start_ref, i, first_key):
    start = jnp.concatenate([start_ref[2 * i : 2 * i + 1, :], start_ref[2 * i + 1 : 2 * i + 2, :]], axis=1)
    key_place = first_key + lax.broadcasted_iota(jnp.int32, (TILE, TILE), 0)
    query_place = i * TILE + lax.broadcasted_iota(jnp.int32, (TILE, TILE), 1)
    return (key_place >= start) & (key_place <= query_place)


def sigmoid(s):
    return 1.0 / (1.0 + jnp.exp(-s))


def forward_tiles(i, low, high, first, keys_ref, key_rows, start_ref, qt, vt_ref, total):
    def step(j, acc):
        s = dot(tile_of(keys_ref, j, key_rows), qt) * SCALE
        mask = tile_mask(start_ref, i, first + j * TILE)
        w = jnp.where(mask, s * sigmoid(s), 0.0).astype(BF16)
        return acc + dot(vt_ref[j], w)

    return lax.fori_loop(low, high, step, total)


def fwd_own_body(low_ref, recv_ref, start_ref, mixt_ref, qt_ref, vt_ref):
    for t in range(HEADS):
        qt_ref[:, t * TOK : (t + 1) * TOK] = flip(recv_ref[t, 0:128, :])
        vt_ref[t // 2, :, (t % 2) * TOK : (t % 2 + 1) * TOK] = flip(recv_ref[t, 256:384, :])
    for i in range(TILES):
        cols = slice(i * TILE, (i + 1) * TILE)
        low = jnp.maximum(low_ref[i] - TILES, 0)
        mixt_ref[:, cols] = forward_tiles(
            i, low, i + 1, 0, recv_ref, slice(128, 256), start_ref, qt_ref[:, cols], vt_ref, jnp.zeros((128, TILE), F32)
        )


def fwd_halo_body(low_ref, halo_ref, start_ref, qt_ref, part_ref, gd_ref, mixt_ref, stats_ref, vt_ref):
    for t in range(HEADS):
        vt_ref[t // 2, :, (t % 2) * TOK : (t % 2 + 1) * TOK] = flip(halo_ref[t, 128:256, :])
    for i in range(TILES):
        cols = slice(i * TILE, (i + 1) * TILE)
        mixt_ref[:, cols] = forward_tiles(
            i, low_ref[i], TILES, -PLANE, halo_ref, slice(0, 128), start_ref, qt_ref[:, cols], vt_ref, part_ref[:, cols]
        )
    for b in range(HEADS):
        mix = mixt_ref[:, b * TOK : (b + 1) * TOK]
        dn = gd_ref[b, 0:128, :].astype(F32) * gd_ref[b, 128:256, :].astype(F32)
        mean = jnp.sum(mix, axis=0, keepdims=True) * (1.0 / 128.0)
        centred = mix - mean
        rows = (
            mean,
            jnp.sum(centred * centred, axis=0, keepdims=True),
            jnp.sum(dn, axis=0, keepdims=True),
            jnp.sum(dn * centred, axis=0, keepdims=True),
        )
        for k, row in enumerate(rows):
            stats_ref[0, 8 * k + b : 8 * k + b + 1, :] = row
    for d in range(1, HEADS):
        stats_ref[d] = stats_ref[0]


def finish(mixt_ref, gd_ref, stats_ref, gated_ref, gg_ref, dmix_ref):
    means = [stats_ref[h, 0:8, :] for h in range(HEADS)]
    mean = sum(means) * (1.0 / HEADS)
    square = sum(stats_ref[h, 8:16, :] for h in range(HEADS))
    square = square + 128.0 * sum((m - mean) * (m - mean) for m in means)
    inverse = lax.rsqrt(square * (1.0 / 1024.0) + EPS)
    dmean = sum(stats_ref[h, 16:24, :] for h in range(HEADS)) * (1.0 / 1024.0)
    cross = sum(stats_ref[h, 24:32, :] + (means[h] - mean) * stats_ref[h, 16:24, :] for h in range(HEADS))
    dcross = cross * inverse * (1.0 / 1024.0)
    for b in range(HEADS):
        cols = slice(b * TOK, (b + 1) * TOK)
        one = slice(b, b + 1)
        inv = inverse[one, :]
        normed = (mixt_ref[:, cols] - mean[one, :]) * inv
        gate = gd_ref[b, 0:128, :].astype(F32)
        dgated = gd_ref[b, 128:256, :].astype(F32)
        gated_ref[:, cols] = (normed * gate).astype(BF16)
        gg_ref[:, cols] = (normed * dgated).astype(BF16)
        dmix_ref[:, cols] = (inv * (dgated * gate - dmean[one, :] - normed * dcross[one, :])).astype(BF16)


def weight_part(gated_ref, cot_ref, out_ref):
    total = dot(gated_ref[:, 0:TOK], cot_ref[0])
    for b in range(1, HEADS):
        total = total + dot(gated_ref[:, b * TOK : (b + 1) * TOK], cot_ref[b])
    out_ref[...] = total.astype(BF16)


def backward_tiles(i, low, high, first, keys_ref, key_rows, value_rows, start_ref, qt, q, dmt, kt_ref, dk_ref, dv_ref, total):
    def step(j, acc):
        s = dot(tile_of(keys_ref, j, key_rows), qt) * SCALE
        mask = tile_mask(start_ref, i, first + j * TILE)
        sig = sigmoid(s)
        w = jnp.where(mask, s * sig, 0.0).astype(BF16)
        dw = dot(tile_of(keys_ref, j, value_rows), dmt)
        ds = jnp.where(mask, dw * (sig * (1.0 + s * (1.0 - sig))) * SCALE, 0.0).astype(BF16)
        dv_ref[j] += dot(w, dmt, NT)
        dk_ref[j] += dot(ds, q)
        return acc + dot(kt_ref[j], ds)

    return lax.fori_loop(low, high, step, total)


def middle_body(
    low_ref, mixt_ref, gd_ref, stats_ref, halo_ref, recv_ref, start_ref, qt_ref, late,
    gated_ref, gg_ref, dmix_ref, dqt_ref, out_ref, part_ref, kt_ref, dk_ref, dv_ref,
):
    finish(mixt_ref, gd_ref, stats_ref, gated_ref, gg_ref, dmix_ref)
    for t in range(HEADS):
        kt_ref[t // 2, :, (t % 2) * TOK : (t % 2 + 1) * TOK] = flip(halo_ref[t, 0:128, :])
    dk_ref[...] = jnp.zeros_like(dk_ref)
    dv_ref[...] = jnp.zeros_like(dv_ref)
    for i in range(TILES):
        cols = slice(i * TILE, (i + 1) * TILE)
        dqt_ref[:, cols] = backward_tiles(
            i, low_ref[i], TILES, -PLANE, halo_ref, slice(0, 128), slice(128, 256), start_ref, qt_ref[:, cols],
            tile_of(recv_ref, i, slice(0, 128)), dmix_ref[:, cols], kt_ref, dk_ref, dv_ref, jnp.zeros((128, TILE), F32),
        )
    for j in range(TILES):
        out_ref[2 * j : 2 * j + 2, 0:128, :] = dk_ref[j].astype(BF16).reshape(2, 128, 128)
        out_ref[2 * j : 2 * j + 2, 128:256, :] = dv_ref[j].astype(BF16).reshape(2, 128, 128)
    cot_ref, copy = late
    copy.wait()
    weight_part(gated_ref, cot_ref, part_ref)


def bwd_own_body(low_ref, recv_ref, start_ref, qt_ref, dmix_ref, part_ref, gated_ref, gg_ref, late, out_ref, kt_ref, dk_ref, dv_ref):
    for b in range(HEADS):
        out_ref[b, 0:128, :] = gated_ref[:, b * TOK : (b + 1) * TOK]
        out_ref[b, 128:256, :] = gg_ref[:, b * TOK : (b + 1) * TOK]
    for t in range(HEADS):
        kt_ref[t // 2, :, (t % 2) * TOK : (t % 2 + 1) * TOK] = flip(recv_ref[t, 128:256, :])
    dk_ref[...] = jnp.zeros_like(dk_ref)
    dv_ref[...] = jnp.zeros_like(dv_ref)
    for i in range(TILES):
        cols = slice(i * TILE, (i + 1) * TILE)
        low = jnp.maximum(low_ref[i] - TILES, 0)
        dqt = backward_tiles(
            i, low, i + 1, 0, recv_ref, slice(128, 256), slice(256, 384), start_ref, qt_ref[:, cols],
            tile_of(recv_ref, i, slice(0, 128)), dmix_ref[:, cols], kt_ref, dk_ref, dv_ref, part_ref[:, cols],
        )
        out_ref[2 * i : 2 * i + 2, 256:384, :] = dqt.T.astype(BF16).reshape(2, 128, 128)
    next_ref, copy = late
    copy.wait()
    for b in range(HEADS):
        rows = slice((b % 2) * TOK, (b % 2 + 1) * TOK)
        out_ref[b, 384:512, :] = (dk_ref[b // 2, rows, :] + next_ref[b, 0:128, :].astype(F32)).astype(BF16)
        out_ref[b, 512:640, :] = (dv_ref[b // 2, rows, :] + next_ref[b, 128:256, :].astype(F32)).astype(BF16)


def final_body(recv_ref, late, out_ref, dq_ref, dk_ref, dv_ref, gg_ref):
    w_ref, copy = late
    for h in range(HEADS):
        cols = slice(h * TOK, (h + 1) * TOK)
        gg_ref[:, cols] = flip(recv_ref[h, 128:256, :])
        dq_ref[:, cols] = recv_ref[h, 256:384, :]
        dk_ref[:, cols] = recv_ref[h, 384:512, :]
        dv_ref[:, cols] = recv_ref[h, 512:640, :]
    copy.wait()
    total = dot(flip(recv_ref[0, 0:128, :]), w_ref[0:TOK, :])
    for h in range(1, HEADS):
        total = total + dot(flip(recv_ref[h, 0:128, :]), w_ref[h * TOK : (h + 1) * TOK, :])
    out_ref[...] = total.astype(BF16)


def plane_exchange(blocks):
    return lax.all_to_all(blocks, PLANE_AXES, 0, 0, tiled=True)


def shards(sizes, queries, keys, values, gates, cotangent, segment, w_out):
    dp, planes = sizes
    q, k, v, gate, cot, seg = (a[0] for a in (queries, keys, values, gates, cotangent, segment))
    cot_plane = lax.all_gather(cot, PLANE_AXES)

    packed = pl.pallas_call(
        pack_body,
        out_shape=shape((8, 384, 128), BF16),
        in_specs=[pl.BlockSpec(memory_space=pltpu.HBM)] * 3,
        out_specs=pl.BlockSpec(memory_space=pltpu.HBM),
        scratch_shapes=[pltpu.SemaphoreType.DMA((3, HEADS))],
        compiler_params=pltpu.CompilerParams(vmem_limit_bytes=VMEM_LIMIT),
        cost_estimate=pl.CostEstimate(flops=1 << 16, bytes_accessed=3 << 19, transcendentals=0),
    )(q, k, v)
    recv = plane_exchange(packed)

    place = lax.axis_index("z") * PLANE
    users = jnp.arange(USERS, dtype=jnp.int32)[:, None]
    first = jnp.sum((seg[None, :] < users).astype(jnp.int32), axis=1)
    mine = lax.dynamic_slice_in_dim(seg, place, PLANE)
    start = jnp.sum(jnp.where(mine[None, :] == users, first[:, None], 0), axis=0) - place
    low = (start[::TILE] + PLANE) // TILE
    start = start.reshape(8, 128)

    pair, cot_now = lax.optimization_barrier((recv[:, 128:384], cot))
    halo = lax.ppermute(pair, "z", [(i, i + 1) for i in range(planes - 1)])
    gd = call(dgated_body, "hhh", shape((8, 256, 128), BF16), 1 << 28)(cot_now, gate, w_out)
    gd_recv = plane_exchange(gd)

    head = shape((128, PLANE), F32)
    head16 = shape((128, PLANE), BF16)
    vt = pltpu.VMEM((TILES, 128, TILE), BF16)
    acc = pltpu.VMEM((TILES, TILE, 128), F32)
    part, qt = call(fwd_own_body, "shh", [head, head16], 1 << 29, [vt])(low, recv, start)
    mixt, stats = call(fwd_halo_body, "shhhhh", [head, shape((8, 32, 128), F32)], 1 << 28, [vt], ROOM)(
        low, halo, start, qt, part, gd_recv
    )
    stats = plane_exchange(stats)
    gated, gg, dmix, dqt, back, partial = call(
        middle_body, "shhhhhhhl", [head16, head16, head16, head, shape((8, 256, 128), BF16), head16], 1 << 29, [vt, acc, acc]
    )(low, mixt, gd_recv, stats, halo, recv, start, qt, cot_plane)
    back = lax.ppermute(back, "z", [(i, i - 1) for i in range(1, planes)])

    shares = lax.all_to_all(partial, ("dp", "z"), 0, 0, tiled=True).reshape(dp * planes, 4, 1024)
    summed = jnp.sum(shares.astype(F32), axis=0)
    route = []
    for d in range(dp):
        for z in range(planes):
            for r in range(8):
                rows = 128 * r + 4 * (d * planes + z)
                route.append(((d * planes + z) * 8 + r, rows // 4))
    weight_grad = lax.ppermute(summed, ("dp", "z", "x", "c"), route)

    sent = call(bwd_own_body, "shhhhhhhl", shape((8, 640, 128), BF16), 1 << 30, [vt, acc, acc], ROOM)(
        low, recv, start, qt, dmix, dqt, gated, gg, back
    )
    got = plane_exchange(sent)
    rows = shape((TOK, 1024), BF16)
    out, dq, dk, dv, gg = call(final_body, "hl", [rows] * 5, 1 << 28, (), VMEM_LIMIT // 2)(got, w_out)
    return out[None], dq[None], dk[None], dv[None], gg[None], weight_grad


def solution(mesh):
    dp, seq = mesh.shape["dp"], mesh.shape["seq"]
    planes = seq // 8
    grid = Mesh(mesh.devices.reshape(dp, planes, 4, 2), ("dp", "z", "x", "c"))
    tokens = P("dp", ("z", "x", "c"), None)
    return jax.shard_map(
        functools.partial(shards, (dp, planes)),
        mesh=grid,
        in_specs=(tokens,) * 5 + (P("dp", None), P()),
        out_specs=(tokens,) * 5 + (P(("dp", "z", "x", "c"), None),),
        check_vma=False,
    )
```

```python
import functools
import math

import jax
import jax.numpy as jnp
from jax import lax
from jax.experimental import pallas as pl
from jax.experimental.pallas import tpu as pltpu
from jax.sharding import Mesh
from jax.sharding import PartitionSpec as P

HEADS = 8
EPS = 1e-05
USERS = 32
TOK = 128
PLANE = 1024
TILE = 256
TILES = PLANE // TILE
SCALE = 1.0 / math.sqrt(128.0)
F32 = jnp.float32
BF16 = jnp.bfloat16
PLANE_AXES = ("x", "c")
VMEM_LIMIT = 60 * 1024 * 1024
ROOM = 30 * 1024 * 1024

NN = (((1,), (0,)), ((), ()))
NT = (((1,), (1,)), ((), ()))
TN = (((0,), (0,)), ((), ()))


def dot(a, b, dims=NN):
    return lax.dot_general(a, b, dims, preferred_element_type=F32)


def flip(block):
    return block.astype(F32).T.astype(BF16)


class Held:
    def __init__(self, ref, copy):
        self.ref, self.copy = ref, copy

    def get(self):
        if self.copy is not None:
            self.copy.wait()
            self.copy = None
        return self.ref


class Made:
    def __init__(self, ref, target, log):
        self.ref, self.target, self.log = ref, target, log

    def send(self, src=(), dst=None):
        where = src if dst is None else dst
        self.log((self.ref.at[src] if src != () else self.ref, self.target.at[where] if where != () else self.target))


def call(body, places, outs, flops, scratch=(), limit=VMEM_LIMIT, sends=16, kept=None, held=None):
    outs, kept, held = list(outs), dict(kept or {}), dict(held or {})

    def build(*args):
        staged = [n for n, place in enumerate(places) if place == "h"]
        shapes = [held[n][1] if n in held else args[n].shape for n in staged]

        def whole(*refs):
            refs = list(refs)
            given, refs = refs[: len(args)], refs[len(args) :]
            results, refs = refs[: len(outs)], refs[len(outs) :]
            here, refs = refs[: len(staged)], refs[len(staged) :]
            made, refs = refs[: len(outs)], refs[len(outs) :]
            in_sems, out_sems, extra = refs[0], refs[1], refs[2:]
            for m, n in enumerate(staged):
                source = given[n].at[held[n][0]] if n in held else given[n]
                copy = pltpu.make_async_copy(source, here[m], in_sems.at[m])
                copy.start()
                given[n] = Held(here[m], copy)
            sent = []

            def log(pair):
                copy = pltpu.make_async_copy(pair[0], pair[1], out_sems.at[len(sent)])
                copy.start()
                sent.append(copy)

            body(*(g for g, place in zip(given, places) if place != "a"), *(Made(v, t, log) for v, t in zip(made, results)), *extra)
            for n in staged:
                given[n].get()
            for copy in sent:
                copy.wait()

        moved = sum(a.size * a.dtype.itemsize for a in args) + sum(o.size * o.dtype.itemsize for o in outs)
        return pl.pallas_call(
            whole,
            out_shape=outs,
            in_specs=[pl.BlockSpec(memory_space=pltpu.SMEM if place == "s" else pltpu.HBM) for place in places],
            out_specs=[pl.BlockSpec(memory_space=pltpu.HBM)] * len(outs),
            input_output_aliases={places.index("a"): 0} if "a" in places else {},
            scratch_shapes=[pltpu.VMEM(dims, args[n].dtype) for dims, n in zip(shapes, staged)]
            + [pltpu.VMEM(kept.get(m, o.shape), o.dtype) for m, o in enumerate(outs)]
            + [pltpu.SemaphoreType.DMA((len(staged) + 1,)), pltpu.SemaphoreType.DMA((sends,))]
            + list(scratch),
            compiler_params=pltpu.CompilerParams(vmem_limit_bytes=limit),
            cost_estimate=pl.CostEstimate(flops=flops, bytes_accessed=moved, transcendentals=0),
        )(*args)

    return build


def shape(dims, dtype):
    return jax.ShapeDtypeStruct(dims, dtype)


def pack_body(q, k, v, out):
    for n, held in enumerate((q, k, v)):
        ref = held.get()
        rows = slice(n * TOK, (n + 1) * TOK)
        for h in range(HEADS):
            out.ref[h, rows, :] = ref[:, h * TOK : (h + 1) * TOK]
        out.send((slice(None), rows))


def dgated_body(cot, gate, w, out):
    gate_ref = gate.get()
    for h in range(HEADS):
        out.ref[h, 0:128, :] = flip(gate_ref[:, h * TOK : (h + 1) * TOK])
    cotangent, w_ref = cot.get()[...], w.get()
    for h in range(HEADS):
        out.ref[h, 128:256, :] = dot(w_ref[h * TOK : (h + 1) * TOK, :], cotangent, NT).astype(BF16)
    out.send()


def tile_of(ref, j, rows):
    return ref[pl.ds(2 * j, 2), rows, :].reshape(TILE, 128)


def tile_mask(start_ref, i, first_key):
    start = jnp.concatenate([start_ref[2 * i : 2 * i + 1, :], start_ref[2 * i + 1 : 2 * i + 2, :]], axis=1)
    key_place = first_key + lax.broadcasted_iota(jnp.int32, (TILE, TILE), 0)
    query_place = i * TILE + lax.broadcasted_iota(jnp.int32, (TILE, TILE), 1)
    return (key_place >= start) & (key_place <= query_place)


def sigmoid(s):
    return 1.0 / (1.0 + jnp.exp(-s))


def flip_tiles(ref, rows, tiles):
    for t in range(HEADS):
        tiles[t // 2, :, (t % 2) * TOK : (t % 2 + 1) * TOK] = flip(ref[t, rows, :])


def forward_tiles(i, low, high, first, keys_ref, key_rows, start_ref, qt, vt_ref, total):
    def step(j, acc):
        s = dot(tile_of(keys_ref, j, key_rows), qt) * SCALE
        mask = tile_mask(start_ref, i, first + j * TILE)
        w = jnp.where(mask, s * sigmoid(s), 0.0).astype(BF16)
        return acc + dot(vt_ref[j], w)

    return lax.fori_loop(low, high, step, total)


def fwd_own_body(low_ref, recv, start, mixt, qt, vt_ref):
    recv_ref, start_ref = recv.get(), start.get()
    flip_tiles(recv_ref, slice(0, 128), qt.ref)
    qt.send()
    flip_tiles(recv_ref, slice(256, 384), vt_ref)
    for i in range(TILES):
        low = jnp.maximum(low_ref[i] - TILES, 0)
        mixt.ref[i] = forward_tiles(
            i, low, i + 1, 0, recv_ref, slice(128, 256), start_ref, qt.ref[i], vt_ref, jnp.zeros((128, TILE), F32)
        )
        mixt.send((i,))


def fwd_halo_body(low_ref, halo, start, qt, part, gd, mixt, stats, vt_ref):
    halo_ref, start_ref = halo.get(), start.get()
    flip_tiles(halo_ref, slice(128, 256), vt_ref)
    qt_ref, part_ref, gd_ref = qt.get(), part.get(), gd.get()
    for i in range(TILES):
        mixt.ref[i] = forward_tiles(
            i, low_ref[i], TILES, -PLANE, halo_ref, slice(0, 128), start_ref, qt_ref[i], vt_ref, part_ref[i]
        )
        mixt.send((i,))
        for b in (2 * i, 2 * i + 1):
            mix = mixt.ref[i, :, (b % 2) * TOK : (b % 2 + 1) * TOK]
            dn = gd_ref[b, 0:128, :].astype(F32) * gd_ref[b, 128:256, :].astype(F32)
            mean = jnp.sum(mix, axis=0, keepdims=True) * (1.0 / 128.0)
            centred = mix - mean
            rows = (
                mean,
                jnp.sum(centred * centred, axis=0, keepdims=True),
                jnp.sum(dn, axis=0, keepdims=True),
                jnp.sum(dn * centred, axis=0, keepdims=True),
            )
            for k, row in enumerate(rows):
                stats.ref[0, 8 * k + b : 8 * k + b + 1, :] = row
    for d in range(HEADS):
        stats.send((0,), (d,))


def finish(mixt_ref, gd_ref, stats_ref, gate_out, dmix_ref):
    means = [stats_ref[h, 0:8, :] for h in range(HEADS)]
    mean = sum(means) * (1.0 / HEADS)
    square = sum(stats_ref[h, 8:16, :] for h in range(HEADS))
    square = square + 128.0 * sum((m - mean) * (m - mean) for m in means)
    inverse = lax.rsqrt(square * (1.0 / 1024.0) + EPS)
    dmean = sum(stats_ref[h, 16:24, :] for h in range(HEADS)) * (1.0 / 1024.0)
    cross = sum(stats_ref[h, 24:32, :] + (means[h] - mean) * stats_ref[h, 16:24, :] for h in range(HEADS))
    dcross = cross * inverse * (1.0 / 1024.0)
    for b in range(HEADS):
        cols = slice((b % 2) * TOK, (b % 2 + 1) * TOK)
        one = slice(b, b + 1)
        inv = inverse[one, :]
        normed = (mixt_ref[b // 2, :, cols] - mean[one, :]) * inv
        gate = gd_ref[b, 0:128, :].astype(F32)
        dgated = gd_ref[b, 128:256, :].astype(F32)
        gate_out[b, 0:128, :] = (normed * gate).astype(BF16)
        gate_out[b, 128:256, :] = (normed * dgated).astype(BF16)
        dmix_ref[b // 2, :, cols] = (inv * (dgated * gate - dmean[one, :] - normed * dcross[one, :])).astype(BF16)


def backward_tiles(i, low, high, first, keys_ref, key_rows, value_rows, start_ref, qt, q, dmt, kt_ref, dk_ref, dv_ref, total):
    def step(j, acc):
        s = dot(tile_of(keys_ref, j, key_rows), qt) * SCALE
        mask = tile_mask(start_ref, i, first + j * TILE)
        sig = sigmoid(s)
        w = jnp.where(mask, s * sig, 0.0).astype(BF16)
        dw = dot(tile_of(keys_ref, j, value_rows), dmt)
        ds = jnp.where(mask, dw * (sig * (1.0 + s * (1.0 - sig))) * SCALE, 0.0).astype(BF16)
        dv_ref[j] += dot(w, dmt, NT)
        dk_ref[j] += dot(ds, q)
        return acc + dot(kt_ref[j], ds)

    return lax.fori_loop(low, high, step, total)


def middle_body(
    low_ref, who_ref, mixt, gd, stats, halo, recv, start, qt, cot, sent, dmix, dqt, back, own, far1, far2, far3, kt_ref, dk_ref, dv_ref
):
    finish(mixt.get(), gd.get(), stats.get(), sent.ref, dmix.ref)
    sent.send((), (slice(None), slice(0, 256)))
    dmix.send()
    halo_ref, recv_ref, start_ref, qt_ref = halo.get(), recv.get(), start.get(), qt.get()
    flip_tiles(halo_ref, slice(0, 128), kt_ref)
    dk_ref[...] = jnp.zeros_like(dk_ref)
    dv_ref[...] = jnp.zeros_like(dv_ref)
    for i in range(TILES):
        dqt.ref[i] = backward_tiles(
            i, low_ref[i], TILES, -PLANE, halo_ref, slice(0, 128), slice(128, 256), start_ref, qt_ref[i],
            tile_of(recv_ref, i, slice(0, 128)), dmix.ref[i], kt_ref, dk_ref, dv_ref, jnp.zeros((128, TILE), F32),
        )
    dqt.send()
    for j in range(TILES):
        back.ref[2 * j : 2 * j + 2, 0:128, :] = dk_ref[j].astype(BF16).reshape(2, 128, 128)
        back.ref[2 * j : 2 * j + 2, 128:256, :] = dv_ref[j].astype(BF16).reshape(2, 128, 128)
    back.send()
    row = lax.broadcasted_iota(jnp.int32, (128, 128), 0)
    feature = lax.broadcasted_iota(jnp.int32, (128, 128), 1)
    replica = jnp.bitwise_and(row // 32 + who_ref[0], 3)
    plane = jnp.bitwise_and(row // 4 + who_ref[1], 7)
    pick = jnp.where(feature == 32 * replica + 4 * plane + jnp.bitwise_and(row, 3), 1.0, 0.0).astype(BF16)
    cot_ref = cot.get()
    total = jnp.zeros((128, 1024), F32)
    for b in range(HEADS):
        total = total + dot(dot(pick, sent.ref[b, 0:128, :]).astype(BF16), cot_ref[b])
    own.ref[...] = total[0:32]
    own.send()
    for n, far in enumerate((far1, far2, far3)):
        far.ref[...] = total[32 * (n + 1) : 32 * (n + 2)].astype(BF16)
        far.send()


def replica_sum_body(own, got1, got2, got3, *outs):
    total = own.get()[...]
    for got in (got1, got2, got3):
        total = total + got.get()[...].astype(F32)
    for s, out in enumerate(outs):
        out.ref[...] = total[4 * s : 4 * s + 4]
        out.send()


def bwd_own_body(low_ref, recv, start, qt, dmix, part, out, dk, dv, kt_ref):
    recv_ref, start_ref = recv.get(), start.get()
    flip_tiles(recv_ref, slice(128, 256), kt_ref)
    dk.ref[...] = jnp.zeros_like(dk.ref)
    dv.ref[...] = jnp.zeros_like(dv.ref)
    qt_ref, dmix_ref, part_ref = qt.get(), dmix.get(), part.get()
    for i in range(TILES - 1, -1, -1):
        low = jnp.maximum(low_ref[i] - TILES, 0)
        dqt = backward_tiles(
            i, low, i + 1, 0, recv_ref, slice(128, 256), slice(256, 384), start_ref, qt_ref[i],
            tile_of(recv_ref, i, slice(0, 128)), dmix_ref[i], kt_ref, dk.ref, dv.ref, part_ref[i],
        )
        out.ref[2 * i : 2 * i + 2] = dqt.T.astype(BF16).reshape(2, 128, 128)
        blocks = slice(2 * i, 2 * i + 2)
        out.send((blocks,), (blocks, slice(256, 384)))
        dk.send((i,))
        dv.send((i,))


def add_body(dk, dv, back, out):
    next_ref, dk_ref, dv_ref = back.get(), dk.get(), dv.get()
    for b in range(HEADS):
        rows = slice((b % 2) * TOK, (b % 2 + 1) * TOK)
        out.ref[b, 0:128, :] = (dk_ref[b // 2, rows, :] + next_ref[b, 0:128, :].astype(F32)).astype(BF16)
        out.ref[b, 128:256, :] = (dv_ref[b // 2, rows, :] + next_ref[b, 128:256, :].astype(F32)).astype(BF16)
    out.send((), (slice(None), slice(384, 640)))


def final_body(recv, w, p0, p1, p2, p3, p4, p5, p6, p7, out, dq, dk, dv, gg, wg):
    total = p0.get()[...]
    for piece in (p1, p2, p3, p4, p5, p6, p7):
        total = total + piece.get()[...]
    wg.ref[...] = total
    wg.send()
    recv_ref, w_ref = recv.get(), w.get()
    for n, made in enumerate((dq, dk, dv)):
        for h in range(HEADS):
            made.ref[:, h * TOK : (h + 1) * TOK] = recv_ref[h, 256 + 128 * n : 384 + 128 * n, :]
        made.send()
    for h in range(HEADS):
        gg.ref[:, h * TOK : (h + 1) * TOK] = flip(recv_ref[h, 128:256, :])
    gg.send()
    total = dot(flip(recv_ref[0, 0:128, :]), w_ref[0:TOK, :])
    for h in range(1, HEADS):
        total = total + dot(flip(recv_ref[h, 0:128, :]), w_ref[h * TOK : (h + 1) * TOK, :])
    out.ref[...] = total.astype(BF16)
    out.send()


def plane_exchange(blocks):
    return lax.all_to_all(blocks, PLANE_AXES, 0, 0, tiled=True)


def shards(sizes, queries, keys, values, gates, cotangent, segment, w_out):
    dp, planes = sizes
    q, k, v, gate, cot, seg = (a[0] for a in (queries, keys, values, gates, cotangent, segment))
    cot_plane = lax.all_gather(cot, PLANE_AXES)
    rows = shape((TOK, 1024), BF16)
    head = shape((TILES, 128, TILE), F32)
    head16 = shape((TILES, 128, TILE), BF16)
    share = shape((4, 1024), F32)
    grad = shape((TILES, TILE, 128), F32)
    vt = pltpu.VMEM((TILES, 128, TILE), BF16)
    acc = pltpu.VMEM((TILES, TILE, 128), F32)

    (packed,) = call(pack_body, "hhh", [shape((8, 384, 128), BF16)], 1 << 16)(q, k, v)
    recv = plane_exchange(packed)

    replica, plane = lax.axis_index("dp"), lax.axis_index("z")
    who = jnp.stack([replica, plane]).astype(jnp.int32)
    place = plane * PLANE
    users = jnp.arange(USERS, dtype=jnp.int32)[:, None]
    first = jnp.sum((seg[None, :] < users).astype(jnp.int32), axis=1)
    mine = lax.dynamic_slice_in_dim(seg, place, PLANE)
    start = jnp.sum(jnp.where(mine[None, :] == users, first[:, None], 0), axis=0) - place
    low = (start[::TILE] + PLANE) // TILE
    start = start.reshape(8, 128)
    (gd,) = call(dgated_body, "hhh", [shape((8, 256, 128), BF16)], 1 << 28)(cot, gate, w_out)

    pair, gd, start, low, who = lax.optimization_barrier((recv[:, 128:384], gd, start, low, who))
    halo = lax.ppermute(pair, "z", [(i, i + 1) for i in range(planes - 1)])
    gd_recv = plane_exchange(gd)
    part, qt = call(fwd_own_body, "shh", [head, head16], 1 << 29, [vt])(low, recv, start)
    mixt, stats = call(fwd_halo_body, "shhhhh", [head, shape((8, 32, 128), F32)], 1 << 28, [vt], kept={1: (1, 32, 128)})(
        low, halo, start, qt, part, gd_recv
    )
    stats = plane_exchange(stats)

    only_q = {6: ((slice(None), slice(0, 128)), (8, 128, 128))}
    far = shape((32, 1024), BF16)
    sent, dmix, dqt, back, own, *fars = call(
        middle_body, "sshhhhhhhh",
        [shape((8, 640, 128), BF16), head16, head, shape((8, 256, 128), BF16), shape((32, 1024), F32), far, far, far],
        1 << 29, [vt, acc, acc], kept={0: (8, 256, 128)}, held=only_q,
    )(low, who, mixt, gd_recv, stats, halo, recv, start, qt, cot_plane)
    back = lax.ppermute(back, "z", [(i, i - 1) for i in range(1, planes)])
    fars = [lax.ppermute(x, "dp", [(i, (i + n + 1) % dp) for i in range(dp)]) for n, x in enumerate(fars)]
    pieces = call(replica_sum_body, "hhhh", [share] * 8, 1 << 16)(own, *fars)
    sent, dk, dv = call(
        bwd_own_body, "shhhhha", [shape((8, 640, 128), BF16), grad, grad], 1 << 30, [vt], kept={0: (8, 128, 128)}
    )(low, recv, start, qt, dmix, dqt, sent)
    (sent,) = call(add_body, "hhha", [shape((8, 640, 128), BF16)], 1 << 20, kept={0: (8, 256, 128)})(dk, dv, back, sent)
    sent, pieces = lax.optimization_barrier((sent, pieces))
    landed = []
    for s, piece in enumerate(pieces):
        route = []
        for d in range(dp):
            for z in range(planes):
                for r in range(8):
                    owner = (r // 2 * planes + (r % 2) * 4 + d) * 8 + (z + s) % 8
                    route.append(((d * planes + z) * 8 + r, owner))
        landed.append(lax.ppermute(piece, ("dp", "z", "x", "c"), route))
    got = plane_exchange(sent)
    out, dq, dk, dv, gg, weight_grad = call(final_body, "h" * 10, [rows] * 5 + [share], 1 << 28, (), ROOM)(got, w_out, *landed)
    return out[None], dq[None], dk[None], dv[None], gg[None], weight_grad


def solution(mesh):
    dp, seq = mesh.shape["dp"], mesh.shape["seq"]
    planes = seq // 8
    grid = Mesh(mesh.devices.reshape(dp, planes, 4, 2), ("dp", "z", "x", "c"))
    tokens = P("dp", ("z", "x", "c"), None)
    return jax.shard_map(
        functools.partial(shards, (dp, planes)),
        mesh=grid,
        in_specs=(tokens,) * 5 + (P("dp", None), P()),
        out_specs=(tokens,) * 5 + (P(("dp", "z", "x", "c"), None),),
        check_vma=False,
    )
```

```python
import functools
import math

import jax
import jax.numpy as jnp
from jax import lax
from jax.experimental import pallas as pl
from jax.experimental.pallas import tpu as pltpu
from jax.sharding import Mesh
from jax.sharding import PartitionSpec as P

HEADS = 8
EPS = 1e-05
USERS = 32
TOK = 128
PLANE = 1024
TILE = 256
TILES = PLANE // TILE
SCALE = 1.0 / math.sqrt(128.0)
F32 = jnp.float32
BF16 = jnp.bfloat16
PLANE_AXES = ("x", "c")
VMEM_LIMIT = 60 * 1024 * 1024
ROOM = 30 * 1024 * 1024
TIGHT = 62_300_000

NN = (((1,), (0,)), ((), ()))
NT = (((1,), (1,)), ((), ()))
TN = (((0,), (0,)), ((), ()))


def dot(a, b, dims=NN):
    return lax.dot_general(a, b, dims, preferred_element_type=F32)


def flip(block):
    return block.astype(F32).T.astype(BF16)


class Held:
    def __init__(self, ref, copy):
        self.ref, self.copy = ref, copy

    def get(self):
        if self.copy is not None:
            self.copy.wait()
            self.copy = None
        return self.ref


class Made:
    def __init__(self, ref, target, log):
        self.ref, self.target, self.log = ref, target, log

    def send(self, src=(), dst=None):
        where = src if dst is None else dst
        self.log((self.ref.at[src] if src != () else self.ref, self.target.at[where] if where != () else self.target))


def call(body, places, outs, flops, scratch=(), limit=VMEM_LIMIT, sends=16, kept=None, held=None):
    outs, kept, held = list(outs), dict(kept or {}), dict(held or {})

    def build(*args):
        staged = [n for n, place in enumerate(places) if place == "h"]
        shapes = [held[n][1] if n in held else args[n].shape for n in staged]

        def whole(*refs):
            refs = list(refs)
            given, refs = refs[: len(args)], refs[len(args) :]
            results, refs = refs[: len(outs)], refs[len(outs) :]
            here, refs = refs[: len(staged)], refs[len(staged) :]
            made, refs = refs[: len(outs)], refs[len(outs) :]
            in_sems, out_sems, extra = refs[0], refs[1], refs[2:]
            for m, n in enumerate(staged):
                source = given[n].at[held[n][0]] if n in held else given[n]
                copy = pltpu.make_async_copy(source, here[m], in_sems.at[m])
                copy.start()
                given[n] = Held(here[m], copy)
            sent = []

            def log(pair):
                copy = pltpu.make_async_copy(pair[0], pair[1], out_sems.at[len(sent)])
                copy.start()
                sent.append(copy)

            body(*(g for g, place in zip(given, places) if place != "a"), *(Made(v, t, log) for v, t in zip(made, results)), *extra)
            for n in staged:
                given[n].get()
            for copy in sent:
                copy.wait()

        moved = sum(a.size * a.dtype.itemsize for a in args) + sum(o.size * o.dtype.itemsize for o in outs)
        return pl.pallas_call(
            whole,
            out_shape=outs,
            in_specs=[pl.BlockSpec(memory_space=pltpu.SMEM if place == "s" else pltpu.HBM) for place in places],
            out_specs=[pl.BlockSpec(memory_space=pltpu.HBM)] * len(outs),
            input_output_aliases={places.index("a"): 0} if "a" in places else {},
            scratch_shapes=[pltpu.VMEM(dims, args[n].dtype) for dims, n in zip(shapes, staged)]
            + [pltpu.VMEM(kept.get(m, o.shape), o.dtype) for m, o in enumerate(outs)]
            + [pltpu.SemaphoreType.DMA((len(staged) + 1,)), pltpu.SemaphoreType.DMA((sends,))]
            + list(scratch),
            compiler_params=pltpu.CompilerParams(vmem_limit_bytes=limit),
            cost_estimate=pl.CostEstimate(flops=flops, bytes_accessed=moved, transcendentals=0),
        )(*args)

    return build


def shape(dims, dtype):
    return jax.ShapeDtypeStruct(dims, dtype)


def pack_body(q, k, v, out):
    for n, held in enumerate((q, k, v)):
        ref = held.get()
        rows = slice(n * TOK, (n + 1) * TOK)
        for h in range(HEADS):
            out.ref[h, rows, :] = ref[:, h * TOK : (h + 1) * TOK]
        out.send((slice(None), rows))


def dgated_body(cot, gate, w, out):
    gate_ref = gate.get()
    for h in range(HEADS):
        out.ref[h, 0:128, :] = flip(gate_ref[:, h * TOK : (h + 1) * TOK])
    cotangent, w_ref = cot.get()[...], w.get()
    for h in range(HEADS):
        out.ref[h, 128:256, :] = dot(w_ref[h * TOK : (h + 1) * TOK, :], cotangent, NT).astype(BF16)
    out.send()


def tile_of(ref, j, rows):
    return ref[pl.ds(2 * j, 2), rows, :].reshape(TILE, 128)


def tile_mask(start_ref, i, first_key):
    start = jnp.concatenate([start_ref[2 * i : 2 * i + 1, :], start_ref[2 * i + 1 : 2 * i + 2, :]], axis=1)
    key_place = first_key + lax.broadcasted_iota(jnp.int32, (TILE, TILE), 0)
    query_place = i * TILE + lax.broadcasted_iota(jnp.int32, (TILE, TILE), 1)
    return (key_place >= start) & (key_place <= query_place)


def sigmoid(s):
    return 1.0 / (1.0 + jnp.exp(-s))


def flip_tiles(ref, rows, tiles):
    for t in range(HEADS):
        tiles[t // 2, :, (t % 2) * TOK : (t % 2 + 1) * TOK] = flip(ref[t, rows, :])


def forward_tiles(i, low, high, first, keys_ref, key_rows, start_ref, qt, vt_ref, total):
    def step(j, acc):
        s = dot(tile_of(keys_ref, j, key_rows), qt) * SCALE
        mask = tile_mask(start_ref, i, first + j * TILE)
        w = jnp.where(mask, s * sigmoid(s), 0.0).astype(BF16)
        return acc + dot(vt_ref[j], w)

    return lax.fori_loop(low, high, step, total)


def fwd_own_body(low_ref, recv, start, mixt, qt, vt_ref):
    recv_ref, start_ref = recv.get(), start.get()
    flip_tiles(recv_ref, slice(0, 128), qt.ref)
    qt.send()
    flip_tiles(recv_ref, slice(256, 384), vt_ref)
    for i in range(TILES):
        low = jnp.maximum(low_ref[i] - TILES, 0)
        mixt.ref[i] = forward_tiles(
            i, low, i + 1, 0, recv_ref, slice(128, 256), start_ref, qt.ref[i], vt_ref, jnp.zeros((128, TILE), F32)
        )
        mixt.send((i,))


def fwd_halo_body(low_ref, halo, start, qt, part, gd, mixt, stats, vt_ref):
    halo_ref, start_ref = halo.get(), start.get()
    flip_tiles(halo_ref, slice(128, 256), vt_ref)
    qt_ref, part_ref, gd_ref = qt.get(), part.get(), gd.get()
    for i in range(TILES):
        mixt.ref[i] = forward_tiles(
            i, low_ref[i], TILES, -PLANE, halo_ref, slice(0, 128), start_ref, qt_ref[i], vt_ref, part_ref[i]
        )
        mixt.send((i,))
        for b in (2 * i, 2 * i + 1):
            mix = mixt.ref[i, :, (b % 2) * TOK : (b % 2 + 1) * TOK]
            dn = gd_ref[b, 0:128, :].astype(F32) * gd_ref[b, 128:256, :].astype(F32)
            mean = jnp.sum(mix, axis=0, keepdims=True) * (1.0 / 128.0)
            centred = mix - mean
            rows = (
                mean,
                jnp.sum(centred * centred, axis=0, keepdims=True),
                jnp.sum(dn, axis=0, keepdims=True),
                jnp.sum(dn * centred, axis=0, keepdims=True),
            )
            for k, row in enumerate(rows):
                stats.ref[0, 8 * k + b : 8 * k + b + 1, :] = row
    for d in range(HEADS):
        stats.send((0,), (d,))


def finish(mixt_ref, gd_ref, stats_ref, gate_out, dmix_ref):
    means = [stats_ref[h, 0:8, :] for h in range(HEADS)]
    mean = sum(means) * (1.0 / HEADS)
    square = sum(stats_ref[h, 8:16, :] for h in range(HEADS))
    square = square + 128.0 * sum((m - mean) * (m - mean) for m in means)
    inverse = lax.rsqrt(square * (1.0 / 1024.0) + EPS)
    dmean = sum(stats_ref[h, 16:24, :] for h in range(HEADS)) * (1.0 / 1024.0)
    cross = sum(stats_ref[h, 24:32, :] + (means[h] - mean) * stats_ref[h, 16:24, :] for h in range(HEADS))
    dcross = cross * inverse * (1.0 / 1024.0)
    for b in range(HEADS):
        cols = slice((b % 2) * TOK, (b % 2 + 1) * TOK)
        one = slice(b, b + 1)
        inv = inverse[one, :]
        normed = (mixt_ref[b // 2, :, cols] - mean[one, :]) * inv
        gate = gd_ref[b, 0:128, :].astype(F32)
        dgated = gd_ref[b, 128:256, :].astype(F32)
        gate_out[b, 0:128, :] = (normed * gate).astype(BF16)
        gate_out[b, 128:256, :] = (normed * dgated).astype(BF16)
        dmix_ref[b // 2, :, cols] = (inv * (dgated * gate - dmean[one, :] - normed * dcross[one, :])).astype(BF16)


def backward_tiles(i, low, high, first, keys_ref, key_rows, value_rows, start_ref, qt, q, dmt, kt_ref, dk_ref, dv_ref, total):
    def step(j, acc):
        s = dot(tile_of(keys_ref, j, key_rows), qt) * SCALE
        mask = tile_mask(start_ref, i, first + j * TILE)
        sig = sigmoid(s)
        w = jnp.where(mask, s * sig, 0.0).astype(BF16)
        dw = dot(tile_of(keys_ref, j, value_rows), dmt)
        ds = jnp.where(mask, dw * (sig * (1.0 + s * (1.0 - sig))) * SCALE, 0.0).astype(BF16)
        dv_ref[j] += dot(w, dmt, NT)
        dk_ref[j] += dot(ds, q)
        return acc + dot(kt_ref[j], ds)

    return lax.fori_loop(low, high, step, total)


def middle_body(
    low_ref, who_ref, mixt, gd, stats, halo, recv, start, qt, cot, sent, dmix, dqt, back, own, far1, far2, far3, kt_ref, dk_ref, dv_ref, all_ref
):
    finish(mixt.get(), gd.get(), stats.get(), sent.ref, dmix.ref)
    sent.send((), (slice(None), slice(0, 256)))
    dmix.send()
    halo_ref, recv_ref, start_ref, qt_ref = halo.get(), recv.get(), start.get(), qt.get()
    flip_tiles(halo_ref, slice(0, 128), kt_ref)
    dk_ref[...] = jnp.zeros_like(dk_ref)
    dv_ref[...] = jnp.zeros_like(dv_ref)
    for i in range(TILES):
        dqt.ref[i] = backward_tiles(
            i, low_ref[i], TILES, -PLANE, halo_ref, slice(0, 128), slice(128, 256), start_ref, qt_ref[i],
            tile_of(recv_ref, i, slice(0, 128)), dmix.ref[i], kt_ref, dk_ref, dv_ref, jnp.zeros((128, TILE), F32),
        )
    dqt.send()
    for j in range(TILES):
        back.ref[2 * j : 2 * j + 2, 0:128, :] = dk_ref[j].astype(BF16).reshape(2, 128, 128)
        back.ref[2 * j : 2 * j + 2, 128:256, :] = dv_ref[j].astype(BF16).reshape(2, 128, 128)
    back.send()
    cot_ref = cot.get()
    total = dot(sent.ref[0, 0:128, :], cot_ref[0])
    for b in range(1, HEADS):
        total = total + dot(sent.ref[b, 0:128, :], cot_ref[b])
    all_ref[...] = total
    for n, made in enumerate((own, far1, far2, far3)):
        block = jnp.bitwise_and(who_ref[0] + n, 3)
        made.ref[...] = all_ref[pl.ds(pl.multiple_of(32 * block, 32), 32), :].astype(made.ref.dtype)
        made.send()


def replica_sum_body(own, got1, got2, got3, out, total_ref, moved_ref):
    total = own.get()[...]
    for got in (got1, got2, got3):
        total = total + got.get()[...].astype(F32)
    total_ref[...] = total
    for j in range(8):
        for b in range(8):
            moved_ref[j, 4 * b : 4 * b + 4, :] = total_ref[4 * j : 4 * j + 4, 128 * b : 128 * b + 128]
    out.ref[...] = moved_ref[...].astype(BF16)
    out.send()


def bwd_own_body(low_ref, recv, start, qt, dmix, part, out, dk, dv, kt_ref):
    recv_ref, start_ref = recv.get(), start.get()
    flip_tiles(recv_ref, slice(128, 256), kt_ref)
    dk.ref[...] = jnp.zeros_like(dk.ref)
    dv.ref[...] = jnp.zeros_like(dv.ref)
    qt_ref, dmix_ref, part_ref = qt.get(), dmix.get(), part.get()
    for i in range(TILES - 1, -1, -1):
        low = jnp.maximum(low_ref[i] - TILES, 0)
        dqt = backward_tiles(
            i, low, i + 1, 0, recv_ref, slice(128, 256), slice(256, 384), start_ref, qt_ref[i],
            tile_of(recv_ref, i, slice(0, 128)), dmix_ref[i], kt_ref, dk.ref, dv.ref, part_ref[i],
        )
        out.ref[2 * i : 2 * i + 2] = dqt.T.astype(BF16).reshape(2, 128, 128)
        blocks = slice(2 * i, 2 * i + 2)
        out.send((blocks,), (blocks, slice(256, 384)))
        dk.send((i,))
        dv.send((i,))


def add_body(dk, dv, back, share, out):
    share_ref, next_ref, dk_ref, dv_ref = share.get(), back.get(), dk.get(), dv.get()
    for b in range(HEADS):
        rows = slice((b % 2) * TOK, (b % 2 + 1) * TOK)
        out.ref[b, 0:128, :] = (dk_ref[b // 2, rows, :] + next_ref[b, 0:128, :].astype(F32)).astype(BF16)
        out.ref[b, 128:256, :] = (dv_ref[b // 2, rows, :] + next_ref[b, 128:256, :].astype(F32)).astype(BF16)
    out.ref[:, 256:288, :] = share_ref[...]
    out.send((), (slice(None), slice(384, 672)))


def final_body(recv, w, out, dq, dk, dv, gg, wg):
    recv_ref = recv.get()
    share = recv_ref[0, 640:672, :].astype(F32)
    for n in range(1, HEADS):
        share = share + recv_ref[n, 640:672, :].astype(F32)
    for b in range(8):
        wg.ref[:, 128 * b : 128 * b + 128] = share[4 * b : 4 * b + 4, :]
    wg.send()
    w_ref = w.get()
    for n, made in enumerate((dq, dk, dv)):
        for h in range(HEADS):
            made.ref[:, h * TOK : (h + 1) * TOK] = recv_ref[h, 256 + 128 * n : 384 + 128 * n, :]
        made.send()
    for h in range(HEADS):
        gg.ref[:, h * TOK : (h + 1) * TOK] = flip(recv_ref[h, 128:256, :])
    gg.send()
    total = dot(flip(recv_ref[0, 0:128, :]), w_ref[0:TOK, :])
    for h in range(1, HEADS):
        total = total + dot(flip(recv_ref[h, 0:128, :]), w_ref[h * TOK : (h + 1) * TOK, :])
    out.ref[...] = total.astype(BF16)
    out.send()


def plane_exchange(blocks):
    return lax.all_to_all(blocks, PLANE_AXES, 0, 0, tiled=True)


def shards(sizes, queries, keys, values, gates, cotangent, segment, w_out):
    dp, planes = sizes
    q, k, v, gate, cot, seg = (a[0] for a in (queries, keys, values, gates, cotangent, segment))
    cot_plane = lax.all_gather(cot, PLANE_AXES)
    rows = shape((TOK, 1024), BF16)
    head = shape((TILES, 128, TILE), F32)
    head16 = shape((TILES, 128, TILE), BF16)
    share = shape((4, 1024), F32)
    grad = shape((TILES, TILE, 128), F32)
    vt = pltpu.VMEM((TILES, 128, TILE), BF16)
    acc = pltpu.VMEM((TILES, TILE, 128), F32)

    (packed,) = call(pack_body, "hhh", [shape((8, 384, 128), BF16)], 1 << 16)(q, k, v)
    recv = plane_exchange(packed)

    replica, plane = lax.axis_index("dp"), lax.axis_index("z")
    who = jnp.stack([replica, plane]).astype(jnp.int32)
    place = plane * PLANE
    users = jnp.arange(USERS, dtype=jnp.int32)[:, None]
    first = jnp.sum((seg[None, :] < users).astype(jnp.int32), axis=1)
    mine = lax.dynamic_slice_in_dim(seg, place, PLANE)
    start = jnp.sum(jnp.where(mine[None, :] == users, first[:, None], 0), axis=0) - place
    low = (start[::TILE] + PLANE) // TILE
    start = start.reshape(8, 128)
    (gd,) = call(dgated_body, "hhh", [shape((8, 256, 128), BF16)], 1 << 28)(cot, gate, w_out)

    pair, gd, start, low, who = lax.optimization_barrier((recv[:, 128:384], gd, start, low, who))
    halo = lax.ppermute(pair, "z", [(i, i + 1) for i in range(planes - 1)])
    gd_recv = plane_exchange(gd)
    part, qt = call(fwd_own_body, "shh", [head, head16], 1 << 29, [vt])(low, recv, start)
    mixt, stats = call(fwd_halo_body, "shhhhh", [head, shape((8, 32, 128), F32)], 1 << 28, [vt], TIGHT, kept={1: (1, 32, 128)})(
        low, halo, start, qt, part, gd_recv
    )
    stats = plane_exchange(stats)

    only_q = {6: ((slice(None), slice(0, 128)), (8, 128, 128))}
    far = shape((32, 1024), BF16)
    sent, dmix, dqt, back, own, *fars = call(
        middle_body, "sshhhhhhhh",
        [shape((8, 672, 128), BF16), head16, head, shape((8, 256, 128), BF16), shape((32, 1024), F32), far, far, far],
        1 << 29, [vt, acc, acc, pltpu.VMEM((128, 1024), F32)], kept={0: (8, 256, 128)}, held=only_q,
    )(low, who, mixt, gd_recv, stats, halo, recv, start, qt, cot_plane)
    back = lax.ppermute(back, "z", [(i, i - 1) for i in range(1, planes)])
    fars = [lax.ppermute(x, "dp", [(i, (i + n + 1) % dp) for i in range(dp)]) for n, x in enumerate(fars)]
    moved = shape((8, 32, 128), BF16)
    (moved,) = call(replica_sum_body, "hhhh", [moved], 1 << 16, [pltpu.VMEM((32, 1024), F32), pltpu.VMEM((8, 32, 128), F32)])(own, *fars)
    route = []
    for d in range(dp):
        for z in range(planes):
            for r in range(8):
                route.append(((d * planes + z) * 8 + r, (r // 2 * planes + (r % 2) * 4 + d) * 8 + z))
    moved = lax.ppermute(moved, ("dp", "z", "x", "c"), route)

    sent, dk, dv = call(
        bwd_own_body, "shhhhha", [shape((8, 672, 128), BF16), grad, grad], 1 << 30, [vt], kept={0: (8, 128, 128)}
    )(low, recv, start, qt, dmix, dqt, sent)
    (sent,) = call(add_body, "hhhha", [shape((8, 672, 128), BF16)], 1 << 20, (), TIGHT, kept={0: (8, 288, 128)})(dk, dv, back, moved, sent)
    got = plane_exchange(sent)
    out, dq, dk, dv, gg, weight_grad = call(final_body, "hh", [rows] * 5 + [share], 1 << 28, (), ROOM)(got, w_out)
    return out[None], dq[None], dk[None], dv[None], gg[None], weight_grad


def solution(mesh):
    dp, seq = mesh.shape["dp"], mesh.shape["seq"]
    planes = seq // 8
    grid = Mesh(mesh.devices.reshape(dp, planes, 4, 2), ("dp", "z", "x", "c"))
    tokens = P("dp", ("z", "x", "c"), None)
    return jax.shard_map(
        functools.partial(shards, (dp, planes)),
        mesh=grid,
        in_specs=(tokens,) * 5 + (P("dp", None), P()),
        out_specs=(tokens,) * 5 + (P(("dp", "z", "x", "c"), None),),
        check_vma=False,
    )
```

```python
import functools
import math

import jax
import jax.numpy as jnp
from jax import lax
from jax.experimental import pallas as pl
from jax.experimental.pallas import tpu as pltpu
from jax.sharding import Mesh
from jax.sharding import PartitionSpec as P

HEADS = 8
EPS = 1e-05
USERS = 32
TOK = 128
PLANE = 1024
TILE = 256
TILES = PLANE // TILE
SCALE = 1.0 / math.sqrt(128.0)
F32 = jnp.float32
BF16 = jnp.bfloat16
PLANE_AXES = ("x", "c")
VMEM_LIMIT = 60 * 1024 * 1024
ROOM = 30 * 1024 * 1024
TIGHT = 62_300_000

NN = (((1,), (0,)), ((), ()))
NT = (((1,), (1,)), ((), ()))
TN = (((0,), (0,)), ((), ()))


def dot(a, b, dims=NN):
    return lax.dot_general(a, b, dims, preferred_element_type=F32)


def flip(block):
    return block.astype(F32).T.astype(BF16)


class Held:
    def __init__(self, ref, copy):
        self.ref, self.copy = ref, copy

    def get(self):
        if self.copy is not None:
            self.copy.wait()
            self.copy = None
        return self.ref


class Made:
    def __init__(self, ref, target, log):
        self.ref, self.target, self.log = ref, target, log

    def send(self, src=(), dst=None):
        where = src if dst is None else dst
        self.log((self.ref.at[src] if src != () else self.ref, self.target.at[where] if where != () else self.target))


def call(body, places, outs, flops, scratch=(), limit=VMEM_LIMIT, sends=16, kept=None, held=None):
    outs, kept, held = list(outs), dict(kept or {}), dict(held or {})

    def build(*args):
        staged = [n for n, place in enumerate(places) if place == "h"]
        shapes = [held[n][1] if n in held else args[n].shape for n in staged]

        def whole(*refs):
            refs = list(refs)
            given, refs = refs[: len(args)], refs[len(args) :]
            results, refs = refs[: len(outs)], refs[len(outs) :]
            here, refs = refs[: len(staged)], refs[len(staged) :]
            made, refs = refs[: len(outs)], refs[len(outs) :]
            in_sems, out_sems, extra = refs[0], refs[1], refs[2:]
            for m, n in enumerate(staged):
                source = given[n].at[held[n][0]] if n in held else given[n]
                copy = pltpu.make_async_copy(source, here[m], in_sems.at[m])
                copy.start()
                given[n] = Held(here[m], copy)
            sent = []

            def log(pair):
                copy = pltpu.make_async_copy(pair[0], pair[1], out_sems.at[len(sent)])
                copy.start()
                sent.append(copy)

            body(*(g for g, place in zip(given, places) if place != "a"), *(Made(v, t, log) for v, t in zip(made, results)), *extra)
            for n in staged:
                given[n].get()
            for copy in sent:
                copy.wait()

        moved = sum(a.size * a.dtype.itemsize for a in args) + sum(o.size * o.dtype.itemsize for o in outs)
        return pl.pallas_call(
            whole,
            out_shape=outs,
            in_specs=[pl.BlockSpec(memory_space=pltpu.SMEM if place == "s" else pltpu.HBM) for place in places],
            out_specs=[pl.BlockSpec(memory_space=pltpu.HBM)] * len(outs),
            input_output_aliases={places.index("a"): 0} if "a" in places else {},
            scratch_shapes=[pltpu.VMEM(dims, args[n].dtype) for dims, n in zip(shapes, staged)]
            + [pltpu.VMEM(kept.get(m, o.shape), o.dtype) for m, o in enumerate(outs)]
            + [pltpu.SemaphoreType.DMA((len(staged) + 1,)), pltpu.SemaphoreType.DMA((sends,))]
            + list(scratch),
            compiler_params=pltpu.CompilerParams(vmem_limit_bytes=limit),
            cost_estimate=pl.CostEstimate(flops=flops, bytes_accessed=moved, transcendentals=0),
        )(*args)

    return build


def shape(dims, dtype):
    return jax.ShapeDtypeStruct(dims, dtype)


def pack_body(q, k, v, out):
    for n, held in enumerate((q, k, v)):
        ref = held.get()
        rows = slice(n * TOK, (n + 1) * TOK)
        for h in range(HEADS):
            out.ref[h, rows, :] = ref[:, h * TOK : (h + 1) * TOK]
        out.send((slice(None), rows))


def dgated_body(cot, gate, w, out):
    gate_ref = gate.get()
    for h in range(HEADS):
        out.ref[h, 0:128, :] = flip(gate_ref[:, h * TOK : (h + 1) * TOK])
    cotangent, w_ref = cot.get()[...], w.get()
    for h in range(HEADS):
        out.ref[h, 128:256, :] = dot(w_ref[h * TOK : (h + 1) * TOK, :], cotangent, NT).astype(BF16)
    out.send()


def tile_of(ref, j, rows):
    return ref[pl.ds(2 * j, 2), rows, :].reshape(TILE, 128)


def tile_mask(start_ref, i, first_key):
    start = jnp.concatenate([start_ref[2 * i : 2 * i + 1, :], start_ref[2 * i + 1 : 2 * i + 2, :]], axis=1)
    key_place = first_key + lax.broadcasted_iota(jnp.int32, (TILE, TILE), 0)
    query_place = i * TILE + lax.broadcasted_iota(jnp.int32, (TILE, TILE), 1)
    return (key_place >= start) & (key_place <= query_place)


def sigmoid(s):
    return 1.0 / (1.0 + jnp.exp(-s))


def flip_tiles(ref, rows, tiles):
    for t in range(HEADS):
        tiles[t // 2, :, (t % 2) * TOK : (t % 2 + 1) * TOK] = flip(ref[t, rows, :])


def forward_tiles(i, low, high, first, keys_ref, key_rows, start_ref, qt, vt_ref, total):
    def step(j, acc):
        s = dot(tile_of(keys_ref, j, key_rows), qt) * SCALE
        mask = tile_mask(start_ref, i, first + j * TILE)
        w = jnp.where(mask, s * sigmoid(s), 0.0).astype(BF16)
        return acc + dot(vt_ref[j], w)

    return lax.fori_loop(low, high, step, total)


def fwd_own_body(low_ref, recv, start, mixt, qt, vt_ref):
    recv_ref, start_ref = recv.get(), start.get()
    flip_tiles(recv_ref, slice(0, 128), qt.ref)
    qt.send()
    flip_tiles(recv_ref, slice(256, 384), vt_ref)
    for i in range(TILES):
        low = jnp.maximum(low_ref[i] - TILES, 0)
        mixt.ref[i] = forward_tiles(
            i, low, i + 1, 0, recv_ref, slice(128, 256), start_ref, qt.ref[i], vt_ref, jnp.zeros((128, TILE), F32)
        )
        mixt.send((i,))


def fwd_halo_body(low_ref, halo, start, qt, part, gd, mixt, stats, vt_ref):
    halo_ref, start_ref = halo.get(), start.get()
    flip_tiles(halo_ref, slice(128, 256), vt_ref)
    qt_ref, part_ref, gd_ref = qt.get(), part.get(), gd.get()
    for i in range(TILES):
        mixt.ref[i] = forward_tiles(
            i, low_ref[i], TILES, -PLANE, halo_ref, slice(0, 128), start_ref, qt_ref[i], vt_ref, part_ref[i]
        )
        mixt.send((i,))
        for b in (2 * i, 2 * i + 1):
            mix = mixt.ref[i, :, (b % 2) * TOK : (b % 2 + 1) * TOK]
            dn = gd_ref[b, 0:128, :].astype(F32) * gd_ref[b, 128:256, :].astype(F32)
            mean = jnp.sum(mix, axis=0, keepdims=True) * (1.0 / 128.0)
            centred = mix - mean
            rows = (
                mean,
                jnp.sum(centred * centred, axis=0, keepdims=True),
                jnp.sum(dn, axis=0, keepdims=True),
                jnp.sum(dn * centred, axis=0, keepdims=True),
            )
            for k, row in enumerate(rows):
                stats.ref[0, 8 * k + b : 8 * k + b + 1, :] = row
    for d in range(HEADS):
        stats.send((0,), (d,))


def finish(mixt_ref, gd_ref, stats_ref, gate_out, dmix_ref):
    means = [stats_ref[h, 0:8, :] for h in range(HEADS)]
    mean = sum(means) * (1.0 / HEADS)
    square = sum(stats_ref[h, 8:16, :] for h in range(HEADS))
    square = square + 128.0 * sum((m - mean) * (m - mean) for m in means)
    inverse = lax.rsqrt(square * (1.0 / 1024.0) + EPS)
    dmean = sum(stats_ref[h, 16:24, :] for h in range(HEADS)) * (1.0 / 1024.0)
    cross = sum(stats_ref[h, 24:32, :] + (means[h] - mean) * stats_ref[h, 16:24, :] for h in range(HEADS))
    dcross = cross * inverse * (1.0 / 1024.0)
    for b in range(HEADS):
        cols = slice((b % 2) * TOK, (b % 2 + 1) * TOK)
        one = slice(b, b + 1)
        inv = inverse[one, :]
        normed = (mixt_ref[b // 2, :, cols] - mean[one, :]) * inv
        gate = gd_ref[b, 0:128, :].astype(F32)
        dgated = gd_ref[b, 128:256, :].astype(F32)
        gate_out[b, 0:128, :] = (normed * gate).astype(BF16)
        gate_out[b, 128:256, :] = (normed * dgated).astype(BF16)
        dmix_ref[b // 2, :, cols] = (inv * (dgated * gate - dmean[one, :] - normed * dcross[one, :])).astype(BF16)


def backward_tiles(i, low, high, first, keys_ref, key_rows, value_rows, start_ref, qt, q, dmt, kt_ref, dk_ref, dv_ref, total):
    def step(j, acc):
        s = dot(tile_of(keys_ref, j, key_rows), qt) * SCALE
        mask = tile_mask(start_ref, i, first + j * TILE)
        sig = sigmoid(s)
        w = jnp.where(mask, s * sig, 0.0).astype(BF16)
        dw = dot(tile_of(keys_ref, j, value_rows), dmt)
        ds = jnp.where(mask, dw * (sig * (1.0 + s * (1.0 - sig))) * SCALE, 0.0).astype(BF16)
        dv_ref[j] += dot(w, dmt, NT)
        dk_ref[j] += dot(ds, q)
        return acc + dot(kt_ref[j], ds)

    return lax.fori_loop(low, high, step, total)


def middle_body(
    low_ref, who_ref, mixt, gd, stats, halo, recv, start, qt, cot, sent, dmix, dqt, back, own, far1, far2, far3, kt_ref, dk_ref, dv_ref, all_ref
):
    finish(mixt.get(), gd.get(), stats.get(), sent.ref, dmix.ref)
    sent.send()
    dmix.send()
    halo_ref, recv_ref, start_ref, qt_ref = halo.get(), recv.get(), start.get(), qt.get()
    flip_tiles(halo_ref, slice(0, 128), kt_ref)
    dk_ref[...] = jnp.zeros_like(dk_ref)
    dv_ref[...] = jnp.zeros_like(dv_ref)
    for i in range(TILES):
        dqt.ref[i] = backward_tiles(
            i, low_ref[i], TILES, -PLANE, halo_ref, slice(0, 128), slice(128, 256), start_ref, qt_ref[i],
            tile_of(recv_ref, i, slice(0, 128)), dmix.ref[i], kt_ref, dk_ref, dv_ref, jnp.zeros((128, TILE), F32),
        )
    dqt.send()
    for j in range(TILES):
        back.ref[2 * j : 2 * j + 2, 0:128, :] = dk_ref[j].astype(BF16).reshape(2, 128, 128)
        back.ref[2 * j : 2 * j + 2, 128:256, :] = dv_ref[j].astype(BF16).reshape(2, 128, 128)
    back.send()
    cot_ref = cot.get()
    total = dot(sent.ref[0, 0:128, :], cot_ref[0])
    for b in range(1, HEADS):
        total = total + dot(sent.ref[b, 0:128, :], cot_ref[b])
    all_ref[...] = total
    for n, made in enumerate((own, far1, far2, far3)):
        block = jnp.bitwise_and(who_ref[0] + n, 3)
        made.ref[...] = all_ref[pl.ds(pl.multiple_of(32 * block, 32), 32), :].astype(made.ref.dtype)
        made.send()


def replica_sum_body(own, got1, got2, got3, out, total_ref, moved_ref):
    total = own.get()[...]
    for got in (got1, got2, got3):
        total = total + got.get()[...].astype(F32)
    total_ref[...] = total
    for j in range(8):
        for b in range(8):
            moved_ref[j, 4 * b : 4 * b + 4, :] = total_ref[4 * j : 4 * j + 4, 128 * b : 128 * b + 128]
    out.ref[...] = moved_ref[...].astype(BF16)
    out.send()


def bwd_own_body(low_ref, recv, start, qt, dmix, part, out, dk, dv, kt_ref):
    recv_ref, start_ref = recv.get(), start.get()
    flip_tiles(recv_ref, slice(128, 256), kt_ref)
    dk.ref[...] = jnp.zeros_like(dk.ref)
    dv.ref[...] = jnp.zeros_like(dv.ref)
    qt_ref, dmix_ref, part_ref = qt.get(), dmix.get(), part.get()
    for i in range(TILES - 1, -1, -1):
        low = jnp.maximum(low_ref[i] - TILES, 0)
        dqt = backward_tiles(
            i, low, i + 1, 0, recv_ref, slice(128, 256), slice(256, 384), start_ref, qt_ref[i],
            tile_of(recv_ref, i, slice(0, 128)), dmix_ref[i], kt_ref, dk.ref, dv.ref, part_ref[i],
        )
        out.ref[2 * i : 2 * i + 2] = dqt.T.astype(BF16).reshape(2, 128, 128)
        blocks = slice(2 * i, 2 * i + 2)
        out.send((blocks,), (blocks, slice(0, 128)))
        dk.send((i,))
        dv.send((i,))


def add_body(dk, dv, back, out):
    next_ref, dk_ref, dv_ref = back.get(), dk.get(), dv.get()
    for b in range(HEADS):
        rows = slice((b % 2) * TOK, (b % 2 + 1) * TOK)
        out.ref[b, 0:128, :] = (dk_ref[b // 2, rows, :] + next_ref[b, 0:128, :].astype(F32)).astype(BF16)
        out.ref[b, 128:256, :] = (dv_ref[b // 2, rows, :] + next_ref[b, 128:256, :].astype(F32)).astype(BF16)
    out.send((), (slice(None), slice(128, 384)))


def share_body(share, out):
    out.ref[...] = share.get()[...]
    out.send((), (slice(None), slice(384, 416)))


def gate_body(recv, w, out, gg):
    recv_ref = recv.get()
    for h in range(HEADS):
        gg.ref[:, h * TOK : (h + 1) * TOK] = flip(recv_ref[h, 128:256, :])
    gg.send()
    w_ref = w.get()
    total = dot(flip(recv_ref[0, 0:128, :]), w_ref[0:TOK, :])
    for h in range(1, HEADS):
        total = total + dot(flip(recv_ref[h, 0:128, :]), w_ref[h * TOK : (h + 1) * TOK, :])
    out.ref[...] = total.astype(BF16)
    out.send()


def final_body(recv, dq, dk, dv, wg):
    recv_ref = recv.get()
    for n, made in enumerate((dq, dk, dv)):
        for h in range(HEADS):
            made.ref[:, h * TOK : (h + 1) * TOK] = recv_ref[h, 128 * n : 128 * n + 128, :]
        made.send()
    share = recv_ref[0, 384:416, :].astype(F32)
    for n in range(1, HEADS):
        share = share + recv_ref[n, 384:416, :].astype(F32)
    for b in range(8):
        wg.ref[:, 128 * b : 128 * b + 128] = share[4 * b : 4 * b + 4, :]
    wg.send()


def plane_exchange(blocks):
    return lax.all_to_all(blocks, PLANE_AXES, 0, 0, tiled=True)


def shards(sizes, queries, keys, values, gates, cotangent, segment, w_out):
    dp, planes = sizes
    q, k, v, gate, cot, seg = (a[0] for a in (queries, keys, values, gates, cotangent, segment))
    cot_plane = lax.all_gather(cot, PLANE_AXES)
    rows = shape((TOK, 1024), BF16)
    head = shape((TILES, 128, TILE), F32)
    head16 = shape((TILES, 128, TILE), BF16)
    share = shape((4, 1024), F32)
    grad = shape((TILES, TILE, 128), F32)
    vt = pltpu.VMEM((TILES, 128, TILE), BF16)
    acc = pltpu.VMEM((TILES, TILE, 128), F32)

    (packed,) = call(pack_body, "hhh", [shape((8, 384, 128), BF16)], 1 << 16)(q, k, v)
    recv = plane_exchange(packed)

    replica, plane = lax.axis_index("dp"), lax.axis_index("z")
    who = jnp.stack([replica, plane]).astype(jnp.int32)
    place = plane * PLANE
    users = jnp.arange(USERS, dtype=jnp.int32)[:, None]
    first = jnp.sum((seg[None, :] < users).astype(jnp.int32), axis=1)
    mine = lax.dynamic_slice_in_dim(seg, place, PLANE)
    start = jnp.sum(jnp.where(mine[None, :] == users, first[:, None], 0), axis=0) - place
    low = (start[::TILE] + PLANE) // TILE
    start = start.reshape(8, 128)
    (gd,) = call(dgated_body, "hhh", [shape((8, 256, 128), BF16)], 1 << 28)(cot, gate, w_out)

    pair, gd, start, low, who = lax.optimization_barrier((recv[:, 128:384], gd, start, low, who))
    halo = lax.ppermute(pair, "z", [(i, i + 1) for i in range(planes - 1)])
    gd_recv = plane_exchange(gd)
    part, qt = call(fwd_own_body, "shh", [head, head16], 1 << 29, [vt])(low, recv, start)
    mixt, stats = call(fwd_halo_body, "shhhhh", [head, shape((8, 32, 128), F32)], 1 << 28, [vt], TIGHT, kept={1: (1, 32, 128)})(
        low, halo, start, qt, part, gd_recv
    )
    stats = plane_exchange(stats)

    only_q = {6: ((slice(None), slice(0, 128)), (8, 128, 128))}
    far = shape((32, 1024), BF16)
    gate_pack, dmix, dqt, back, own, *fars = call(
        middle_body, "sshhhhhhhh",
        [shape((8, 256, 128), BF16), head16, head, shape((8, 256, 128), BF16), shape((32, 1024), F32), far, far, far],
        1 << 29, [vt, acc, acc, pltpu.VMEM((128, 1024), F32)], held=only_q,
    )(low, who, mixt, gd_recv, stats, halo, recv, start, qt, cot_plane)
    back = lax.ppermute(back, "z", [(i, i - 1) for i in range(1, planes)])
    fars = [lax.ppermute(x, "dp", [(i, (i + n + 1) % dp) for i in range(dp)]) for n, x in enumerate(fars)]
    moved = shape((8, 32, 128), BF16)
    (moved,) = call(replica_sum_body, "hhhh", [moved], 1 << 16, [pltpu.VMEM((32, 1024), F32), pltpu.VMEM((8, 32, 128), F32)])(own, *fars)
    route = []
    for d in range(dp):
        for z in range(planes):
            for r in range(8):
                route.append(((d * planes + z) * 8 + r, (r // 2 * planes + (r % 2) * 4 + d) * 8 + z))
    got_gate = plane_exchange(gate_pack)

    sent, dk, dv = call(
        bwd_own_body, "shhhhh", [shape((8, 416, 128), BF16), grad, grad], 1 << 30, [vt], kept={0: (8, 128, 128)}
    )(low, recv, start, qt, dmix, dqt)
    moved, back, dk = lax.optimization_barrier((moved, back, dk))
    moved = lax.ppermute(moved, ("dp", "z", "x", "c"), route)
    sent, got_gate = lax.optimization_barrier((sent, got_gate))
    whole = [shape((8, 416, 128), BF16)]
    (sent,) = call(add_body, "hhha", whole, 1 << 20, (), TIGHT, kept={0: (8, 256, 128)})(dk, dv, back, sent)
    (sent,) = call(share_body, "ha", whole, 1 << 10, kept={0: (8, 32, 128)})(moved, sent)
    got = plane_exchange(sent)
    out, gg = call(gate_body, "hh", [rows, rows], 1 << 28)(got_gate, w_out)
    dq, dk, dv, weight_grad = call(final_body, "h", [rows] * 3 + [share], 1 << 20, (), ROOM)(got)
    return out[None], dq[None], dk[None], dv[None], gg[None], weight_grad


def solution(mesh):
    dp, seq = mesh.shape["dp"], mesh.shape["seq"]
    planes = seq // 8
    grid = Mesh(mesh.devices.reshape(dp, planes, 4, 2), ("dp", "z", "x", "c"))
    tokens = P("dp", ("z", "x", "c"), None)
    return jax.shard_map(
        functools.partial(shards, (dp, planes)),
        mesh=grid,
        in_specs=(tokens,) * 5 + (P("dp", None), P()),
        out_specs=(tokens,) * 5 + (P(("dp", "z", "x", "c"), None),),
        check_vma=False,
    )
```

```python
import functools
import math

import jax
import jax.numpy as jnp
from jax import lax
from jax.experimental import pallas as pl
from jax.experimental.pallas import tpu as pltpu
from jax.sharding import Mesh
from jax.sharding import PartitionSpec as P

HEADS = 8
EPS = 1e-05
USERS = 32
TOK = 128
PLANE = 1024
TILE = 256
TILES = PLANE // TILE
SCALE = 1.0 / math.sqrt(128.0)
F32 = jnp.float32
BF16 = jnp.bfloat16
PLANE_AXES = ("x", "c")
VMEM_LIMIT = 60 * 1024 * 1024
ROOM = 30 * 1024 * 1024
TIGHT = 62_300_000

NN = (((1,), (0,)), ((), ()))
NT = (((1,), (1,)), ((), ()))
TN = (((0,), (0,)), ((), ()))


def dot(a, b, dims=NN):
    return lax.dot_general(a, b, dims, preferred_element_type=F32)


def flip(block):
    return block.astype(F32).T.astype(BF16)


class Held:
    def __init__(self, ref, copy):
        self.ref, self.copy = ref, copy

    def get(self):
        if self.copy is not None:
            self.copy.wait()
            self.copy = None
        return self.ref


class Made:
    def __init__(self, ref, target, log):
        self.ref, self.target, self.log = ref, target, log

    def send(self, src=(), dst=None):
        where = src if dst is None else dst
        self.log((self.ref.at[src] if src != () else self.ref, self.target.at[where] if where != () else self.target))


def call(body, places, outs, flops, scratch=(), limit=VMEM_LIMIT, sends=16, kept=None, held=None):
    outs, kept, held = list(outs), dict(kept or {}), dict(held or {})

    def build(*args):
        staged = [n for n, place in enumerate(places) if place == "h"]
        shapes = [held[n][1] if n in held else args[n].shape for n in staged]

        def whole(*refs):
            refs = list(refs)
            given, refs = refs[: len(args)], refs[len(args) :]
            results, refs = refs[: len(outs)], refs[len(outs) :]
            here, refs = refs[: len(staged)], refs[len(staged) :]
            made, refs = refs[: len(outs)], refs[len(outs) :]
            in_sems, out_sems, extra = refs[0], refs[1], refs[2:]
            for m, n in enumerate(staged):
                source = given[n].at[held[n][0]] if n in held else given[n]
                copy = pltpu.make_async_copy(source, here[m], in_sems.at[m])
                copy.start()
                given[n] = Held(here[m], copy)
            sent = []

            def log(pair):
                copy = pltpu.make_async_copy(pair[0], pair[1], out_sems.at[len(sent)])
                copy.start()
                sent.append(copy)

            body(*(g for g, place in zip(given, places) if place != "a"), *(Made(v, t, log) for v, t in zip(made, results)), *extra)
            for n in staged:
                given[n].get()
            for copy in sent:
                copy.wait()

        moved = sum(a.size * a.dtype.itemsize for a in args) + sum(o.size * o.dtype.itemsize for o in outs)
        return pl.pallas_call(
            whole,
            out_shape=outs,
            in_specs=[pl.BlockSpec(memory_space=pltpu.SMEM if place == "s" else pltpu.HBM) for place in places],
            out_specs=[pl.BlockSpec(memory_space=pltpu.HBM)] * len(outs),
            input_output_aliases={places.index("a"): 0} if "a" in places else {},
            scratch_shapes=[pltpu.VMEM(dims, args[n].dtype) for dims, n in zip(shapes, staged)]
            + [pltpu.VMEM(kept.get(m, o.shape), o.dtype) for m, o in enumerate(outs)]
            + [pltpu.SemaphoreType.DMA((len(staged) + 1,)), pltpu.SemaphoreType.DMA((sends,))]
            + list(scratch),
            compiler_params=pltpu.CompilerParams(vmem_limit_bytes=limit),
            cost_estimate=pl.CostEstimate(flops=flops, bytes_accessed=moved, transcendentals=0),
        )(*args)

    return build


def shape(dims, dtype):
    return jax.ShapeDtypeStruct(dims, dtype)


def pack_body(q, k, v, out):
    for n, held in enumerate((q, k, v)):
        ref = held.get()
        rows = slice(n * TOK, (n + 1) * TOK)
        for h in range(HEADS):
            out.ref[h, rows, :] = ref[:, h * TOK : (h + 1) * TOK]
        out.send((slice(None), rows))


def dgated_body(cot, gate, w, out):
    gate_ref = gate.get()
    for h in range(HEADS):
        out.ref[h, 0:128, :] = flip(gate_ref[:, h * TOK : (h + 1) * TOK])
    cotangent, w_ref = cot.get()[...], w.get()
    for h in range(HEADS):
        out.ref[h, 128:256, :] = dot(w_ref[h * TOK : (h + 1) * TOK, :], cotangent, NT).astype(BF16)
    out.send()


def tile_of(ref, j, rows):
    return ref[pl.ds(2 * j, 2), rows, :].reshape(TILE, 128)


def tile_mask(start_ref, i, first_key):
    start = jnp.concatenate([start_ref[2 * i : 2 * i + 1, :], start_ref[2 * i + 1 : 2 * i + 2, :]], axis=1)
    key_place = first_key + lax.broadcasted_iota(jnp.int32, (TILE, TILE), 0)
    query_place = i * TILE + lax.broadcasted_iota(jnp.int32, (TILE, TILE), 1)
    return (key_place >= start) & (key_place <= query_place)


def sigmoid(s):
    return 1.0 / (1.0 + jnp.exp(-s))


def flip_tiles(ref, rows, tiles):
    for t in range(HEADS):
        tiles[t // 2, :, (t % 2) * TOK : (t % 2 + 1) * TOK] = flip(ref[t, rows, :])


def forward_tiles(i, low, high, first, keys_ref, key_rows, start_ref, qt, vt_ref, total):
    def step(j, acc):
        s = dot(tile_of(keys_ref, j, key_rows), qt) * SCALE
        mask = tile_mask(start_ref, i, first + j * TILE)
        w = jnp.where(mask, s * sigmoid(s), 0.0).astype(BF16)
        return acc + dot(vt_ref[j], w)

    return lax.fori_loop(low, high, step, total)


def fwd_own_body(low_ref, recv, start, mixt, qt, vt_ref):
    recv_ref, start_ref = recv.get(), start.get()
    flip_tiles(recv_ref, slice(0, 128), qt.ref)
    qt.send()
    flip_tiles(recv_ref, slice(256, 384), vt_ref)
    for i in range(TILES):
        low = jnp.maximum(low_ref[i] - TILES, 0)
        mixt.ref[i] = forward_tiles(
            i, low, i + 1, 0, recv_ref, slice(128, 256), start_ref, qt.ref[i], vt_ref, jnp.zeros((128, TILE), F32)
        )
        mixt.send((i,))


def fwd_halo_body(low_ref, halo, start, qt, part, gd, mixt, stats, vt_ref):
    halo_ref, start_ref = halo.get(), start.get()
    flip_tiles(halo_ref, slice(128, 256), vt_ref)
    qt_ref, part_ref, gd_ref = qt.get(), part.get(), gd.get()
    for i in range(TILES):
        mixt.ref[i] = forward_tiles(
            i, low_ref[i], TILES, -PLANE, halo_ref, slice(0, 128), start_ref, qt_ref[i], vt_ref, part_ref[i]
        )
        mixt.send((i,))
        for b in (2 * i, 2 * i + 1):
            mix = mixt.ref[i, :, (b % 2) * TOK : (b % 2 + 1) * TOK]
            dn = gd_ref[b, 0:128, :].astype(F32) * gd_ref[b, 128:256, :].astype(F32)
            mean = jnp.sum(mix, axis=0, keepdims=True) * (1.0 / 128.0)
            centred = mix - mean
            rows = (
                mean,
                jnp.sum(centred * centred, axis=0, keepdims=True),
                jnp.sum(dn, axis=0, keepdims=True),
                jnp.sum(dn * centred, axis=0, keepdims=True),
            )
            for k, row in enumerate(rows):
                stats.ref[0, 8 * k + b : 8 * k + b + 1, :] = row
    for d in range(HEADS):
        stats.send((0,), (d,))


def finish(mixt_ref, gd_ref, stats_ref, gate_out, dmix_ref):
    means = [stats_ref[h, 0:8, :] for h in range(HEADS)]
    mean = sum(means) * (1.0 / HEADS)
    square = sum(stats_ref[h, 8:16, :] for h in range(HEADS))
    square = square + 128.0 * sum((m - mean) * (m - mean) for m in means)
    inverse = lax.rsqrt(square * (1.0 / 1024.0) + EPS)
    dmean = sum(stats_ref[h, 16:24, :] for h in range(HEADS)) * (1.0 / 1024.0)
    cross = sum(stats_ref[h, 24:32, :] + (means[h] - mean) * stats_ref[h, 16:24, :] for h in range(HEADS))
    dcross = cross * inverse * (1.0 / 1024.0)
    for b in range(HEADS):
        cols = slice((b % 2) * TOK, (b % 2 + 1) * TOK)
        one = slice(b, b + 1)
        inv = inverse[one, :]
        normed = (mixt_ref[b // 2, :, cols] - mean[one, :]) * inv
        gate = gd_ref[b, 0:128, :].astype(F32)
        dgated = gd_ref[b, 128:256, :].astype(F32)
        gate_out[b, 0:128, :] = (normed * gate).astype(BF16)
        gate_out[b, 128:256, :] = (normed * dgated).astype(BF16)
        dmix_ref[b // 2, :, cols] = (inv * (dgated * gate - dmean[one, :] - normed * dcross[one, :])).astype(BF16)


def backward_tiles(i, low, high, first, keys_ref, key_rows, value_rows, start_ref, qt, q, dmt, kt_ref, dk_ref, dv_ref, total):
    def step(j, acc):
        s = dot(tile_of(keys_ref, j, key_rows), qt) * SCALE
        mask = tile_mask(start_ref, i, first + j * TILE)
        sig = sigmoid(s)
        w = jnp.where(mask, s * sig, 0.0).astype(BF16)
        dw = dot(tile_of(keys_ref, j, value_rows), dmt)
        ds = jnp.where(mask, dw * (sig * (1.0 + s * (1.0 - sig))) * SCALE, 0.0).astype(BF16)
        dv_ref[j] += dot(w, dmt, NT)
        dk_ref[j] += dot(ds, q)
        return acc + dot(kt_ref[j], ds)

    return lax.fori_loop(low, high, step, total)


def middle_body(
    low_ref, who_ref, mixt, gd, stats, halo, recv, start, qt, cot, sent, dmix, dqt, back, own, far1, far2, far3, kt_ref, dk_ref, dv_ref, all_ref
):
    finish(mixt.get(), gd.get(), stats.get(), sent.ref, dmix.ref)
    sent.send()
    dmix.send()
    halo_ref, recv_ref, start_ref, qt_ref = halo.get(), recv.get(), start.get(), qt.get()
    flip_tiles(halo_ref, slice(0, 128), kt_ref)
    dk_ref[...] = jnp.zeros_like(dk_ref)
    dv_ref[...] = jnp.zeros_like(dv_ref)
    for i in range(TILES):
        dqt.ref[i] = backward_tiles(
            i, low_ref[i], TILES, -PLANE, halo_ref, slice(0, 128), slice(128, 256), start_ref, qt_ref[i],
            tile_of(recv_ref, i, slice(0, 128)), dmix.ref[i], kt_ref, dk_ref, dv_ref, jnp.zeros((128, TILE), F32),
        )
    dqt.send()
    for j in range(TILES):
        back.ref[2 * j : 2 * j + 2, 0:128, :] = dk_ref[j].astype(BF16).reshape(2, 128, 128)
        back.ref[2 * j : 2 * j + 2, 128:256, :] = dv_ref[j].astype(BF16).reshape(2, 128, 128)
    back.send()
    cot_ref = cot.get()
    total = dot(sent.ref[0, 0:128, :], cot_ref[0])
    for b in range(1, HEADS):
        total = total + dot(sent.ref[b, 0:128, :], cot_ref[b])
    all_ref[...] = total
    for n, made in enumerate((own, far1, far2, far3)):
        block = jnp.bitwise_and(who_ref[0] + n, 3)
        made.ref[...] = all_ref[pl.ds(pl.multiple_of(32 * block, 32), 32), :].astype(made.ref.dtype)
        made.send()


def replica_sum_body(own, got1, got2, got3, out, total_ref, moved_ref):
    total = own.get()[...]
    for got in (got1, got2, got3):
        total = total + got.get()[...].astype(F32)
    total_ref[...] = total
    for j in range(8):
        for b in range(8):
            moved_ref[j, 4 * b : 4 * b + 4, :] = total_ref[4 * j : 4 * j + 4, 128 * b : 128 * b + 128]
    out.ref[...] = moved_ref[...].astype(BF16)
    out.send()


def bwd_own_body(low_ref, recv, start, qt, dmix, part, out, dk, dv, kt_ref):
    recv_ref, start_ref = recv.get(), start.get()
    flip_tiles(recv_ref, slice(128, 256), kt_ref)
    dk.ref[...] = jnp.zeros_like(dk.ref)
    dv.ref[...] = jnp.zeros_like(dv.ref)
    qt_ref, dmix_ref, part_ref = qt.get(), dmix.get(), part.get()
    for i in range(TILES - 1, -1, -1):
        low = jnp.maximum(low_ref[i] - TILES, 0)
        dqt = backward_tiles(
            i, low, i + 1, 0, recv_ref, slice(128, 256), slice(256, 384), start_ref, qt_ref[i],
            tile_of(recv_ref, i, slice(0, 128)), dmix_ref[i], kt_ref, dk.ref, dv.ref, part_ref[i],
        )
        out.ref[2 * i : 2 * i + 2] = dqt.T.astype(BF16).reshape(2, 128, 128)
        blocks = slice(2 * i, 2 * i + 2)
        out.send((blocks,), (blocks, slice(0, 128)))
        dk.send((i,))
        dv.send((i,))


def add_body(dk, dv, back, out):
    next_ref, dk_ref, dv_ref = back.get(), dk.get(), dv.get()
    for b in range(HEADS):
        rows = slice((b % 2) * TOK, (b % 2 + 1) * TOK)
        out.ref[b, 0:128, :] = (dk_ref[b // 2, rows, :] + next_ref[b, 0:128, :].astype(F32)).astype(BF16)
        out.ref[b, 128:256, :] = (dv_ref[b // 2, rows, :] + next_ref[b, 128:256, :].astype(F32)).astype(BF16)
    out.send((), (slice(None), slice(128, 384)))


def gate_body(recv, w, out, gg):
    recv_ref = recv.get()
    for h in range(HEADS):
        gg.ref[:, h * TOK : (h + 1) * TOK] = flip(recv_ref[h, 128:256, :])
    gg.send()
    w_ref = w.get()
    total = dot(flip(recv_ref[0, 0:128, :]), w_ref[0:TOK, :])
    for h in range(1, HEADS):
        total = total + dot(flip(recv_ref[h, 0:128, :]), w_ref[h * TOK : (h + 1) * TOK, :])
    out.ref[...] = total.astype(BF16)
    out.send()


def final_body(recv, dq, dk, dv):
    recv_ref = recv.get()
    for n, made in enumerate((dq, dk, dv)):
        for h in range(HEADS):
            made.ref[:, h * TOK : (h + 1) * TOK] = recv_ref[h, 128 * n : 128 * n + 128, :]
        made.send()


def weight_body(recv, wg):
    recv_ref = recv.get()
    share = recv_ref[0].astype(F32)
    for n in range(1, HEADS):
        share = share + recv_ref[n].astype(F32)
    for b in range(8):
        wg.ref[:, 128 * b : 128 * b + 128] = share[4 * b : 4 * b + 4, :]
    wg.send()


def plane_exchange(blocks):
    return lax.all_to_all(blocks, PLANE_AXES, 0, 0, tiled=True)


def shards(sizes, queries, keys, values, gates, cotangent, segment, w_out):
    dp, planes = sizes
    q, k, v, gate, cot, seg = (a[0] for a in (queries, keys, values, gates, cotangent, segment))
    cot_plane = lax.all_gather(cot, PLANE_AXES)
    rows = shape((TOK, 1024), BF16)
    head = shape((TILES, 128, TILE), F32)
    head16 = shape((TILES, 128, TILE), BF16)
    share = shape((4, 1024), F32)
    grad = shape((TILES, TILE, 128), F32)
    vt = pltpu.VMEM((TILES, 128, TILE), BF16)
    acc = pltpu.VMEM((TILES, TILE, 128), F32)

    (packed,) = call(pack_body, "hhh", [shape((8, 384, 128), BF16)], 1 << 16)(q, k, v)
    recv = plane_exchange(packed)

    replica, plane = lax.axis_index("dp"), lax.axis_index("z")
    who = jnp.stack([replica, plane]).astype(jnp.int32)
    place = plane * PLANE
    users = jnp.arange(USERS, dtype=jnp.int32)[:, None]
    first = jnp.sum((seg[None, :] < users).astype(jnp.int32), axis=1)
    mine = lax.dynamic_slice_in_dim(seg, place, PLANE)
    start = jnp.sum(jnp.where(mine[None, :] == users, first[:, None], 0), axis=0) - place
    low = (start[::TILE] + PLANE) // TILE
    start = start.reshape(8, 128)
    (gd,) = call(dgated_body, "hhh", [shape((8, 256, 128), BF16)], 1 << 28)(cot, gate, w_out)

    pair, gd, start, low, who = lax.optimization_barrier((recv[:, 128:384], gd, start, low, who))
    halo = lax.ppermute(pair, "z", [(i, i + 1) for i in range(planes - 1)])
    gd_recv = plane_exchange(gd)
    part, qt = call(fwd_own_body, "shh", [head, head16], 1 << 29, [vt])(low, recv, start)
    mixt, stats = call(fwd_halo_body, "shhhhh", [head, shape((8, 32, 128), F32)], 1 << 28, [vt], TIGHT, kept={1: (1, 32, 128)})(
        low, halo, start, qt, part, gd_recv
    )
    stats = plane_exchange(stats)

    only_q = {6: ((slice(None), slice(0, 128)), (8, 128, 128))}
    far = shape((32, 1024), BF16)
    gate_pack, dmix, dqt, back, own, *fars = call(
        middle_body, "sshhhhhhhh",
        [shape((8, 256, 128), BF16), head16, head, shape((8, 256, 128), BF16), shape((32, 1024), F32), far, far, far],
        1 << 29, [vt, acc, acc, pltpu.VMEM((128, 1024), F32)], held=only_q,
    )(low, who, mixt, gd_recv, stats, halo, recv, start, qt, cot_plane)
    back = lax.ppermute(back, "z", [(i, i - 1) for i in range(1, planes)])
    fars = [lax.ppermute(x, "dp", [(i, (i + n + 1) % dp) for i in range(dp)]) for n, x in enumerate(fars)]
    moved = shape((8, 32, 128), BF16)
    (moved,) = call(replica_sum_body, "hhhh", [moved], 1 << 16, [pltpu.VMEM((32, 1024), F32), pltpu.VMEM((8, 32, 128), F32)])(own, *fars)
    route = []
    for d in range(dp):
        for z in range(planes):
            for r in range(8):
                route.append(((d * planes + z) * 8 + r, (r // 2 * planes + (r % 2) * 4 + d) * 8 + z))
    got_gate = plane_exchange(gate_pack)

    sent, dk, dv = call(
        bwd_own_body, "shhhhh", [shape((8, 384, 128), BF16), grad, grad], 1 << 30, [vt], kept={0: (8, 128, 128)}
    )(low, recv, start, qt, dmix, dqt)
    sent, got_gate = lax.optimization_barrier((sent, got_gate))
    (sent,) = call(add_body, "hhha", [shape((8, 384, 128), BF16)], 1 << 20, (), TIGHT, kept={0: (8, 256, 128)})(dk, dv, back, sent)
    sent, moved = lax.optimization_barrier((sent, moved))
    moved = lax.ppermute(moved, ("dp", "z", "x", "c"), route)
    got = plane_exchange(sent)
    out, gg = call(gate_body, "hh", [rows, rows], 1 << 28)(got_gate, w_out)
    moved, got = lax.optimization_barrier((moved, got))
    dq, dk, dv = call(final_body, "h", [rows] * 3, 1 << 20, (), ROOM)(got)
    (weight_grad,) = call(weight_body, "h", [share], 1 << 16, (), ROOM)(plane_exchange(moved))
    return out[None], dq[None], dk[None], dv[None], gg[None], weight_grad


def solution(mesh):
    dp, seq = mesh.shape["dp"], mesh.shape["seq"]
    planes = seq // 8
    grid = Mesh(mesh.devices.reshape(dp, planes, 4, 2), ("dp", "z", "x", "c"))
    tokens = P("dp", ("z", "x", "c"), None)
    return jax.shard_map(
        functools.partial(shards, (dp, planes)),
        mesh=grid,
        in_specs=(tokens,) * 5 + (P("dp", None), P()),
        out_specs=(tokens,) * 5 + (P(("dp", "z", "x", "c"), None),),
        check_vma=False,
    )
```

```python
import functools
import math

import jax
import jax.numpy as jnp
from jax import lax
from jax.experimental import pallas as pl
from jax.experimental.pallas import tpu as pltpu
from jax.sharding import Mesh
from jax.sharding import PartitionSpec as P

HEADS = 8
EPS = 1e-05
USERS = 32
TOK = 128
PLANE = 1024
TILE = 256
TILES = PLANE // TILE
SCALE = 1.0 / math.sqrt(128.0)
F32 = jnp.float32
BF16 = jnp.bfloat16
PLANE_AXES = ("x", "c")
VMEM_LIMIT = 60 * 1024 * 1024
ROOM = 30 * 1024 * 1024
TIGHT = 62_300_000

NN = (((1,), (0,)), ((), ()))
NT = (((1,), (1,)), ((), ()))
TN = (((0,), (0,)), ((), ()))


def dot(a, b, dims=NN):
    return lax.dot_general(a, b, dims, preferred_element_type=F32)


def flip(block):
    return block.astype(F32).T.astype(BF16)


class Held:
    def __init__(self, ref, copy):
        self.ref, self.copy = ref, copy

    def get(self):
        if self.copy is not None:
            self.copy.wait()
            self.copy = None
        return self.ref


class Made:
    def __init__(self, ref, target, log):
        self.ref, self.target, self.log = ref, target, log

    def send(self, src=(), dst=None):
        where = src if dst is None else dst
        self.log((self.ref.at[src] if src != () else self.ref, self.target.at[where] if where != () else self.target))


def call(body, places, outs, flops, scratch=(), limit=VMEM_LIMIT, sends=16, kept=None, held=None):
    outs, kept, held = list(outs), dict(kept or {}), dict(held or {})

    def build(*args):
        staged = [n for n, place in enumerate(places) if place == "h"]
        shapes = [held[n][1] if n in held else args[n].shape for n in staged]

        def whole(*refs):
            refs = list(refs)
            given, refs = refs[: len(args)], refs[len(args) :]
            results, refs = refs[: len(outs)], refs[len(outs) :]
            here, refs = refs[: len(staged)], refs[len(staged) :]
            made, refs = refs[: len(outs)], refs[len(outs) :]
            in_sems, out_sems, extra = refs[0], refs[1], refs[2:]
            for m, n in enumerate(staged):
                source = given[n].at[held[n][0]] if n in held else given[n]
                copy = pltpu.make_async_copy(source, here[m], in_sems.at[m])
                copy.start()
                given[n] = Held(here[m], copy)
            sent = []

            def log(pair):
                copy = pltpu.make_async_copy(pair[0], pair[1], out_sems.at[len(sent)])
                copy.start()
                sent.append(copy)

            body(*(g for g, place in zip(given, places) if place != "a"), *(Made(v, t, log) for v, t in zip(made, results)), *extra)
            for n in staged:
                given[n].get()
            for copy in sent:
                copy.wait()

        moved = sum(a.size * a.dtype.itemsize for a in args) + sum(o.size * o.dtype.itemsize for o in outs)
        return pl.pallas_call(
            whole,
            out_shape=outs,
            in_specs=[pl.BlockSpec(memory_space=pltpu.SMEM if place == "s" else pltpu.HBM) for place in places],
            out_specs=[pl.BlockSpec(memory_space=pltpu.HBM)] * len(outs),
            input_output_aliases={places.index("a"): 0} if "a" in places else {},
            scratch_shapes=[pltpu.VMEM(dims, args[n].dtype) for dims, n in zip(shapes, staged)]
            + [pltpu.VMEM(kept.get(m, o.shape), o.dtype) for m, o in enumerate(outs)]
            + [pltpu.SemaphoreType.DMA((len(staged) + 1,)), pltpu.SemaphoreType.DMA((sends,))]
            + list(scratch),
            compiler_params=pltpu.CompilerParams(vmem_limit_bytes=limit),
            cost_estimate=pl.CostEstimate(flops=flops, bytes_accessed=moved, transcendentals=0),
        )(*args)

    return build


def shape(dims, dtype):
    return jax.ShapeDtypeStruct(dims, dtype)


def pack_body(q, k, v, out):
    for n, held in enumerate((q, k, v)):
        ref = held.get()
        rows = slice(n * TOK, (n + 1) * TOK)
        for h in range(HEADS):
            out.ref[h, rows, :] = ref[:, h * TOK : (h + 1) * TOK]
        out.send((slice(None), rows))


def dgated_body(cot, gate, w, out):
    gate_ref = gate.get()
    for h in range(HEADS):
        out.ref[h, 0:128, :] = flip(gate_ref[:, h * TOK : (h + 1) * TOK])
    cotangent, w_ref = cot.get()[...], w.get()
    for h in range(HEADS):
        out.ref[h, 128:256, :] = dot(w_ref[h * TOK : (h + 1) * TOK, :], cotangent, NT).astype(BF16)
    out.send()


def tile_of(ref, j, rows):
    return ref[pl.ds(2 * j, 2), rows, :].reshape(TILE, 128)


def tile_mask(start_ref, i, first_key):
    start = jnp.concatenate([start_ref[2 * i : 2 * i + 1, :], start_ref[2 * i + 1 : 2 * i + 2, :]], axis=1)
    key_place = first_key + lax.broadcasted_iota(jnp.int32, (TILE, TILE), 0)
    query_place = i * TILE + lax.broadcasted_iota(jnp.int32, (TILE, TILE), 1)
    return (key_place >= start) & (key_place <= query_place)


def sigmoid(s):
    return 1.0 / (1.0 + jnp.exp(-s))


def flip_tiles(ref, rows, tiles):
    for t in range(HEADS):
        tiles[t // 2, :, (t % 2) * TOK : (t % 2 + 1) * TOK] = flip(ref[t, rows, :])


def forward_tiles(i, low, high, first, keys_ref, key_rows, start_ref, qt, vt_ref, total):
    def step(j, acc):
        s = dot(tile_of(keys_ref, j, key_rows), qt) * SCALE
        mask = tile_mask(start_ref, i, first + j * TILE)
        w = jnp.where(mask, s * sigmoid(s), 0.0).astype(BF16)
        return acc + dot(vt_ref[j], w)

    return lax.fori_loop(low, high, step, total)


def fwd_own_body(low_ref, recv, start, mixt, qt, vt_ref):
    recv_ref, start_ref = recv.get(), start.get()
    flip_tiles(recv_ref, slice(0, 128), qt.ref)
    qt.send()
    flip_tiles(recv_ref, slice(256, 384), vt_ref)
    for i in range(TILES):
        low = jnp.maximum(low_ref[i] - TILES, 0)
        mixt.ref[i] = forward_tiles(
            i, low, i + 1, 0, recv_ref, slice(128, 256), start_ref, qt.ref[i], vt_ref, jnp.zeros((128, TILE), F32)
        )
        mixt.send((i,))


def fwd_halo_body(low_ref, halo, start, qt, part, gd, mixt, stats, vt_ref):
    halo_ref, start_ref = halo.get(), start.get()
    flip_tiles(halo_ref, slice(128, 256), vt_ref)
    qt_ref, part_ref, gd_ref = qt.get(), part.get(), gd.get()
    for i in range(TILES):
        mixt.ref[i] = forward_tiles(
            i, low_ref[i], TILES, -PLANE, halo_ref, slice(0, 128), start_ref, qt_ref[i], vt_ref, part_ref[i]
        )
        mixt.send((i,))
        for b in (2 * i, 2 * i + 1):
            mix = mixt.ref[i, :, (b % 2) * TOK : (b % 2 + 1) * TOK]
            dn = gd_ref[b, 0:128, :].astype(F32) * gd_ref[b, 128:256, :].astype(F32)
            mean = jnp.sum(mix, axis=0, keepdims=True) * (1.0 / 128.0)
            centred = mix - mean
            rows = (
                mean,
                jnp.sum(centred * centred, axis=0, keepdims=True),
                jnp.sum(dn, axis=0, keepdims=True),
                jnp.sum(dn * centred, axis=0, keepdims=True),
            )
            for k, row in enumerate(rows):
                stats.ref[0, 8 * k + b : 8 * k + b + 1, :] = row
    for d in range(HEADS):
        stats.send((0,), (d,))


def finish(mixt_ref, gd_ref, stats_ref, gate_out, dmix_ref):
    means = [stats_ref[h, 0:8, :] for h in range(HEADS)]
    mean = sum(means) * (1.0 / HEADS)
    square = sum(stats_ref[h, 8:16, :] for h in range(HEADS))
    square = square + 128.0 * sum((m - mean) * (m - mean) for m in means)
    inverse = lax.rsqrt(square * (1.0 / 1024.0) + EPS)
    dmean = sum(stats_ref[h, 16:24, :] for h in range(HEADS)) * (1.0 / 1024.0)
    cross = sum(stats_ref[h, 24:32, :] + (means[h] - mean) * stats_ref[h, 16:24, :] for h in range(HEADS))
    dcross = cross * inverse * (1.0 / 1024.0)
    for b in range(HEADS):
        cols = slice((b % 2) * TOK, (b % 2 + 1) * TOK)
        one = slice(b, b + 1)
        inv = inverse[one, :]
        normed = (mixt_ref[b // 2, :, cols] - mean[one, :]) * inv
        gate = gd_ref[b, 0:128, :].astype(F32)
        dgated = gd_ref[b, 128:256, :].astype(F32)
        gate_out[b, 0:128, :] = (normed * gate).astype(BF16)
        gate_out[b, 128:256, :] = (normed * dgated).astype(BF16)
        dmix_ref[b // 2, :, cols] = (inv * (dgated * gate - dmean[one, :] - normed * dcross[one, :])).astype(BF16)


def backward_tiles(i, low, high, first, keys_ref, key_rows, value_rows, start_ref, qt, q, dmt, kt_ref, dk_ref, dv_ref, total):
    def step(j, acc):
        s = dot(tile_of(keys_ref, j, key_rows), qt) * SCALE
        mask = tile_mask(start_ref, i, first + j * TILE)
        sig = sigmoid(s)
        w = jnp.where(mask, s * sig, 0.0).astype(BF16)
        dw = dot(tile_of(keys_ref, j, value_rows), dmt)
        ds = jnp.where(mask, dw * (sig * (1.0 + s * (1.0 - sig))) * SCALE, 0.0).astype(BF16)
        dv_ref[j] += dot(w, dmt, NT)
        dk_ref[j] += dot(ds, q)
        return acc + dot(kt_ref[j], ds)

    return lax.fori_loop(low, high, step, total)


def middle_body(
    low_ref, who_ref, mixt, gd, stats, halo, recv, start, qt, cot, sent, dmix, dqt, back, own, far1, far2, far3, kt_ref, dk_ref, dv_ref, all_ref
):
    finish(mixt.get(), gd.get(), stats.get(), sent.ref, dmix.ref)
    sent.send((), (slice(None), slice(0, 256)))
    dmix.send()
    halo_ref, recv_ref, start_ref, qt_ref = halo.get(), recv.get(), start.get(), qt.get()
    flip_tiles(halo_ref, slice(0, 128), kt_ref)
    dk_ref[...] = jnp.zeros_like(dk_ref)
    dv_ref[...] = jnp.zeros_like(dv_ref)
    for i in range(TILES):
        dqt.ref[i] = backward_tiles(
            i, low_ref[i], TILES, -PLANE, halo_ref, slice(0, 128), slice(128, 256), start_ref, qt_ref[i],
            tile_of(recv_ref, i, slice(0, 128)), dmix.ref[i], kt_ref, dk_ref, dv_ref, jnp.zeros((128, TILE), F32),
        )
    dqt.send()
    for j in range(TILES):
        back.ref[2 * j : 2 * j + 2, 0:128, :] = dk_ref[j].astype(BF16).reshape(2, 128, 128)
        back.ref[2 * j : 2 * j + 2, 128:256, :] = dv_ref[j].astype(BF16).reshape(2, 128, 128)
    back.send()
    cot_ref = cot.get()
    total = dot(sent.ref[0, 0:128, :], cot_ref[0])
    for b in range(1, HEADS):
        total = total + dot(sent.ref[b, 0:128, :], cot_ref[b])
    all_ref[...] = total
    for n, made in enumerate((own, far1, far2, far3)):
        block = jnp.bitwise_and(who_ref[0] + n, 3)
        made.ref[...] = all_ref[pl.ds(pl.multiple_of(32 * block, 32), 32), :].astype(made.ref.dtype)
        made.send()


def replica_sum_body(own, got1, got2, got3, out, total_ref, moved_ref):
    total = own.get()[...]
    for got in (got1, got2, got3):
        total = total + got.get()[...].astype(F32)
    total_ref[...] = total
    for j in range(8):
        for b in range(8):
            moved_ref[j, 4 * b : 4 * b + 4, :] = total_ref[4 * j : 4 * j + 4, 128 * b : 128 * b + 128]
    out.ref[...] = moved_ref[...].astype(BF16)
    out.send()


def bwd_own_body(low_ref, recv, start, qt, dmix, part, out, dk, dv, kt_ref):
    recv_ref, start_ref = recv.get(), start.get()
    flip_tiles(recv_ref, slice(128, 256), kt_ref)
    dk.ref[...] = jnp.zeros_like(dk.ref)
    dv.ref[...] = jnp.zeros_like(dv.ref)
    qt_ref, dmix_ref, part_ref = qt.get(), dmix.get(), part.get()
    for i in range(TILES - 1, -1, -1):
        low = jnp.maximum(low_ref[i] - TILES, 0)
        dqt = backward_tiles(
            i, low, i + 1, 0, recv_ref, slice(128, 256), slice(256, 384), start_ref, qt_ref[i],
            tile_of(recv_ref, i, slice(0, 128)), dmix_ref[i], kt_ref, dk.ref, dv.ref, part_ref[i],
        )
        out.ref[2 * i : 2 * i + 2] = dqt.T.astype(BF16).reshape(2, 128, 128)
        blocks = slice(2 * i, 2 * i + 2)
        out.send((blocks,), (blocks, slice(256, 384)))
        dk.send((i,))
        dv.send((i,))


def add_body(dk, dv, back, out):
    next_ref, dk_ref, dv_ref = back.get(), dk.get(), dv.get()
    for b in range(HEADS):
        rows = slice((b % 2) * TOK, (b % 2 + 1) * TOK)
        out.ref[b, 0:128, :] = (dk_ref[b // 2, rows, :] + next_ref[b, 0:128, :].astype(F32)).astype(BF16)
        out.ref[b, 128:256, :] = (dv_ref[b // 2, rows, :] + next_ref[b, 128:256, :].astype(F32)).astype(BF16)
    out.send((), (slice(None), slice(384, 640)))


def final_body(recv, w, out, dq, dk, dv, gg):
    recv_ref = recv.get()
    for n, made in enumerate((dq, dk, dv)):
        for h in range(HEADS):
            made.ref[:, h * TOK : (h + 1) * TOK] = recv_ref[h, 256 + 128 * n : 384 + 128 * n, :]
        made.send()
    for h in range(HEADS):
        gg.ref[:, h * TOK : (h + 1) * TOK] = flip(recv_ref[h, 128:256, :])
    gg.send()
    w_ref = w.get()
    total = dot(flip(recv_ref[0, 0:128, :]), w_ref[0:TOK, :])
    for h in range(1, HEADS):
        total = total + dot(flip(recv_ref[h, 0:128, :]), w_ref[h * TOK : (h + 1) * TOK, :])
    out.ref[...] = total.astype(BF16)
    out.send()


def weight_body(who_ref, recv, wg):
    recv_ref = recv.get()
    rank = who_ref[2]
    share = recv_ref[0, rank].astype(F32)
    for n in range(1, HEADS):
        share = share + recv_ref[n, rank].astype(F32)
    for b in range(8):
        wg.ref[:, 128 * b : 128 * b + 128] = share[4 * b : 4 * b + 4, :]
    wg.send()


def plane_exchange(blocks):
    return lax.all_to_all(blocks, PLANE_AXES, 0, 0, tiled=True)


def shards(sizes, queries, keys, values, gates, cotangent, segment, w_out):
    dp, planes = sizes
    q, k, v, gate, cot, seg = (a[0] for a in (queries, keys, values, gates, cotangent, segment))
    cot_plane = lax.all_gather(cot, PLANE_AXES)
    rows = shape((TOK, 1024), BF16)
    head = shape((TILES, 128, TILE), F32)
    head16 = shape((TILES, 128, TILE), BF16)
    share = shape((4, 1024), F32)
    grad = shape((TILES, TILE, 128), F32)
    vt = pltpu.VMEM((TILES, 128, TILE), BF16)
    acc = pltpu.VMEM((TILES, TILE, 128), F32)

    (packed,) = call(pack_body, "hhh", [shape((8, 384, 128), BF16)], 1 << 16)(q, k, v)
    recv = plane_exchange(packed)

    replica, plane = lax.axis_index("dp"), lax.axis_index("z")
    who = jnp.stack([replica, plane, lax.axis_index(PLANE_AXES)]).astype(jnp.int32)
    place = plane * PLANE
    users = jnp.arange(USERS, dtype=jnp.int32)[:, None]
    first = jnp.sum((seg[None, :] < users).astype(jnp.int32), axis=1)
    mine = lax.dynamic_slice_in_dim(seg, place, PLANE)
    start = jnp.sum(jnp.where(mine[None, :] == users, first[:, None], 0), axis=0) - place
    low = (start[::TILE] + PLANE) // TILE
    start = start.reshape(8, 128)
    (gd,) = call(dgated_body, "hhh", [shape((8, 256, 128), BF16)], 1 << 28)(cot, gate, w_out)

    pair, gd, start, low, who = lax.optimization_barrier((recv[:, 128:384], gd, start, low, who))
    halo = lax.ppermute(pair, "z", [(i, i + 1) for i in range(planes - 1)])
    gd_recv = plane_exchange(gd)
    part, qt = call(fwd_own_body, "shh", [head, head16], 1 << 29, [vt])(low, recv, start)
    mixt, stats = call(fwd_halo_body, "shhhhh", [head, shape((8, 32, 128), F32)], 1 << 28, [vt], TIGHT, kept={1: (1, 32, 128)})(
        low, halo, start, qt, part, gd_recv
    )
    stats = plane_exchange(stats)

    only_q = {6: ((slice(None), slice(0, 128)), (8, 128, 128))}
    far = shape((32, 1024), BF16)
    sent, dmix, dqt, back, own, *fars = call(
        middle_body, "sshhhhhhhh",
        [shape((8, 640, 128), BF16), head16, head, shape((8, 256, 128), BF16), shape((32, 1024), F32), far, far, far],
        1 << 29, [vt, acc, acc, pltpu.VMEM((128, 1024), F32)], kept={0: (8, 256, 128)}, held=only_q,
    )(low, who, mixt, gd_recv, stats, halo, recv, start, qt, cot_plane)
    back = lax.ppermute(back, "z", [(i, i - 1) for i in range(1, planes)])
    fars = [lax.ppermute(x, "dp", [(i, (i + n + 1) % dp) for i in range(dp)]) for n, x in enumerate(fars)]
    moved = shape((8, 32, 128), BF16)
    (moved,) = call(replica_sum_body, "hhhh", [moved], 1 << 16, [pltpu.VMEM((32, 1024), F32), pltpu.VMEM((8, 32, 128), F32)])(own, *fars)
    route = []
    for d in range(dp):
        for z in range(planes):
            for r in range(8):
                route.append(((d * planes + z) * 8 + r, (r // 2 * planes + (r % 2) * 4 + d) * 8 + z))

    sent, dk, dv = call(
        bwd_own_body, "shhhhha", [shape((8, 640, 128), BF16), grad, grad], 1 << 30, [vt], kept={0: (8, 128, 128)}
    )(low, recv, start, qt, dmix, dqt, sent)
    (sent,) = call(add_body, "hhha", [shape((8, 640, 128), BF16)], 1 << 20, (), TIGHT, kept={0: (8, 256, 128)})(dk, dv, back, sent)
    sent, moved = lax.optimization_barrier((sent, moved))
    moved = lax.ppermute(moved, ("dp", "z", "x", "c"), route)
    got = plane_exchange(sent)
    shares = lax.all_gather(moved, PLANE_AXES)
    out, dq, dk, dv, gg = call(final_body, "hh", [rows] * 5, 1 << 28, (), ROOM)(got, w_out)
    (weight_grad,) = call(weight_body, "sh", [share], 1 << 16)(who, shares)
    return out[None], dq[None], dk[None], dv[None], gg[None], weight_grad


def solution(mesh):
    dp, seq = mesh.shape["dp"], mesh.shape["seq"]
    planes = seq // 8
    grid = Mesh(mesh.devices.reshape(dp, planes, 4, 2), ("dp", "z", "x", "c"))
    tokens = P("dp", ("z", "x", "c"), None)
    return jax.shard_map(
        functools.partial(shards, (dp, planes)),
        mesh=grid,
        in_specs=(tokens,) * 5 + (P("dp", None), P()),
        out_specs=(tokens,) * 5 + (P(("dp", "z", "x", "c"), None),),
        check_vma=False,
    )
```

```python
import functools
import math

import jax
import jax.numpy as jnp
from jax import lax
from jax.experimental import pallas as pl
from jax.experimental.pallas import tpu as pltpu
from jax.sharding import Mesh
from jax.sharding import PartitionSpec as P

HEADS = 8
EPS = 1e-05
USERS = 32
TOK = 128
PLANE = 1024
TILE = 256
TILES = PLANE // TILE
SCALE = 1.0 / math.sqrt(128.0)
F32 = jnp.float32
BF16 = jnp.bfloat16
PLANE_AXES = ("x", "c")
VMEM_LIMIT = 60 * 1024 * 1024
ROOM = 30 * 1024 * 1024

NN = (((1,), (0,)), ((), ()))
NT = (((1,), (1,)), ((), ()))
TN = (((0,), (0,)), ((), ()))


def dot(a, b, dims=NN):
    return lax.dot_general(a, b, dims, preferred_element_type=F32)


def flip(block):
    return block.astype(F32).T.astype(BF16)


class Held:
    def __init__(self, ref, copy):
        self.ref, self.copy = ref, copy

    def get(self):
        if self.copy is not None:
            self.copy.wait()
            self.copy = None
        return self.ref


class Made:
    def __init__(self, ref, target, log):
        self.ref, self.target, self.log = ref, target, log

    def send(self, src=(), dst=None):
        where = src if dst is None else dst
        self.log((self.ref.at[src] if src != () else self.ref, self.target.at[where] if where != () else self.target))


def call(body, places, outs, flops, scratch=(), limit=VMEM_LIMIT, sends=16, kept=None, held=None):
    outs, kept, held = list(outs), dict(kept or {}), dict(held or {})

    def build(*args):
        staged = [n for n, place in enumerate(places) if place == "h"]
        shapes = [held[n][1] if n in held else args[n].shape for n in staged]

        def whole(*refs):
            refs = list(refs)
            given, refs = refs[: len(args)], refs[len(args) :]
            results, refs = refs[: len(outs)], refs[len(outs) :]
            here, refs = refs[: len(staged)], refs[len(staged) :]
            made, refs = refs[: len(outs)], refs[len(outs) :]
            in_sems, out_sems, extra = refs[0], refs[1], refs[2:]
            for m, n in enumerate(staged):
                source = given[n].at[held[n][0]] if n in held else given[n]
                copy = pltpu.make_async_copy(source, here[m], in_sems.at[m])
                copy.start()
                given[n] = Held(here[m], copy)
            sent = []

            def log(pair):
                copy = pltpu.make_async_copy(pair[0], pair[1], out_sems.at[len(sent)])
                copy.start()
                sent.append(copy)

            body(*(g for g, place in zip(given, places) if place != "a"), *(Made(v, t, log) for v, t in zip(made, results)), *extra)
            for n in staged:
                given[n].get()
            for copy in sent:
                copy.wait()

        moved = sum(a.size * a.dtype.itemsize for a in args) + sum(o.size * o.dtype.itemsize for o in outs)
        return pl.pallas_call(
            whole,
            out_shape=outs,
            in_specs=[pl.BlockSpec(memory_space=pltpu.SMEM if place == "s" else pltpu.HBM) for place in places],
            out_specs=[pl.BlockSpec(memory_space=pltpu.HBM)] * len(outs),
            input_output_aliases={places.index("a"): 0} if "a" in places else {},
            scratch_shapes=[pltpu.VMEM(dims, args[n].dtype) for dims, n in zip(shapes, staged)]
            + [pltpu.VMEM(kept.get(m, o.shape), o.dtype) for m, o in enumerate(outs)]
            + [pltpu.SemaphoreType.DMA((len(staged) + 1,)), pltpu.SemaphoreType.DMA((sends,))]
            + list(scratch),
            compiler_params=pltpu.CompilerParams(vmem_limit_bytes=limit),
            cost_estimate=pl.CostEstimate(flops=flops, bytes_accessed=moved, transcendentals=0),
        )(*args)

    return build


def shape(dims, dtype):
    return jax.ShapeDtypeStruct(dims, dtype)


def pack_body(q, k, v, out):
    for n, held in enumerate((q, k, v)):
        ref = held.get()
        rows = slice(n * TOK, (n + 1) * TOK)
        for h in range(HEADS):
            out.ref[h, rows, :] = ref[:, h * TOK : (h + 1) * TOK]
        out.send((slice(None), rows))


def dgated_body(cot, gate, w, out):
    gate_ref = gate.get()
    for h in range(HEADS):
        out.ref[h, 0:128, :] = flip(gate_ref[:, h * TOK : (h + 1) * TOK])
    cotangent, w_ref = cot.get()[...], w.get()
    for h in range(HEADS):
        out.ref[h, 128:256, :] = dot(w_ref[h * TOK : (h + 1) * TOK, :], cotangent, NT).astype(BF16)
    out.send()


def tile_of(ref, j, rows):
    return ref[pl.ds(2 * j, 2), rows, :].reshape(TILE, 128)


def tile_mask(start_ref, i, first_key):
    start = jnp.concatenate([start_ref[2 * i : 2 * i + 1, :], start_ref[2 * i + 1 : 2 * i + 2, :]], axis=1)
    key_place = first_key + lax.broadcasted_iota(jnp.int32, (TILE, TILE), 0)
    query_place = i * TILE + lax.broadcasted_iota(jnp.int32, (TILE, TILE), 1)
    return (key_place >= start) & (key_place <= query_place)


def sigmoid(s):
    return 1.0 / (1.0 + jnp.exp(-s))


def flip_tiles(ref, rows, tiles):
    for t in range(HEADS):
        tiles[t // 2, :, (t % 2) * TOK : (t % 2 + 1) * TOK] = flip(ref[t, rows, :])


def forward_tiles(i, low, high, first, keys_ref, key_rows, start_ref, qt, vt_ref, total):
    def step(j, acc):
        s = dot(tile_of(keys_ref, j, key_rows), qt) * SCALE
        mask = tile_mask(start_ref, i, first + j * TILE)
        w = jnp.where(mask, s * sigmoid(s), 0.0).astype(BF16)
        return acc + dot(vt_ref[j], w)

    return lax.fori_loop(low, high, step, total)


def fwd_own_body(low_ref, recv, start, mixt, qt, vt_ref):
    recv_ref, start_ref = recv.get(), start.get()
    flip_tiles(recv_ref, slice(0, 128), qt.ref)
    qt.send()
    flip_tiles(recv_ref, slice(256, 384), vt_ref)
    for i in range(TILES):
        low = jnp.maximum(low_ref[i] - TILES, 0)
        mixt.ref[i] = forward_tiles(
            i, low, i + 1, 0, recv_ref, slice(128, 256), start_ref, qt.ref[i], vt_ref, jnp.zeros((128, TILE), F32)
        )
        mixt.send((i,))


def fwd_halo_body(low_ref, halo, start, qt, part, gd, mixt, stats, vt_ref):
    halo_ref, start_ref = halo.get(), start.get()
    flip_tiles(halo_ref, slice(128, 256), vt_ref)
    qt_ref, part_ref, gd_ref = qt.get(), part.get(), gd.get()
    for i in range(TILES):
        mixt.ref[i] = forward_tiles(
            i, low_ref[i], TILES, -PLANE, halo_ref, slice(0, 128), start_ref, qt_ref[i], vt_ref, part_ref[i]
        )
        mixt.send((i,))
        for b in (2 * i, 2 * i + 1):
            mix = mixt.ref[i, :, (b % 2) * TOK : (b % 2 + 1) * TOK]
            dn = gd_ref[b, 0:128, :].astype(F32) * gd_ref[b, 128:256, :].astype(F32)
            mean = jnp.sum(mix, axis=0, keepdims=True) * (1.0 / 128.0)
            centred = mix - mean
            rows = (
                mean,
                jnp.sum(centred * centred, axis=0, keepdims=True),
                jnp.sum(dn, axis=0, keepdims=True),
                jnp.sum(dn * centred, axis=0, keepdims=True),
            )
            for k, row in enumerate(rows):
                stats.ref[0, 8 * k + b : 8 * k + b + 1, :] = row
    for d in range(HEADS):
        stats.send((0,), (d,))


def finish(mixt_ref, gd_ref, stats_ref, gate_out, dmix_ref):
    means = [stats_ref[h, 0:8, :] for h in range(HEADS)]
    mean = sum(means) * (1.0 / HEADS)
    square = sum(stats_ref[h, 8:16, :] for h in range(HEADS))
    square = square + 128.0 * sum((m - mean) * (m - mean) for m in means)
    inverse = lax.rsqrt(square * (1.0 / 1024.0) + EPS)
    dmean = sum(stats_ref[h, 16:24, :] for h in range(HEADS)) * (1.0 / 1024.0)
    cross = sum(stats_ref[h, 24:32, :] + (means[h] - mean) * stats_ref[h, 16:24, :] for h in range(HEADS))
    dcross = cross * inverse * (1.0 / 1024.0)
    for b in range(HEADS):
        cols = slice((b % 2) * TOK, (b % 2 + 1) * TOK)
        one = slice(b, b + 1)
        inv = inverse[one, :]
        normed = (mixt_ref[b // 2, :, cols] - mean[one, :]) * inv
        gate = gd_ref[b, 0:128, :].astype(F32)
        dgated = gd_ref[b, 128:256, :].astype(F32)
        gate_out[b, 0:128, :] = (normed * gate).astype(BF16)
        gate_out[b, 128:256, :] = (normed * dgated).astype(BF16)
        dmix_ref[b // 2, :, cols] = (inv * (dgated * gate - dmean[one, :] - normed * dcross[one, :])).astype(BF16)


def backward_tiles(i, low, high, first, keys_ref, key_rows, value_rows, start_ref, qt, q, dmt, kt_ref, dk_ref, dv_ref, total):
    def step(j, acc):
        s = dot(tile_of(keys_ref, j, key_rows), qt) * SCALE
        mask = tile_mask(start_ref, i, first + j * TILE)
        sig = sigmoid(s)
        w = jnp.where(mask, s * sig, 0.0).astype(BF16)
        dw = dot(tile_of(keys_ref, j, value_rows), dmt)
        ds = jnp.where(mask, dw * (sig * (1.0 + s * (1.0 - sig))) * SCALE, 0.0).astype(BF16)
        dv_ref[j] += dot(w, dmt, NT)
        dk_ref[j] += dot(ds, q)
        return acc + dot(kt_ref[j], ds)

    return lax.fori_loop(low, high, step, total)


def middle_body(
    low_ref, mixt, gd, stats, halo, recv, start, qt, cot, sent, dmix, dqt, back, shares, kt_ref, dk_ref, dv_ref, all_ref, moved_ref
):
    finish(mixt.get(), gd.get(), stats.get(), sent.ref, dmix.ref)
    sent.send((), (slice(None), slice(0, 256)))
    dmix.send()
    halo_ref, recv_ref, start_ref, qt_ref = halo.get(), recv.get(), start.get(), qt.get()
    flip_tiles(halo_ref, slice(0, 128), kt_ref)
    dk_ref[...] = jnp.zeros_like(dk_ref)
    dv_ref[...] = jnp.zeros_like(dv_ref)
    for i in range(TILES):
        dqt.ref[i] = backward_tiles(
            i, low_ref[i], TILES, -PLANE, halo_ref, slice(0, 128), slice(128, 256), start_ref, qt_ref[i],
            tile_of(recv_ref, i, slice(0, 128)), dmix.ref[i], kt_ref, dk_ref, dv_ref, jnp.zeros((128, TILE), F32),
        )
    dqt.send()
    for j in range(TILES):
        back.ref[2 * j : 2 * j + 2, 0:128, :] = dk_ref[j].astype(BF16).reshape(2, 128, 128)
        back.ref[2 * j : 2 * j + 2, 128:256, :] = dv_ref[j].astype(BF16).reshape(2, 128, 128)
    back.send()
    cot_ref = cot.get()
    total = dot(sent.ref[0, 0:128, :], cot_ref[0])
    for b in range(1, HEADS):
        total = total + dot(sent.ref[b, 0:128, :], cot_ref[b])
    all_ref[...] = total
    for m in range(32):
        for b in range(8):
            moved_ref[m, 4 * b : 4 * b + 4, :] = all_ref[4 * m : 4 * m + 4, 128 * b : 128 * b + 128]
    shares.ref[...] = moved_ref[...].astype(BF16)
    shares.send()


def bwd_own_body(low_ref, recv, start, qt, dmix, part, back, out, kt_ref, dk_ref, dv_ref):
    recv_ref, start_ref = recv.get(), start.get()
    flip_tiles(recv_ref, slice(128, 256), kt_ref)
    dk_ref[...] = jnp.zeros_like(dk_ref)
    dv_ref[...] = jnp.zeros_like(dv_ref)
    qt_ref, dmix_ref, part_ref = qt.get(), dmix.get(), part.get()
    for i in range(TILES - 1, -1, -1):
        low = jnp.maximum(low_ref[i] - TILES, 0)
        dqt = backward_tiles(
            i, low, i + 1, 0, recv_ref, slice(128, 256), slice(256, 384), start_ref, qt_ref[i],
            tile_of(recv_ref, i, slice(0, 128)), dmix_ref[i], kt_ref, dk_ref, dv_ref, part_ref[i],
        )
        next_ref = back.get()
        blocks = slice(2 * i, 2 * i + 2)
        out.ref[blocks, 0:128, :] = dqt.T.astype(BF16).reshape(2, 128, 128)
        for b in (2 * i, 2 * i + 1):
            rows = slice((b % 2) * TOK, (b % 2 + 1) * TOK)
            out.ref[b, 128:256, :] = (dk_ref[i, rows, :] + next_ref[b, 0:128, :].astype(F32)).astype(BF16)
            out.ref[b, 256:384, :] = (dv_ref[i, rows, :] + next_ref[b, 128:256, :].astype(F32)).astype(BF16)
        out.send((blocks,), (blocks, slice(256, 640)))


def final_body(recv, w, piece, out, dq, dk, dv, gg, wg):
    piece_ref = piece.get()
    for b in range(8):
        wg.ref[:, 128 * b : 128 * b + 128] = piece_ref[4 * b : 4 * b + 4, :]
    wg.send()
    recv_ref = recv.get()
    for n, made in enumerate((dq, dk, dv)):
        for h in range(HEADS):
            made.ref[:, h * TOK : (h + 1) * TOK] = recv_ref[h, 256 + 128 * n : 384 + 128 * n, :]
        made.send()
    for h in range(HEADS):
        gg.ref[:, h * TOK : (h + 1) * TOK] = flip(recv_ref[h, 128:256, :])
    gg.send()
    w_ref = w.get()
    total = dot(flip(recv_ref[0, 0:128, :]), w_ref[0:TOK, :])
    for h in range(1, HEADS):
        total = total + dot(flip(recv_ref[h, 0:128, :]), w_ref[h * TOK : (h + 1) * TOK, :])
    out.ref[...] = total.astype(BF16)
    out.send()


def plane_exchange(blocks):
    return lax.all_to_all(blocks, PLANE_AXES, 0, 0, tiled=True)


def shards(sizes, queries, keys, values, gates, cotangent, segment, w_out):
    dp, planes = sizes
    q, k, v, gate, cot, seg = (a[0] for a in (queries, keys, values, gates, cotangent, segment))
    cot_plane = lax.all_gather(cot, PLANE_AXES)
    rows = shape((TOK, 1024), BF16)
    head = shape((TILES, 128, TILE), F32)
    head16 = shape((TILES, 128, TILE), BF16)
    share = shape((4, 1024), F32)
    vt = pltpu.VMEM((TILES, 128, TILE), BF16)
    acc = pltpu.VMEM((TILES, TILE, 128), F32)

    (packed,) = call(pack_body, "hhh", [shape((8, 384, 128), BF16)], 1 << 16)(q, k, v)
    recv = plane_exchange(packed)

    plane = lax.axis_index("z")
    place = plane * PLANE
    users = jnp.arange(USERS, dtype=jnp.int32)[:, None]
    first = jnp.sum((seg[None, :] < users).astype(jnp.int32), axis=1)
    mine = lax.dynamic_slice_in_dim(seg, place, PLANE)
    start = jnp.sum(jnp.where(mine[None, :] == users, first[:, None], 0), axis=0) - place
    low = (start[::TILE] + PLANE) // TILE
    start = start.reshape(8, 128)
    (gd,) = call(dgated_body, "hhh", [shape((8, 256, 128), BF16)], 1 << 28)(cot, gate, w_out)

    pair, gd, start, low = lax.optimization_barrier((recv[:, 128:384], gd, start, low))
    halo = lax.ppermute(pair, "z", [(i, i + 1) for i in range(planes - 1)])
    gd_recv = plane_exchange(gd)
    part, qt = call(fwd_own_body, "shh", [head, head16], 1 << 29, [vt])(low, recv, start)
    mixt, stats = call(fwd_halo_body, "shhhhh", [head, shape((8, 32, 128), F32)], 1 << 28, [vt], kept={1: (1, 32, 128)})(
        low, halo, start, qt, part, gd_recv
    )
    stats = plane_exchange(stats)

    only_q = {5: ((slice(None), slice(0, 128)), (8, 128, 128))}
    sent, dmix, dqt, back, shares = call(
        middle_body, "shhhhhhhh",
        [shape((8, 640, 128), BF16), head16, head, shape((8, 256, 128), BF16), shape((32, 32, 128), BF16)],
        1 << 29, [vt, acc, acc, pltpu.VMEM((128, 1024), F32), pltpu.VMEM((32, 32, 128), F32)],
        kept={0: (8, 256, 128)}, held=only_q,
    )(low, mixt, gd_recv, stats, halo, recv, start, qt, cot_plane)
    back = lax.ppermute(back, "z", [(i, i - 1) for i in range(1, planes)])
    shares = lax.all_to_all(shares, ("dp", "z"), 0, 0, tiled=True)
    back, shares = lax.optimization_barrier((back, shares))
    (sent,) = call(
        bwd_own_body, "shhhhhha", [shape((8, 640, 128), BF16)], 1 << 30, [vt, acc, acc], kept={0: (8, 384, 128)}
    )(low, recv, start, qt, dmix, dqt, back, sent)
    got = plane_exchange(sent)
    piece = jnp.sum(shares.astype(F32), axis=0)
    route = []
    for d in range(dp):
        for z in range(planes):
            for r in range(8):
                rank = 32 * r + d * planes + z
                route.append(((d * planes + z) * 8 + r, rank))
    piece = lax.ppermute(piece, ("dp", "z", "x", "c"), route)
    out, dq, dk, dv, gg, weight_grad = call(final_body, "hhh", [rows] * 5 + [share], 1 << 28, (), ROOM)(got, w_out, piece)
    return out[None], dq[None], dk[None], dv[None], gg[None], weight_grad


def solution(mesh):
    dp, seq = mesh.shape["dp"], mesh.shape["seq"]
    planes = seq // 8
    grid = Mesh(mesh.devices.reshape(dp, planes, 4, 2), ("dp", "z", "x", "c"))
    tokens = P("dp", ("z", "x", "c"), None)
    return jax.shard_map(
        functools.partial(shards, (dp, planes)),
        mesh=grid,
        in_specs=(tokens,) * 5 + (P("dp", None), P()),
        out_specs=(tokens,) * 5 + (P(("dp", "z", "x", "c"), None),),
        check_vma=False,
    )
```

```python
import functools
import math

import jax
import jax.numpy as jnp
from jax import lax
from jax.experimental import pallas as pl
from jax.experimental.pallas import tpu as pltpu
from jax.sharding import Mesh
from jax.sharding import PartitionSpec as P

HEADS = 8
EPS = 1e-05
USERS = 32
TOK = 128
PLANE = 1024
TILE = 256
TILES = PLANE // TILE
SCALE = 1.0 / math.sqrt(128.0)
F32 = jnp.float32
BF16 = jnp.bfloat16
PLANE_AXES = ("x", "c")
VMEM_LIMIT = 60 * 1024 * 1024
ROOM = 30 * 1024 * 1024
TIGHT = 62_300_000

NN = (((1,), (0,)), ((), ()))
NT = (((1,), (1,)), ((), ()))
TN = (((0,), (0,)), ((), ()))


def dot(a, b, dims=NN):
    return lax.dot_general(a, b, dims, preferred_element_type=F32)


def flip(block):
    return block.astype(F32).T.astype(BF16)


class Held:
    def __init__(self, ref, copy):
        self.ref, self.copy = ref, copy

    def get(self):
        if self.copy is not None:
            self.copy.wait()
            self.copy = None
        return self.ref


class Made:
    def __init__(self, ref, target, log):
        self.ref, self.target, self.log = ref, target, log

    def send(self, src=(), dst=None):
        where = src if dst is None else dst
        self.log((self.ref.at[src] if src != () else self.ref, self.target.at[where] if where != () else self.target))


def call(body, places, outs, flops, scratch=(), limit=VMEM_LIMIT, sends=16, kept=None, held=None):
    outs, kept, held = list(outs), dict(kept or {}), dict(held or {})

    def build(*args):
        staged = [n for n, place in enumerate(places) if place == "h"]
        shapes = [held[n][1] if n in held else args[n].shape for n in staged]

        def whole(*refs):
            refs = list(refs)
            given, refs = refs[: len(args)], refs[len(args) :]
            results, refs = refs[: len(outs)], refs[len(outs) :]
            here, refs = refs[: len(staged)], refs[len(staged) :]
            made, refs = refs[: len(outs)], refs[len(outs) :]
            in_sems, out_sems, extra = refs[0], refs[1], refs[2:]
            for m, n in enumerate(staged):
                source = given[n].at[held[n][0]] if n in held else given[n]
                copy = pltpu.make_async_copy(source, here[m], in_sems.at[m])
                copy.start()
                given[n] = Held(here[m], copy)
            sent = []

            def log(pair):
                copy = pltpu.make_async_copy(pair[0], pair[1], out_sems.at[len(sent)])
                copy.start()
                sent.append(copy)

            body(*(g for g, place in zip(given, places) if place != "a"), *(Made(v, t, log) for v, t in zip(made, results)), *extra)
            for n in staged:
                given[n].get()
            for copy in sent:
                copy.wait()

        moved = sum(a.size * a.dtype.itemsize for a in args) + sum(o.size * o.dtype.itemsize for o in outs)
        return pl.pallas_call(
            whole,
            out_shape=outs,
            in_specs=[pl.BlockSpec(memory_space=pltpu.SMEM if place == "s" else pltpu.HBM) for place in places],
            out_specs=[pl.BlockSpec(memory_space=pltpu.HBM)] * len(outs),
            input_output_aliases={places.index("a"): 0} if "a" in places else {},
            scratch_shapes=[pltpu.VMEM(dims, args[n].dtype) for dims, n in zip(shapes, staged)]
            + [pltpu.VMEM(kept.get(m, o.shape), o.dtype) for m, o in enumerate(outs)]
            + [pltpu.SemaphoreType.DMA((len(staged) + 1,)), pltpu.SemaphoreType.DMA((sends,))]
            + list(scratch),
            compiler_params=pltpu.CompilerParams(vmem_limit_bytes=limit),
            cost_estimate=pl.CostEstimate(flops=flops, bytes_accessed=moved, transcendentals=0),
        )(*args)

    return build


def shape(dims, dtype):
    return jax.ShapeDtypeStruct(dims, dtype)


def pack_body(q, k, v, out):
    for n, held in enumerate((q, k, v)):
        ref = held.get()
        rows = slice(n * TOK, (n + 1) * TOK)
        for h in range(HEADS):
            out.ref[h, rows, :] = ref[:, h * TOK : (h + 1) * TOK]
        out.send((slice(None), rows))


def dgated_body(cot, gate, w, out):
    gate_ref = gate.get()
    for h in range(HEADS):
        out.ref[h, 0:128, :] = flip(gate_ref[:, h * TOK : (h + 1) * TOK])
    cotangent, w_ref = cot.get()[...], w.get()
    for h in range(HEADS):
        out.ref[h, 128:256, :] = dot(w_ref[h * TOK : (h + 1) * TOK, :], cotangent, NT).astype(BF16)
    out.send()


def tile_of(ref, j, rows):
    return ref[pl.ds(2 * j, 2), rows, :].reshape(TILE, 128)


def tile_mask(start_ref, i, first_key):
    start = jnp.concatenate([start_ref[2 * i : 2 * i + 1, :], start_ref[2 * i + 1 : 2 * i + 2, :]], axis=1)
    key_place = first_key + lax.broadcasted_iota(jnp.int32, (TILE, TILE), 0)
    query_place = i * TILE + lax.broadcasted_iota(jnp.int32, (TILE, TILE), 1)
    return (key_place >= start) & (key_place <= query_place)


def sigmoid(s):
    return 1.0 / (1.0 + jnp.exp(-s))


def flip_tiles(ref, rows, tiles):
    for t in range(HEADS):
        tiles[t // 2, :, (t % 2) * TOK : (t % 2 + 1) * TOK] = flip(ref[t, rows, :])


def forward_tiles(i, low, high, first, keys_ref, key_rows, start_ref, qt, vt_ref, total):
    def step(j, acc):
        s = dot(tile_of(keys_ref, j, key_rows), qt) * SCALE
        mask = tile_mask(start_ref, i, first + j * TILE)
        w = jnp.where(mask, s * sigmoid(s), 0.0).astype(BF16)
        return acc + dot(vt_ref[j], w)

    return lax.fori_loop(low, high, step, total)


def fwd_own_body(low_ref, recv, start, mixt, qt, vt_ref):
    recv_ref, start_ref = recv.get(), start.get()
    flip_tiles(recv_ref, slice(0, 128), qt.ref)
    qt.send()
    flip_tiles(recv_ref, slice(256, 384), vt_ref)
    for i in range(TILES):
        low = jnp.maximum(low_ref[i] - TILES, 0)
        mixt.ref[i] = forward_tiles(
            i, low, i + 1, 0, recv_ref, slice(128, 256), start_ref, qt.ref[i], vt_ref, jnp.zeros((128, TILE), F32)
        )
        mixt.send((i,))


def fwd_halo_body(low_ref, halo, start, qt, part, gd, mixt, stats, vt_ref):
    halo_ref, start_ref = halo.get(), start.get()
    flip_tiles(halo_ref, slice(128, 256), vt_ref)
    qt_ref, part_ref, gd_ref = qt.get(), part.get(), gd.get()
    for i in range(TILES):
        mixt.ref[i] = forward_tiles(
            i, low_ref[i], TILES, -PLANE, halo_ref, slice(0, 128), start_ref, qt_ref[i], vt_ref, part_ref[i]
        )
        mixt.send((i,))
        for b in (2 * i, 2 * i + 1):
            mix = mixt.ref[i, :, (b % 2) * TOK : (b % 2 + 1) * TOK]
            dn = gd_ref[b, 0:128, :].astype(F32) * gd_ref[b, 128:256, :].astype(F32)
            mean = jnp.sum(mix, axis=0, keepdims=True) * (1.0 / 128.0)
            centred = mix - mean
            rows = (
                mean,
                jnp.sum(centred * centred, axis=0, keepdims=True),
                jnp.sum(dn, axis=0, keepdims=True),
                jnp.sum(dn * centred, axis=0, keepdims=True),
            )
            for k, row in enumerate(rows):
                stats.ref[0, 8 * k + b : 8 * k + b + 1, :] = row
    for d in range(HEADS):
        stats.send((0,), (d,))


def finish(mixt_ref, gd_ref, stats_ref, gate_out, dmix_ref):
    means = [stats_ref[h, 0:8, :] for h in range(HEADS)]
    mean = sum(means) * (1.0 / HEADS)
    square = sum(stats_ref[h, 8:16, :] for h in range(HEADS))
    square = square + 128.0 * sum((m - mean) * (m - mean) for m in means)
    inverse = lax.rsqrt(square * (1.0 / 1024.0) + EPS)
    dmean = sum(stats_ref[h, 16:24, :] for h in range(HEADS)) * (1.0 / 1024.0)
    cross = sum(stats_ref[h, 24:32, :] + (means[h] - mean) * stats_ref[h, 16:24, :] for h in range(HEADS))
    dcross = cross * inverse * (1.0 / 1024.0)
    for b in range(HEADS):
        cols = slice((b % 2) * TOK, (b % 2 + 1) * TOK)
        one = slice(b, b + 1)
        inv = inverse[one, :]
        normed = (mixt_ref[b // 2, :, cols] - mean[one, :]) * inv
        gate = gd_ref[b, 0:128, :].astype(F32)
        dgated = gd_ref[b, 128:256, :].astype(F32)
        gate_out[b, 0:128, :] = (normed * gate).astype(BF16)
        gate_out[b, 128:256, :] = (normed * dgated).astype(BF16)
        dmix_ref[b // 2, :, cols] = (inv * (dgated * gate - dmean[one, :] - normed * dcross[one, :])).astype(BF16)


def backward_tiles(i, low, high, first, keys_ref, key_rows, value_rows, start_ref, qt, q, dmt, kt_ref, dk_ref, dv_ref, total):
    def step(j, acc):
        s = dot(tile_of(keys_ref, j, key_rows), qt) * SCALE
        mask = tile_mask(start_ref, i, first + j * TILE)
        sig = sigmoid(s)
        w = jnp.where(mask, s * sig, 0.0).astype(BF16)
        dw = dot(tile_of(keys_ref, j, value_rows), dmt)
        ds = jnp.where(mask, dw * (sig * (1.0 + s * (1.0 - sig))) * SCALE, 0.0).astype(BF16)
        dv_ref[j] += dot(w, dmt, NT)
        dk_ref[j] += dot(ds, q)
        return acc + dot(kt_ref[j], ds)

    return lax.fori_loop(low, high, step, total)


def middle_body(
    low_ref, who_ref, mixt, gd, stats, halo, recv, start, qt, cot, sent, dmix, dqt, back, own, far1, far2, far3, kt_ref, dk_ref, dv_ref, all_ref
):
    finish(mixt.get(), gd.get(), stats.get(), sent.ref, dmix.ref)
    sent.send((), (slice(None), slice(0, 256)))
    dmix.send()
    halo_ref, recv_ref, start_ref, qt_ref = halo.get(), recv.get(), start.get(), qt.get()
    flip_tiles(halo_ref, slice(0, 128), kt_ref)
    dk_ref[...] = jnp.zeros_like(dk_ref)
    dv_ref[...] = jnp.zeros_like(dv_ref)
    for i in range(TILES):
        dqt.ref[i] = backward_tiles(
            i, low_ref[i], TILES, -PLANE, halo_ref, slice(0, 128), slice(128, 256), start_ref, qt_ref[i],
            tile_of(recv_ref, i, slice(0, 128)), dmix.ref[i], kt_ref, dk_ref, dv_ref, jnp.zeros((128, TILE), F32),
        )
    dqt.send()
    for j in range(TILES):
        back.ref[2 * j : 2 * j + 2, 0:128, :] = dk_ref[j].astype(BF16).reshape(2, 128, 128)
        back.ref[2 * j : 2 * j + 2, 128:256, :] = dv_ref[j].astype(BF16).reshape(2, 128, 128)
    back.send()
    cot_ref = cot.get()
    total = dot(sent.ref[0, 0:128, :], cot_ref[0])
    for b in range(1, HEADS):
        total = total + dot(sent.ref[b, 0:128, :], cot_ref[b])
    all_ref[...] = total
    for n, made in enumerate((own, far1, far2, far3)):
        block = jnp.bitwise_and(who_ref[0] + n, 3)
        made.ref[...] = all_ref[pl.ds(pl.multiple_of(32 * block, 32), 32), :].astype(made.ref.dtype)
        made.send()


def replica_sum_body(own, got1, got2, got3, out, total_ref, moved_ref):
    total = own.get()[...]
    for got in (got1, got2, got3):
        total = total + got.get()[...].astype(F32)
    total_ref[...] = total
    for j in range(8):
        for b in range(8):
            moved_ref[j, 4 * b : 4 * b + 4, :] = total_ref[4 * j : 4 * j + 4, 128 * b : 128 * b + 128]
    out.ref[...] = moved_ref[...].astype(BF16)
    out.send()


def bwd_own_body(low_ref, recv, start, qt, dmix, part, out, dk, dv, kt_ref):
    recv_ref, start_ref = recv.get(), start.get()
    flip_tiles(recv_ref, slice(128, 256), kt_ref)
    dk.ref[...] = jnp.zeros_like(dk.ref)
    dv.ref[...] = jnp.zeros_like(dv.ref)
    qt_ref, dmix_ref, part_ref = qt.get(), dmix.get(), part.get()
    for i in range(TILES - 1, -1, -1):
        low = jnp.maximum(low_ref[i] - TILES, 0)
        dqt = backward_tiles(
            i, low, i + 1, 0, recv_ref, slice(128, 256), slice(256, 384), start_ref, qt_ref[i],
            tile_of(recv_ref, i, slice(0, 128)), dmix_ref[i], kt_ref, dk.ref, dv.ref, part_ref[i],
        )
        out.ref[2 * i : 2 * i + 2] = dqt.T.astype(BF16).reshape(2, 128, 128)
        blocks = slice(2 * i, 2 * i + 2)
        out.send((blocks,), (blocks, slice(256, 384)))
        dk.send((i,))
        dv.send((i,))


def add_body(dk, dv, back, out):
    next_ref, dk_ref, dv_ref = back.get(), dk.get(), dv.get()
    for b in range(HEADS):
        rows = slice((b % 2) * TOK, (b % 2 + 1) * TOK)
        out.ref[b, 0:128, :] = (dk_ref[b // 2, rows, :] + next_ref[b, 0:128, :].astype(F32)).astype(BF16)
        out.ref[b, 128:256, :] = (dv_ref[b // 2, rows, :] + next_ref[b, 128:256, :].astype(F32)).astype(BF16)
    out.send((), (slice(None), slice(384, 640)))


def final_body(recv, w, out, dq, dk, dv, gg):
    recv_ref = recv.get()
    for n, made in enumerate((dq, dk, dv)):
        for h in range(HEADS):
            made.ref[:, h * TOK : (h + 1) * TOK] = recv_ref[h, 256 + 128 * n : 384 + 128 * n, :]
        made.send()
    for h in range(HEADS):
        gg.ref[:, h * TOK : (h + 1) * TOK] = flip(recv_ref[h, 128:256, :])
    gg.send()
    w_ref = w.get()
    total = dot(flip(recv_ref[0, 0:128, :]), w_ref[0:TOK, :])
    for h in range(1, HEADS):
        total = total + dot(flip(recv_ref[h, 0:128, :]), w_ref[h * TOK : (h + 1) * TOK, :])
    out.ref[...] = total.astype(BF16)
    out.send()


def weight_body(recv, wg):
    recv_ref = recv.get()
    share = recv_ref[0].astype(F32)
    for n in range(1, HEADS):
        share = share + recv_ref[n].astype(F32)
    for b in range(8):
        wg.ref[:, 128 * b : 128 * b + 128] = share[4 * b : 4 * b + 4, :]
    wg.send()


def plane_exchange(blocks):
    return lax.all_to_all(blocks, PLANE_AXES, 0, 0, tiled=True)


def shards(sizes, queries, keys, values, gates, cotangent, segment, w_out):
    dp, planes = sizes
    q, k, v, gate, cot, seg = (a[0] for a in (queries, keys, values, gates, cotangent, segment))
    cot_plane = lax.all_gather(cot, PLANE_AXES)
    rows = shape((TOK, 1024), BF16)
    head = shape((TILES, 128, TILE), F32)
    head16 = shape((TILES, 128, TILE), BF16)
    share = shape((4, 1024), F32)
    grad = shape((TILES, TILE, 128), F32)
    vt = pltpu.VMEM((TILES, 128, TILE), BF16)
    acc = pltpu.VMEM((TILES, TILE, 128), F32)

    (packed,) = call(pack_body, "hhh", [shape((8, 384, 128), BF16)], 1 << 16)(q, k, v)
    recv = plane_exchange(packed)

    replica, plane = lax.axis_index("dp"), lax.axis_index("z")
    who = jnp.stack([replica, plane]).astype(jnp.int32)
    place = plane * PLANE
    users = jnp.arange(USERS, dtype=jnp.int32)[:, None]
    first = jnp.sum((seg[None, :] < users).astype(jnp.int32), axis=1)
    mine = lax.dynamic_slice_in_dim(seg, place, PLANE)
    start = jnp.sum(jnp.where(mine[None, :] == users, first[:, None], 0), axis=0) - place
    low = (start[::TILE] + PLANE) // TILE
    start = start.reshape(8, 128)
    (gd,) = call(dgated_body, "hhh", [shape((8, 256, 128), BF16)], 1 << 28)(cot, gate, w_out)

    pair, gd, start, low, who = lax.optimization_barrier((recv[:, 128:384], gd, start, low, who))
    halo = lax.ppermute(pair, "z", [(i, i + 1) for i in range(planes - 1)])
    gd_recv = plane_exchange(gd)
    part, qt = call(fwd_own_body, "shh", [head, head16], 1 << 29, [vt])(low, recv, start)
    mixt, stats = call(fwd_halo_body, "shhhhh", [head, shape((8, 32, 128), F32)], 1 << 28, [vt], TIGHT, kept={1: (1, 32, 128)})(
        low, halo, start, qt, part, gd_recv
    )
    stats = plane_exchange(stats)

    only_q = {6: ((slice(None), slice(0, 128)), (8, 128, 128))}
    far = shape((32, 1024), BF16)
    sent, dmix, dqt, back, own, *fars = call(
        middle_body, "sshhhhhhhh",
        [shape((8, 640, 128), BF16), head16, head, shape((8, 256, 128), BF16), shape((32, 1024), F32), far, far, far],
        1 << 29, [vt, acc, acc, pltpu.VMEM((128, 1024), F32)], kept={0: (8, 256, 128)}, held=only_q,
    )(low, who, mixt, gd_recv, stats, halo, recv, start, qt, cot_plane)
    back = lax.ppermute(back, "z", [(i, i - 1) for i in range(1, planes)])
    fars = [lax.ppermute(x, "dp", [(i, (i + n + 1) % dp) for i in range(dp)]) for n, x in enumerate(fars)]
    moved = shape((8, 32, 128), BF16)
    (moved,) = call(replica_sum_body, "hhhh", [moved], 1 << 16, [pltpu.VMEM((32, 1024), F32), pltpu.VMEM((8, 32, 128), F32)])(own, *fars)
    route = []
    for d in range(dp):
        for z in range(planes):
            for r in range(8):
                route.append(((d * planes + z) * 8 + r, (r // 2 * planes + (r % 2) * 4 + d) * 8 + z))

    sent, dk, dv = call(
        bwd_own_body, "shhhhha", [shape((8, 640, 128), BF16), grad, grad], 1 << 30, [vt], kept={0: (8, 128, 128)}
    )(low, recv, start, qt, dmix, dqt, sent)
    (sent,) = call(add_body, "hhha", [shape((8, 640, 128), BF16)], 1 << 20, (), TIGHT, kept={0: (8, 256, 128)})(dk, dv, back, sent)
    sent, moved = lax.optimization_barrier((sent, moved))
    moved = lax.ppermute(moved, ("dp", "z", "x", "c"), route)
    got = plane_exchange(sent)
    moved, got = lax.optimization_barrier((moved, got))
    shares = plane_exchange(moved)
    out, dq, dk, dv, gg = call(final_body, "hh", [rows] * 5, 1 << 28, (), ROOM)(got, w_out)
    (weight_grad,) = call(weight_body, "h", [share], 1 << 16, (), ROOM)(shares)
    return out[None], dq[None], dk[None], dv[None], gg[None], weight_grad


def solution(mesh):
    dp, seq = mesh.shape["dp"], mesh.shape["seq"]
    planes = seq // 8
    grid = Mesh(mesh.devices.reshape(dp, planes, 4, 2), ("dp", "z", "x", "c"))
    tokens = P("dp", ("z", "x", "c"), None)
    return jax.shard_map(
        functools.partial(shards, (dp, planes)),
        mesh=grid,
        in_specs=(tokens,) * 5 + (P("dp", None), P()),
        out_specs=(tokens,) * 5 + (P(("dp", "z", "x", "c"), None),),
        check_vma=False,
    )
```

```python
import functools
import math

import jax
import jax.numpy as jnp
from jax import lax
from jax.experimental import pallas as pl
from jax.experimental.pallas import tpu as pltpu
from jax.sharding import Mesh
from jax.sharding import PartitionSpec as P

HEADS = 8
EPS = 1e-05
USERS = 32
TOK = 128
PLANE = 1024
TILE = 256
TILES = PLANE // TILE
SCALE = 1.0 / math.sqrt(128.0)
F32 = jnp.float32
BF16 = jnp.bfloat16
PLANE_AXES = ("x", "c")
VMEM_LIMIT = 60 * 1024 * 1024
ROOM = 30 * 1024 * 1024
TIGHT = 62_300_000

NN = (((1,), (0,)), ((), ()))
NT = (((1,), (1,)), ((), ()))
TN = (((0,), (0,)), ((), ()))


def dot(a, b, dims=NN):
    return lax.dot_general(a, b, dims, preferred_element_type=F32)


def flip(block):
    return block.astype(F32).T.astype(BF16)


class Held:
    def __init__(self, ref, copy):
        self.ref, self.copy = ref, copy

    def get(self):
        if self.copy is not None:
            self.copy.wait()
            self.copy = None
        return self.ref


class Made:
    def __init__(self, ref, target, log):
        self.ref, self.target, self.log = ref, target, log

    def send(self, src=(), dst=None):
        where = src if dst is None else dst
        self.log((self.ref.at[src] if src != () else self.ref, self.target.at[where] if where != () else self.target))


def call(body, places, outs, flops, scratch=(), limit=VMEM_LIMIT, sends=16, kept=None, held=None):
    outs, kept, held = list(outs), dict(kept or {}), dict(held or {})

    def build(*args):
        staged = [n for n, place in enumerate(places) if place == "h"]
        shapes = [held[n][1] if n in held else args[n].shape for n in staged]

        def whole(*refs):
            refs = list(refs)
            given, refs = refs[: len(args)], refs[len(args) :]
            results, refs = refs[: len(outs)], refs[len(outs) :]
            here, refs = refs[: len(staged)], refs[len(staged) :]
            made, refs = refs[: len(outs)], refs[len(outs) :]
            in_sems, out_sems, extra = refs[0], refs[1], refs[2:]
            for m, n in enumerate(staged):
                source = given[n].at[held[n][0]] if n in held else given[n]
                copy = pltpu.make_async_copy(source, here[m], in_sems.at[m])
                copy.start()
                given[n] = Held(here[m], copy)
            sent = []

            def log(pair):
                copy = pltpu.make_async_copy(pair[0], pair[1], out_sems.at[len(sent)])
                copy.start()
                sent.append(copy)

            body(*(g for g, place in zip(given, places) if place != "a"), *(Made(v, t, log) for v, t in zip(made, results)), *extra)
            for n in staged:
                given[n].get()
            for copy in sent:
                copy.wait()

        moved = sum(a.size * a.dtype.itemsize for a in args) + sum(o.size * o.dtype.itemsize for o in outs)
        return pl.pallas_call(
            whole,
            out_shape=outs,
            in_specs=[pl.BlockSpec(memory_space=pltpu.SMEM if place == "s" else pltpu.HBM) for place in places],
            out_specs=[pl.BlockSpec(memory_space=pltpu.HBM)] * len(outs),
            input_output_aliases={places.index("a"): 0} if "a" in places else {},
            scratch_shapes=[pltpu.VMEM(dims, args[n].dtype) for dims, n in zip(shapes, staged)]
            + [pltpu.VMEM(kept.get(m, o.shape), o.dtype) for m, o in enumerate(outs)]
            + [pltpu.SemaphoreType.DMA((len(staged) + 1,)), pltpu.SemaphoreType.DMA((sends,))]
            + list(scratch),
            compiler_params=pltpu.CompilerParams(vmem_limit_bytes=limit),
            cost_estimate=pl.CostEstimate(flops=flops, bytes_accessed=moved, transcendentals=0),
        )(*args)

    return build


def shape(dims, dtype):
    return jax.ShapeDtypeStruct(dims, dtype)


def pack_body(q, k, v, out):
    for n, held in enumerate((q, k, v)):
        ref = held.get()
        rows = slice(n * TOK, (n + 1) * TOK)
        for h in range(HEADS):
            out.ref[h, rows, :] = ref[:, h * TOK : (h + 1) * TOK]
        out.send((slice(None), rows))


def dgated_body(cot, gate, w, out):
    gate_ref = gate.get()
    for h in range(HEADS):
        out.ref[h, 0:128, :] = flip(gate_ref[:, h * TOK : (h + 1) * TOK])
    cotangent, w_ref = cot.get()[...], w.get()
    for h in range(HEADS):
        out.ref[h, 128:256, :] = dot(w_ref[h * TOK : (h + 1) * TOK, :], cotangent, NT).astype(BF16)
    out.send()


def tile_of(ref, j, rows):
    return ref[pl.ds(2 * j, 2), rows, :].reshape(TILE, 128)


def tile_mask(start_ref, i, first_key):
    start = jnp.concatenate([start_ref[2 * i : 2 * i + 1, :], start_ref[2 * i + 1 : 2 * i + 2, :]], axis=1)
    key_place = first_key + lax.broadcasted_iota(jnp.int32, (TILE, TILE), 0)
    query_place = i * TILE + lax.broadcasted_iota(jnp.int32, (TILE, TILE), 1)
    return (key_place >= start) & (key_place <= query_place)


def sigmoid(s):
    return 1.0 / (1.0 + jnp.exp(-s))


def flip_tiles(ref, rows, tiles):
    for t in range(HEADS):
        tiles[t // 2, :, (t % 2) * TOK : (t % 2 + 1) * TOK] = flip(ref[t, rows, :])


def forward_tiles(i, low, high, first, keys_ref, key_rows, start_ref, qt, vt_ref, total):
    def step(j, acc):
        s = dot(tile_of(keys_ref, j, key_rows), qt) * SCALE
        mask = tile_mask(start_ref, i, first + j * TILE)
        w = jnp.where(mask, s * sigmoid(s), 0.0).astype(BF16)
        return acc + dot(vt_ref[j], w)

    return lax.fori_loop(low, high, step, total)


def fwd_own_body(low_ref, recv, start, mixt, qt, vt_ref):
    recv_ref, start_ref = recv.get(), start.get()
    flip_tiles(recv_ref, slice(0, 128), qt.ref)
    qt.send()
    flip_tiles(recv_ref, slice(256, 384), vt_ref)
    for i in range(TILES):
        low = jnp.maximum(low_ref[i] - TILES, 0)
        mixt.ref[i] = forward_tiles(
            i, low, i + 1, 0, recv_ref, slice(128, 256), start_ref, qt.ref[i], vt_ref, jnp.zeros((128, TILE), F32)
        )
        mixt.send((i,))


def fwd_halo_body(low_ref, halo, start, qt, part, gd, mixt, stats, vt_ref):
    halo_ref, start_ref = halo.get(), start.get()
    flip_tiles(halo_ref, slice(128, 256), vt_ref)
    qt_ref, part_ref, gd_ref = qt.get(), part.get(), gd.get()
    for i in range(TILES):
        mixt.ref[i] = forward_tiles(
            i, low_ref[i], TILES, -PLANE, halo_ref, slice(0, 128), start_ref, qt_ref[i], vt_ref, part_ref[i]
        )
        mixt.send((i,))
        for b in (2 * i, 2 * i + 1):
            mix = mixt.ref[i, :, (b % 2) * TOK : (b % 2 + 1) * TOK]
            dn = gd_ref[b, 0:128, :].astype(F32) * gd_ref[b, 128:256, :].astype(F32)
            mean = jnp.sum(mix, axis=0, keepdims=True) * (1.0 / 128.0)
            centred = mix - mean
            rows = (
                mean,
                jnp.sum(centred * centred, axis=0, keepdims=True),
                jnp.sum(dn, axis=0, keepdims=True),
                jnp.sum(dn * centred, axis=0, keepdims=True),
            )
            for k, row in enumerate(rows):
                stats.ref[0, 8 * k + b : 8 * k + b + 1, :] = row
    for d in range(HEADS):
        stats.send((0,), (d,))


def finish(mixt_ref, gd_ref, stats_ref, gate_out, dmix_ref):
    means = [stats_ref[h, 0:8, :] for h in range(HEADS)]
    mean = sum(means) * (1.0 / HEADS)
    square = sum(stats_ref[h, 8:16, :] for h in range(HEADS))
    square = square + 128.0 * sum((m - mean) * (m - mean) for m in means)
    inverse = lax.rsqrt(square * (1.0 / 1024.0) + EPS)
    dmean = sum(stats_ref[h, 16:24, :] for h in range(HEADS)) * (1.0 / 1024.0)
    cross = sum(stats_ref[h, 24:32, :] + (means[h] - mean) * stats_ref[h, 16:24, :] for h in range(HEADS))
    dcross = cross * inverse * (1.0 / 1024.0)
    for b in range(HEADS):
        cols = slice((b % 2) * TOK, (b % 2 + 1) * TOK)
        one = slice(b, b + 1)
        inv = inverse[one, :]
        normed = (mixt_ref[b // 2, :, cols] - mean[one, :]) * inv
        gate = gd_ref[b, 0:128, :].astype(F32)
        dgated = gd_ref[b, 128:256, :].astype(F32)
        gate_out[b, 0:128, :] = (normed * gate).astype(BF16)
        gate_out[b, 128:256, :] = (normed * dgated).astype(BF16)
        dmix_ref[b // 2, :, cols] = (inv * (dgated * gate - dmean[one, :] - normed * dcross[one, :])).astype(BF16)


def backward_tiles(i, low, high, first, keys_ref, key_rows, value_rows, start_ref, qt, q, dmt, kt_ref, dk_ref, dv_ref, total):
    def step(j, acc):
        s = dot(tile_of(keys_ref, j, key_rows), qt) * SCALE
        mask = tile_mask(start_ref, i, first + j * TILE)
        sig = sigmoid(s)
        w = jnp.where(mask, s * sig, 0.0).astype(BF16)
        dw = dot(tile_of(keys_ref, j, value_rows), dmt)
        ds = jnp.where(mask, dw * (sig * (1.0 + s * (1.0 - sig))) * SCALE, 0.0).astype(BF16)
        dv_ref[j] += dot(w, dmt, NT)
        dk_ref[j] += dot(ds, q)
        return acc + dot(kt_ref[j], ds)

    return lax.fori_loop(low, high, step, total)


def middle_body(
    low_ref, who_ref, mixt, gd, stats, halo, recv, start, qt, near, mate, sent, dmix, dqt, back, own, far1, far2, far3, kt_ref, dk_ref, dv_ref, all_ref
):
    finish(mixt.get(), gd.get(), stats.get(), sent.ref, dmix.ref)
    sent.send((), (slice(None), slice(0, 256)))
    dmix.send()
    halo_ref, recv_ref, start_ref, qt_ref = halo.get(), recv.get(), start.get(), qt.get()
    flip_tiles(halo_ref, slice(0, 128), kt_ref)
    dk_ref[...] = jnp.zeros_like(dk_ref)
    dv_ref[...] = jnp.zeros_like(dv_ref)
    for i in range(TILES):
        dqt.ref[i] = backward_tiles(
            i, low_ref[i], TILES, -PLANE, halo_ref, slice(0, 128), slice(128, 256), start_ref, qt_ref[i],
            tile_of(recv_ref, i, slice(0, 128)), dmix.ref[i], kt_ref, dk_ref, dv_ref, jnp.zeros((128, TILE), F32),
        )
    dqt.send()
    for j in range(TILES):
        back.ref[2 * j : 2 * j + 2, 0:128, :] = dk_ref[j].astype(BF16).reshape(2, 128, 128)
        back.ref[2 * j : 2 * j + 2, 128:256, :] = dv_ref[j].astype(BF16).reshape(2, 128, 128)
    back.send()
    near_ref, mate_ref = near.get(), mate.get()
    total = jnp.zeros((128, 1024), F32)
    for n in range(4):
        first = 2 * jnp.bitwise_and(who_ref[2] + n, 3)
        total = total + dot(sent.ref[first + who_ref[3], 0:128, :], near_ref[n])
        total = total + dot(sent.ref[first + 1 - who_ref[3], 0:128, :], mate_ref[n])
    all_ref[...] = total
    for n, made in enumerate((own, far1, far2, far3)):
        block = jnp.bitwise_and(who_ref[0] + n, 3)
        made.ref[...] = all_ref[pl.ds(pl.multiple_of(32 * block, 32), 32), :].astype(made.ref.dtype)
        made.send()


def replica_sum_body(own, got1, got2, got3, out, total_ref, moved_ref):
    total = own.get()[...]
    for got in (got1, got2, got3):
        total = total + got.get()[...].astype(F32)
    total_ref[...] = total
    for j in range(8):
        for b in range(8):
            moved_ref[j, 4 * b : 4 * b + 4, :] = total_ref[4 * j : 4 * j + 4, 128 * b : 128 * b + 128]
    out.ref[...] = moved_ref[...].astype(BF16)
    out.send()


def bwd_own_body(low_ref, recv, start, qt, dmix, part, out, dk, dv, kt_ref):
    recv_ref, start_ref = recv.get(), start.get()
    flip_tiles(recv_ref, slice(128, 256), kt_ref)
    dk.ref[...] = jnp.zeros_like(dk.ref)
    dv.ref[...] = jnp.zeros_like(dv.ref)
    qt_ref, dmix_ref, part_ref = qt.get(), dmix.get(), part.get()
    for i in range(TILES - 1, -1, -1):
        low = jnp.maximum(low_ref[i] - TILES, 0)
        dqt = backward_tiles(
            i, low, i + 1, 0, recv_ref, slice(128, 256), slice(256, 384), start_ref, qt_ref[i],
            tile_of(recv_ref, i, slice(0, 128)), dmix_ref[i], kt_ref, dk.ref, dv.ref, part_ref[i],
        )
        out.ref[2 * i : 2 * i + 2] = dqt.T.astype(BF16).reshape(2, 128, 128)
        blocks = slice(2 * i, 2 * i + 2)
        out.send((blocks,), (blocks, slice(256, 384)))
        dk.send((i,))
        dv.send((i,))


def add_body(dk, dv, back, out):
    next_ref, dk_ref, dv_ref = back.get(), dk.get(), dv.get()
    for b in range(HEADS):
        rows = slice((b % 2) * TOK, (b % 2 + 1) * TOK)
        out.ref[b, 0:128, :] = (dk_ref[b // 2, rows, :] + next_ref[b, 0:128, :].astype(F32)).astype(BF16)
        out.ref[b, 128:256, :] = (dv_ref[b // 2, rows, :] + next_ref[b, 128:256, :].astype(F32)).astype(BF16)
    out.send((), (slice(None), slice(384, 640)))


def final_body(recv, w, out, dq, dk, dv, gg):
    recv_ref = recv.get()
    for n, made in enumerate((dq, dk, dv)):
        for h in range(HEADS):
            made.ref[:, h * TOK : (h + 1) * TOK] = recv_ref[h, 256 + 128 * n : 384 + 128 * n, :]
        made.send()
    for h in range(HEADS):
        gg.ref[:, h * TOK : (h + 1) * TOK] = flip(recv_ref[h, 128:256, :])
    gg.send()
    w_ref = w.get()
    total = dot(flip(recv_ref[0, 0:128, :]), w_ref[0:TOK, :])
    for h in range(1, HEADS):
        total = total + dot(flip(recv_ref[h, 0:128, :]), w_ref[h * TOK : (h + 1) * TOK, :])
    out.ref[...] = total.astype(BF16)
    out.send()


def weight_body(recv, wg):
    recv_ref = recv.get()
    share = recv_ref[0].astype(F32)
    for n in range(1, HEADS):
        share = share + recv_ref[n].astype(F32)
    for b in range(8):
        wg.ref[:, 128 * b : 128 * b + 128] = share[4 * b : 4 * b + 4, :]
    wg.send()


def plane_exchange(blocks):
    return lax.all_to_all(blocks, PLANE_AXES, 0, 0, tiled=True)


def shards(sizes, queries, keys, values, gates, cotangent, segment, w_out):
    dp, planes = sizes
    q, k, v, gate, cot, seg = (a[0] for a in (queries, keys, values, gates, cotangent, segment))
    rows = shape((TOK, 1024), BF16)
    head = shape((TILES, 128, TILE), F32)
    head16 = shape((TILES, 128, TILE), BF16)
    share = shape((4, 1024), F32)
    grad = shape((TILES, TILE, 128), F32)
    vt = pltpu.VMEM((TILES, 128, TILE), BF16)
    acc = pltpu.VMEM((TILES, TILE, 128), F32)

    (packed,) = call(pack_body, "hhh", [shape((8, 384, 128), BF16)], 1 << 16)(q, k, v)
    recv = plane_exchange(packed)

    replica, plane = lax.axis_index("dp"), lax.axis_index("z")
    who = jnp.stack([replica, plane, lax.axis_index("x"), lax.axis_index("c")]).astype(jnp.int32)
    place = plane * PLANE
    users = jnp.arange(USERS, dtype=jnp.int32)[:, None]
    first = jnp.sum((seg[None, :] < users).astype(jnp.int32), axis=1)
    mine = lax.dynamic_slice_in_dim(seg, place, PLANE)
    start = jnp.sum(jnp.where(mine[None, :] == users, first[:, None], 0), axis=0) - place
    low = (start[::TILE] + PLANE) // TILE
    start = start.reshape(8, 128)
    (gd,) = call(dgated_body, "hhh", [shape((8, 256, 128), BF16)], 1 << 28)(cot, gate, w_out)

    along = [lax.ppermute(cot, "x", [(i, (i - n) % 4) for i in range(4)]) for n in (1, 2, 3)]
    pair, gd, start, low, who, *along = lax.optimization_barrier((recv[:, 128:384], gd, start, low, who, *along))
    halo = lax.ppermute(pair, "z", [(i, i + 1) for i in range(planes - 1)])
    gd_recv = plane_exchange(gd)
    near = jnp.stack([cot, *along])
    part, qt = call(fwd_own_body, "shh", [head, head16], 1 << 29, [vt])(low, recv, start)
    halo, gd_recv, near, part = lax.optimization_barrier((halo, gd_recv, near, part))
    mate = lax.ppermute(near, "c", [(0, 1), (1, 0)])
    mixt, stats = call(fwd_halo_body, "shhhhh", [head, shape((8, 32, 128), F32)], 1 << 28, [vt], TIGHT, kept={1: (1, 32, 128)})(
        low, halo, start, qt, part, gd_recv
    )
    stats, near, mate = lax.optimization_barrier((stats, near, mate))
    stats = plane_exchange(stats)

    only_q = {6: ((slice(None), slice(0, 128)), (8, 128, 128))}
    far = shape((32, 1024), BF16)
    sent, dmix, dqt, back, own, *fars = call(
        middle_body, "sshhhhhhhhh",
        [shape((8, 640, 128), BF16), head16, head, shape((8, 256, 128), BF16), shape((32, 1024), F32), far, far, far],
        1 << 29, [vt, acc, acc, pltpu.VMEM((128, 1024), F32)], kept={0: (8, 256, 128)}, held=only_q,
    )(low, who, mixt, gd_recv, stats, halo, recv, start, qt, near, mate)
    back = lax.ppermute(back, "z", [(i, i - 1) for i in range(1, planes)])
    fars = [lax.ppermute(x, "dp", [(i, (i + n + 1) % dp) for i in range(dp)]) for n, x in enumerate(fars)]
    moved = shape((8, 32, 128), BF16)
    (moved,) = call(replica_sum_body, "hhhh", [moved], 1 << 16, [pltpu.VMEM((32, 1024), F32), pltpu.VMEM((8, 32, 128), F32)])(own, *fars)
    route = []
    for d in range(dp):
        for z in range(planes):
            for r in range(8):
                route.append(((d * planes + z) * 8 + r, (r // 2 * planes + (r % 2) * 4 + d) * 8 + z))

    sent, dk, dv = call(
        bwd_own_body, "shhhhha", [shape((8, 640, 128), BF16), grad, grad], 1 << 30, [vt], kept={0: (8, 128, 128)}
    )(low, recv, start, qt, dmix, dqt, sent)
    (sent,) = call(add_body, "hhha", [shape((8, 640, 128), BF16)], 1 << 20, (), TIGHT, kept={0: (8, 256, 128)})(dk, dv, back, sent)
    sent, moved = lax.optimization_barrier((sent, moved))
    moved = lax.ppermute(moved, ("dp", "z", "x", "c"), route)
    got = plane_exchange(sent)
    moved, got = lax.optimization_barrier((moved, got))
    shares = plane_exchange(moved)
    out, dq, dk, dv, gg = call(final_body, "hh", [rows] * 5, 1 << 28, (), ROOM)(got, w_out)
    (weight_grad,) = call(weight_body, "h", [share], 1 << 16, (), ROOM)(shares)
    return out[None], dq[None], dk[None], dv[None], gg[None], weight_grad


def solution(mesh):
    dp, seq = mesh.shape["dp"], mesh.shape["seq"]
    planes = seq // 8
    grid = Mesh(mesh.devices.reshape(dp, planes, 4, 2), ("dp", "z", "x", "c"))
    tokens = P("dp", ("z", "x", "c"), None)
    return jax.shard_map(
        functools.partial(shards, (dp, planes)),
        mesh=grid,
        in_specs=(tokens,) * 5 + (P("dp", None), P()),
        out_specs=(tokens,) * 5 + (P(("dp", "z", "x", "c"), None),),
        check_vma=False,
    )
```

```python
import functools
import math

import jax
import jax.numpy as jnp
from jax import lax
from jax.experimental import pallas as pl
from jax.experimental.pallas import tpu as pltpu
from jax.sharding import Mesh
from jax.sharding import PartitionSpec as P

HEADS = 8
EPS = 1e-05
USERS = 32
TOK = 128
PLANE = 1024
TILE = 256
TILES = PLANE // TILE
SCALE = 1.0 / math.sqrt(128.0)
F32 = jnp.float32
BF16 = jnp.bfloat16
PLANE_AXES = ("x", "c")
VMEM_LIMIT = 60 * 1024 * 1024
ROOM = 30 * 1024 * 1024
TIGHT = 62_300_000

NN = (((1,), (0,)), ((), ()))
NT = (((1,), (1,)), ((), ()))
TN = (((0,), (0,)), ((), ()))


def dot(a, b, dims=NN):
    return lax.dot_general(a, b, dims, preferred_element_type=F32)


def flip(block):
    return block.astype(F32).T.astype(BF16)


class Held:
    def __init__(self, ref, copy):
        self.ref, self.copy = ref, copy

    def get(self):
        if self.copy is not None:
            self.copy.wait()
            self.copy = None
        return self.ref


class Made:
    def __init__(self, ref, target, log):
        self.ref, self.target, self.log = ref, target, log

    def send(self, src=(), dst=None):
        where = src if dst is None else dst
        self.log((self.ref.at[src] if src != () else self.ref, self.target.at[where] if where != () else self.target))


def call(body, places, outs, flops, scratch=(), limit=VMEM_LIMIT, sends=16, kept=None, held=None):
    outs, kept, held = list(outs), dict(kept or {}), dict(held or {})

    def build(*args):
        staged = [n for n, place in enumerate(places) if place == "h"]
        shapes = [held[n][1] if n in held else args[n].shape for n in staged]

        def whole(*refs):
            refs = list(refs)
            given, refs = refs[: len(args)], refs[len(args) :]
            results, refs = refs[: len(outs)], refs[len(outs) :]
            here, refs = refs[: len(staged)], refs[len(staged) :]
            made, refs = refs[: len(outs)], refs[len(outs) :]
            in_sems, out_sems, extra = refs[0], refs[1], refs[2:]
            for m, n in enumerate(staged):
                source = given[n].at[held[n][0]] if n in held else given[n]
                copy = pltpu.make_async_copy(source, here[m], in_sems.at[m])
                copy.start()
                given[n] = Held(here[m], copy)
            sent = []

            def log(pair):
                copy = pltpu.make_async_copy(pair[0], pair[1], out_sems.at[len(sent)])
                copy.start()
                sent.append(copy)

            body(*(g for g, place in zip(given, places) if place != "a"), *(Made(v, t, log) for v, t in zip(made, results)), *extra)
            for n in staged:
                given[n].get()
            for copy in sent:
                copy.wait()

        moved = sum(a.size * a.dtype.itemsize for a in args) + sum(o.size * o.dtype.itemsize for o in outs)
        return pl.pallas_call(
            whole,
            out_shape=outs,
            in_specs=[pl.BlockSpec(memory_space=pltpu.SMEM if place == "s" else pltpu.HBM) for place in places],
            out_specs=[pl.BlockSpec(memory_space=pltpu.HBM)] * len(outs),
            input_output_aliases={places.index("a"): 0} if "a" in places else {},
            scratch_shapes=[pltpu.VMEM(dims, args[n].dtype) for dims, n in zip(shapes, staged)]
            + [pltpu.VMEM(kept.get(m, o.shape), o.dtype) for m, o in enumerate(outs)]
            + [pltpu.SemaphoreType.DMA((len(staged) + 1,)), pltpu.SemaphoreType.DMA((sends,))]
            + list(scratch),
            compiler_params=pltpu.CompilerParams(vmem_limit_bytes=limit),
            cost_estimate=pl.CostEstimate(flops=flops, bytes_accessed=moved, transcendentals=0),
        )(*args)

    return build


def shape(dims, dtype):
    return jax.ShapeDtypeStruct(dims, dtype)


def pack_body(q, k, v, out):
    for n, held in enumerate((q, k, v)):
        ref = held.get()
        rows = slice(n * TOK, (n + 1) * TOK)
        for h in range(HEADS):
            out.ref[h, rows, :] = ref[:, h * TOK : (h + 1) * TOK]
        out.send((slice(None), rows))


def dgated_body(cot, gate, w, out):
    gate_ref = gate.get()
    for h in range(HEADS):
        out.ref[h, 0:128, :] = flip(gate_ref[:, h * TOK : (h + 1) * TOK])
    cotangent, w_ref = cot.get()[...], w.get()
    for h in range(HEADS):
        out.ref[h, 128:256, :] = dot(w_ref[h * TOK : (h + 1) * TOK, :], cotangent, NT).astype(BF16)
    out.send()


def tile_of(ref, j, rows):
    return ref[pl.ds(2 * j, 2), rows, :].reshape(TILE, 128)


def tile_mask(start_ref, i, first_key):
    start = jnp.concatenate([start_ref[2 * i : 2 * i + 1, :], start_ref[2 * i + 1 : 2 * i + 2, :]], axis=1)
    key_place = first_key + lax.broadcasted_iota(jnp.int32, (TILE, TILE), 0)
    query_place = i * TILE + lax.broadcasted_iota(jnp.int32, (TILE, TILE), 1)
    return (key_place >= start) & (key_place <= query_place)


def sigmoid(s):
    return 1.0 / (1.0 + jnp.exp(-s))


def flip_tiles(ref, rows, tiles):
    for t in range(HEADS):
        tiles[t // 2, :, (t % 2) * TOK : (t % 2 + 1) * TOK] = flip(ref[t, rows, :])


def forward_tiles(i, low, high, first, keys_ref, key_rows, start_ref, qt, vt_ref, total):
    def step(j, acc):
        s = dot(tile_of(keys_ref, j, key_rows), qt) * SCALE
        mask = tile_mask(start_ref, i, first + j * TILE)
        w = jnp.where(mask, s * sigmoid(s), 0.0).astype(BF16)
        return acc + dot(vt_ref[j], w)

    return lax.fori_loop(low, high, step, total)


def fwd_own_body(low_ref, recv, start, mixt, qt, vt_ref):
    recv_ref, start_ref = recv.get(), start.get()
    flip_tiles(recv_ref, slice(0, 128), qt.ref)
    qt.send()
    flip_tiles(recv_ref, slice(256, 384), vt_ref)
    for i in range(TILES):
        low = jnp.maximum(low_ref[i] - TILES, 0)
        mixt.ref[i] = forward_tiles(
            i, low, i + 1, 0, recv_ref, slice(128, 256), start_ref, qt.ref[i], vt_ref, jnp.zeros((128, TILE), F32)
        )
        mixt.send((i,))


def fwd_halo_body(low_ref, halo, start, qt, part, gd, mixt, stats, vt_ref):
    halo_ref, start_ref = halo.get(), start.get()
    flip_tiles(halo_ref, slice(128, 256), vt_ref)
    qt_ref, part_ref, gd_ref = qt.get(), part.get(), gd.get()
    for i in range(TILES):
        mixt.ref[i] = forward_tiles(
            i, low_ref[i], TILES, -PLANE, halo_ref, slice(0, 128), start_ref, qt_ref[i], vt_ref, part_ref[i]
        )
        mixt.send((i,))
        for b in (2 * i, 2 * i + 1):
            mix = mixt.ref[i, :, (b % 2) * TOK : (b % 2 + 1) * TOK]
            dn = gd_ref[b, 0:128, :].astype(F32) * gd_ref[b, 128:256, :].astype(F32)
            mean = jnp.sum(mix, axis=0, keepdims=True) * (1.0 / 128.0)
            centred = mix - mean
            rows = (
                mean,
                jnp.sum(centred * centred, axis=0, keepdims=True),
                jnp.sum(dn, axis=0, keepdims=True),
                jnp.sum(dn * centred, axis=0, keepdims=True),
            )
            for k, row in enumerate(rows):
                stats.ref[0, 8 * k + b : 8 * k + b + 1, :] = row
    for d in range(HEADS):
        stats.send((0,), (d,))


def finish(mixt_ref, gd_ref, stats_ref, gate_out, dmix_ref):
    means = [stats_ref[h, 0:8, :] for h in range(HEADS)]
    mean = sum(means) * (1.0 / HEADS)
    square = sum(stats_ref[h, 8:16, :] for h in range(HEADS))
    square = square + 128.0 * sum((m - mean) * (m - mean) for m in means)
    inverse = lax.rsqrt(square * (1.0 / 1024.0) + EPS)
    dmean = sum(stats_ref[h, 16:24, :] for h in range(HEADS)) * (1.0 / 1024.0)
    cross = sum(stats_ref[h, 24:32, :] + (means[h] - mean) * stats_ref[h, 16:24, :] for h in range(HEADS))
    dcross = cross * inverse * (1.0 / 1024.0)
    for b in range(HEADS):
        cols = slice((b % 2) * TOK, (b % 2 + 1) * TOK)
        one = slice(b, b + 1)
        inv = inverse[one, :]
        normed = (mixt_ref[b // 2, :, cols] - mean[one, :]) * inv
        gate = gd_ref[b, 0:128, :].astype(F32)
        dgated = gd_ref[b, 128:256, :].astype(F32)
        gate_out[b, 0:128, :] = (normed * gate).astype(BF16)
        gate_out[b, 128:256, :] = (normed * dgated).astype(BF16)
        dmix_ref[b // 2, :, cols] = (inv * (dgated * gate - dmean[one, :] - normed * dcross[one, :])).astype(BF16)


def backward_tiles(i, low, high, first, keys_ref, key_rows, value_rows, start_ref, qt, q, dmt, kt_ref, dk_ref, dv_ref, total):
    def step(j, acc):
        s = dot(tile_of(keys_ref, j, key_rows), qt) * SCALE
        mask = tile_mask(start_ref, i, first + j * TILE)
        sig = sigmoid(s)
        w = jnp.where(mask, s * sig, 0.0).astype(BF16)
        dw = dot(tile_of(keys_ref, j, value_rows), dmt)
        ds = jnp.where(mask, dw * (sig * (1.0 + s * (1.0 - sig))) * SCALE, 0.0).astype(BF16)
        dv_ref[j] += dot(w, dmt, NT)
        dk_ref[j] += dot(ds, q)
        return acc + dot(kt_ref[j], ds)

    return lax.fori_loop(low, high, step, total)


def middle_body(
    low_ref, who_ref, mixt, gd, stats, halo, recv, start, qt, near, mate, sent, dmix, dqt, back, own, far1, far2, far3, kt_ref, dk_ref, dv_ref, all_ref
):
    finish(mixt.get(), gd.get(), stats.get(), sent.ref, dmix.ref)
    sent.send((), (slice(None), slice(0, 256)))
    dmix.send()
    halo_ref, recv_ref, start_ref, qt_ref = halo.get(), recv.get(), start.get(), qt.get()
    flip_tiles(halo_ref, slice(0, 128), kt_ref)
    dk_ref[...] = jnp.zeros_like(dk_ref)
    dv_ref[...] = jnp.zeros_like(dv_ref)
    for i in range(TILES):
        dqt.ref[i] = backward_tiles(
            i, low_ref[i], TILES, -PLANE, halo_ref, slice(0, 128), slice(128, 256), start_ref, qt_ref[i],
            tile_of(recv_ref, i, slice(0, 128)), dmix.ref[i], kt_ref, dk_ref, dv_ref, jnp.zeros((128, TILE), F32),
        )
    dqt.send()
    for j in range(TILES):
        back.ref[2 * j : 2 * j + 2, 0:128, :] = dk_ref[j].astype(BF16).reshape(2, 128, 128)
        back.ref[2 * j : 2 * j + 2, 128:256, :] = dv_ref[j].astype(BF16).reshape(2, 128, 128)
    back.send()
    near_ref, mate_ref = near.get(), mate.get()
    total = jnp.zeros((128, 1024), F32)
    for n in range(4):
        first = 2 * jnp.bitwise_and(who_ref[2] + n, 3)
        total = total + dot(sent.ref[first + who_ref[3], 0:128, :], near_ref[n])
        total = total + dot(sent.ref[first + 1 - who_ref[3], 0:128, :], mate_ref[n])
    all_ref[...] = total
    for n, made in enumerate((own, far1, far2, far3)):
        block = jnp.bitwise_and(who_ref[0] + n, 3)
        made.ref[...] = all_ref[pl.ds(pl.multiple_of(32 * block, 32), 32), :].astype(made.ref.dtype)
        made.send()


def replica_sum_body(own, got1, got2, got3, out, total_ref, moved_ref):
    total = own.get()[...]
    for got in (got1, got2, got3):
        total = total + got.get()[...].astype(F32)
    total_ref[...] = total
    for j in range(8):
        for b in range(8):
            moved_ref[j, 4 * b : 4 * b + 4, :] = total_ref[4 * j : 4 * j + 4, 128 * b : 128 * b + 128]
    out.ref[...] = moved_ref[...].astype(BF16)
    out.send()


def bwd_own_body(low_ref, recv, start, qt, dmix, part, out, dk, dv, kt_ref):
    recv_ref, start_ref = recv.get(), start.get()
    flip_tiles(recv_ref, slice(128, 256), kt_ref)
    dk.ref[...] = jnp.zeros_like(dk.ref)
    dv.ref[...] = jnp.zeros_like(dv.ref)
    qt_ref, dmix_ref, part_ref = qt.get(), dmix.get(), part.get()
    for i in range(TILES - 1, -1, -1):
        low = jnp.maximum(low_ref[i] - TILES, 0)
        dqt = backward_tiles(
            i, low, i + 1, 0, recv_ref, slice(128, 256), slice(256, 384), start_ref, qt_ref[i],
            tile_of(recv_ref, i, slice(0, 128)), dmix_ref[i], kt_ref, dk.ref, dv.ref, part_ref[i],
        )
        out.ref[2 * i : 2 * i + 2] = dqt.T.astype(BF16).reshape(2, 128, 128)
        blocks = slice(2 * i, 2 * i + 2)
        out.send((blocks,), (blocks, slice(256, 384)))
        dk.send((i,))
        dv.send((i,))


def add_body(dk, dv, back, out):
    next_ref, dk_ref, dv_ref = back.get(), dk.get(), dv.get()
    for b in range(HEADS):
        rows = slice((b % 2) * TOK, (b % 2 + 1) * TOK)
        out.ref[b, 0:128, :] = (dk_ref[b // 2, rows, :] + next_ref[b, 0:128, :].astype(F32)).astype(BF16)
        out.ref[b, 128:256, :] = (dv_ref[b // 2, rows, :] + next_ref[b, 128:256, :].astype(F32)).astype(BF16)
    out.send((), (slice(None), slice(384, 640)))


def final_body(recv, w, out, dq, dk, dv, gg):
    recv_ref = recv.get()
    for n, made in enumerate((dq, dk, dv)):
        for h in range(HEADS):
            made.ref[:, h * TOK : (h + 1) * TOK] = recv_ref[h, 256 + 128 * n : 384 + 128 * n, :]
        made.send()
    for h in range(HEADS):
        gg.ref[:, h * TOK : (h + 1) * TOK] = flip(recv_ref[h, 128:256, :])
    gg.send()
    w_ref = w.get()
    total = dot(flip(recv_ref[0, 0:128, :]), w_ref[0:TOK, :])
    for h in range(1, HEADS):
        total = total + dot(flip(recv_ref[h, 0:128, :]), w_ref[h * TOK : (h + 1) * TOK, :])
    out.ref[...] = total.astype(BF16)
    out.send()


def weight_body(recv, wg):
    recv_ref = recv.get()
    share = recv_ref[0].astype(F32)
    for n in range(1, HEADS):
        share = share + recv_ref[n].astype(F32)
    for b in range(8):
        wg.ref[:, 128 * b : 128 * b + 128] = share[4 * b : 4 * b + 4, :]
    wg.send()


def plane_exchange(blocks):
    return lax.all_to_all(blocks, PLANE_AXES, 0, 0, tiled=True)


def shards(sizes, queries, keys, values, gates, cotangent, segment, w_out):
    dp, planes = sizes
    q, k, v, gate, cot, seg = (a[0] for a in (queries, keys, values, gates, cotangent, segment))
    rows = shape((TOK, 1024), BF16)
    head = shape((TILES, 128, TILE), F32)
    head16 = shape((TILES, 128, TILE), BF16)
    share = shape((4, 1024), F32)
    grad = shape((TILES, TILE, 128), F32)
    vt = pltpu.VMEM((TILES, 128, TILE), BF16)
    acc = pltpu.VMEM((TILES, TILE, 128), F32)

    (packed,) = call(pack_body, "hhh", [shape((8, 384, 128), BF16)], 1 << 16)(q, k, v)
    recv = plane_exchange(packed)

    replica, plane = lax.axis_index("dp"), lax.axis_index("z")
    who = jnp.stack([replica, plane, lax.axis_index("x"), lax.axis_index("c")]).astype(jnp.int32)
    place = plane * PLANE
    users = jnp.arange(USERS, dtype=jnp.int32)[:, None]
    first = jnp.sum((seg[None, :] < users).astype(jnp.int32), axis=1)
    mine = lax.dynamic_slice_in_dim(seg, place, PLANE)
    start = jnp.sum(jnp.where(mine[None, :] == users, first[:, None], 0), axis=0) - place
    low = (start[::TILE] + PLANE) // TILE
    start = start.reshape(8, 128)
    (gd,) = call(dgated_body, "hhh", [shape((8, 256, 128), BF16)], 1 << 28)(cot, gate, w_out)

    low, cot_later = lax.optimization_barrier((low, cot))
    along = [lax.ppermute(cot_later, "x", [(i, (i - n) % 4) for i in range(4)]) for n in (1, 2, 3)]
    pair, gd, start, low, who, *along = lax.optimization_barrier((recv[:, 128:384], gd, start, low, who, *along))
    halo = lax.ppermute(pair, "z", [(i, i + 1) for i in range(planes - 1)])
    gd_recv = plane_exchange(gd)
    near = jnp.stack([cot, *along])
    part, qt = call(fwd_own_body, "shh", [head, head16], 1 << 29, [vt])(low, recv, start)
    halo, gd_recv, near, part = lax.optimization_barrier((halo, gd_recv, near, part))
    mate = lax.ppermute(near, "c", [(0, 1), (1, 0)])
    mixt, stats = call(fwd_halo_body, "shhhhh", [head, shape((8, 32, 128), F32)], 1 << 28, [vt], TIGHT, kept={1: (1, 32, 128)})(
        low, halo, start, qt, part, gd_recv
    )
    stats, near, mate = lax.optimization_barrier((stats, near, mate))
    stats = plane_exchange(stats)

    only_q = {6: ((slice(None), slice(0, 128)), (8, 128, 128))}
    far = shape((32, 1024), BF16)
    sent, dmix, dqt, back, own, *fars = call(
        middle_body, "sshhhhhhhhh",
        [shape((8, 640, 128), BF16), head16, head, shape((8, 256, 128), BF16), shape((32, 1024), F32), far, far, far],
        1 << 29, [vt, acc, acc, pltpu.VMEM((128, 1024), F32)], kept={0: (8, 256, 128)}, held=only_q,
    )(low, who, mixt, gd_recv, stats, halo, recv, start, qt, near, mate)
    back = lax.ppermute(back, "z", [(i, i - 1) for i in range(1, planes)])
    fars = [lax.ppermute(x, "dp", [(i, (i + n + 1) % dp) for i in range(dp)]) for n, x in enumerate(fars)]
    moved = shape((8, 32, 128), BF16)
    (moved,) = call(replica_sum_body, "hhhh", [moved], 1 << 16, [pltpu.VMEM((32, 1024), F32), pltpu.VMEM((8, 32, 128), F32)])(own, *fars)
    route = []
    for d in range(dp):
        for z in range(planes):
            for r in range(8):
                route.append(((d * planes + z) * 8 + r, (r // 2 * planes + (r % 2) * 4 + d) * 8 + z))

    sent, dk, dv = call(
        bwd_own_body, "shhhhha", [shape((8, 640, 128), BF16), grad, grad], 1 << 30, [vt], kept={0: (8, 128, 128)}
    )(low, recv, start, qt, dmix, dqt, sent)
    (sent,) = call(add_body, "hhha", [shape((8, 640, 128), BF16)], 1 << 20, (), TIGHT, kept={0: (8, 256, 128)})(dk, dv, back, sent)
    sent, moved = lax.optimization_barrier((sent, moved))
    moved = lax.ppermute(moved, ("dp", "z", "x", "c"), route)
    got = plane_exchange(sent)
    moved, got = lax.optimization_barrier((moved, got))
    shares = plane_exchange(moved)
    out, dq, dk, dv, gg = call(final_body, "hh", [rows] * 5, 1 << 28, (), ROOM)(got, w_out)
    (weight_grad,) = call(weight_body, "h", [share], 1 << 16, (), ROOM)(shares)
    return out[None], dq[None], dk[None], dv[None], gg[None], weight_grad


def solution(mesh):
    dp, seq = mesh.shape["dp"], mesh.shape["seq"]
    planes = seq // 8
    grid = Mesh(mesh.devices.reshape(dp, planes, 4, 2), ("dp", "z", "x", "c"))
    tokens = P("dp", ("z", "x", "c"), None)
    return jax.shard_map(
        functools.partial(shards, (dp, planes)),
        mesh=grid,
        in_specs=(tokens,) * 5 + (P("dp", None), P()),
        out_specs=(tokens,) * 5 + (P(("dp", "z", "x", "c"), None),),
        check_vma=False,
    )
```

```python
import functools
import math

import jax
import jax.numpy as jnp
from jax import lax
from jax.experimental import pallas as pl
from jax.experimental.pallas import tpu as pltpu
from jax.sharding import Mesh
from jax.sharding import PartitionSpec as P

HEADS = 8
EPS = 1e-05
USERS = 32
TOK = 128
PLANE = 1024
TILE = 256
TILES = PLANE // TILE
SCALE = 1.0 / math.sqrt(128.0)
F32 = jnp.float32
BF16 = jnp.bfloat16
PLANE_AXES = ("x", "c")
VMEM_LIMIT = 60 * 1024 * 1024
ROOM = 30 * 1024 * 1024
TIGHT = 62_300_000

NN = (((1,), (0,)), ((), ()))
NT = (((1,), (1,)), ((), ()))
TN = (((0,), (0,)), ((), ()))


def dot(a, b, dims=NN):
    return lax.dot_general(a, b, dims, preferred_element_type=F32)


def flip(block):
    return block.astype(F32).T.astype(BF16)


class Held:
    def __init__(self, ref, copy):
        self.ref, self.copy = ref, copy

    def get(self):
        if self.copy is not None:
            self.copy.wait()
            self.copy = None
        return self.ref


class Made:
    def __init__(self, ref, target, log):
        self.ref, self.target, self.log = ref, target, log

    def send(self, src=(), dst=None):
        where = src if dst is None else dst
        self.log((self.ref.at[src] if src != () else self.ref, self.target.at[where] if where != () else self.target))


def call(body, places, outs, flops, scratch=(), limit=VMEM_LIMIT, sends=16, kept=None, held=None):
    outs, kept, held = list(outs), dict(kept or {}), dict(held or {})

    def build(*args):
        staged = [n for n, place in enumerate(places) if place == "h"]
        shapes = [held[n][1] if n in held else args[n].shape for n in staged]

        def whole(*refs):
            refs = list(refs)
            given, refs = refs[: len(args)], refs[len(args) :]
            results, refs = refs[: len(outs)], refs[len(outs) :]
            here, refs = refs[: len(staged)], refs[len(staged) :]
            made, refs = refs[: len(outs)], refs[len(outs) :]
            in_sems, out_sems, extra = refs[0], refs[1], refs[2:]
            for m, n in enumerate(staged):
                source = given[n].at[held[n][0]] if n in held else given[n]
                copy = pltpu.make_async_copy(source, here[m], in_sems.at[m])
                copy.start()
                given[n] = Held(here[m], copy)
            sent = []

            def log(pair):
                copy = pltpu.make_async_copy(pair[0], pair[1], out_sems.at[len(sent)])
                copy.start()
                sent.append(copy)

            body(*(g for g, place in zip(given, places) if place != "a"), *(Made(v, t, log) for v, t in zip(made, results)), *extra)
            for n in staged:
                given[n].get()
            for copy in sent:
                copy.wait()

        moved = sum(a.size * a.dtype.itemsize for a in args) + sum(o.size * o.dtype.itemsize for o in outs)
        return pl.pallas_call(
            whole,
            out_shape=outs,
            in_specs=[pl.BlockSpec(memory_space=pltpu.SMEM if place == "s" else pltpu.HBM) for place in places],
            out_specs=[pl.BlockSpec(memory_space=pltpu.HBM)] * len(outs),
            input_output_aliases={places.index("a"): 0} if "a" in places else {},
            scratch_shapes=[pltpu.VMEM(dims, args[n].dtype) for dims, n in zip(shapes, staged)]
            + [pltpu.VMEM(kept.get(m, o.shape), o.dtype) for m, o in enumerate(outs)]
            + [pltpu.SemaphoreType.DMA((len(staged) + 1,)), pltpu.SemaphoreType.DMA((sends,))]
            + list(scratch),
            compiler_params=pltpu.CompilerParams(vmem_limit_bytes=limit),
            cost_estimate=pl.CostEstimate(flops=flops, bytes_accessed=moved, transcendentals=0),
        )(*args)

    return build


def shape(dims, dtype):
    return jax.ShapeDtypeStruct(dims, dtype)


def pack_body(q, k, v, out):
    for n, held in enumerate((q, k, v)):
        ref = held.get()
        rows = slice(n * TOK, (n + 1) * TOK)
        for h in range(HEADS):
            out.ref[h, rows, :] = ref[:, h * TOK : (h + 1) * TOK]
        out.send((slice(None), rows))


def dgated_body(cot, gate, w, out):
    gate_ref = gate.get()
    for h in range(HEADS):
        out.ref[h, 0:128, :] = flip(gate_ref[:, h * TOK : (h + 1) * TOK])
    cotangent, w_ref = cot.get()[...], w.get()
    for h in range(HEADS):
        out.ref[h, 128:256, :] = dot(w_ref[h * TOK : (h + 1) * TOK, :], cotangent, NT).astype(BF16)
    out.send()


def tile_of(ref, j, rows):
    return ref[pl.ds(2 * j, 2), rows, :].reshape(TILE, 128)


def tile_mask(start_ref, i, first_key):
    start = jnp.concatenate([start_ref[2 * i : 2 * i + 1, :], start_ref[2 * i + 1 : 2 * i + 2, :]], axis=1)
    key_place = first_key + lax.broadcasted_iota(jnp.int32, (TILE, TILE), 0)
    query_place = i * TILE + lax.broadcasted_iota(jnp.int32, (TILE, TILE), 1)
    return (key_place >= start) & (key_place <= query_place)


def sigmoid(s):
    return 1.0 / (1.0 + jnp.exp(-s))


def flip_tiles(ref, rows, tiles):
    for t in range(HEADS):
        tiles[t // 2, :, (t % 2) * TOK : (t % 2 + 1) * TOK] = flip(ref[t, rows, :])


def forward_tiles(i, low, high, first, keys_ref, key_rows, start_ref, qt, vt_ref, total):
    def step(j, acc):
        s = dot(tile_of(keys_ref, j, key_rows), qt) * SCALE
        mask = tile_mask(start_ref, i, first + j * TILE)
        w = jnp.where(mask, s * sigmoid(s), 0.0).astype(BF16)
        return acc + dot(vt_ref[j], w)

    return lax.fori_loop(low, high, step, total)


def fwd_own_body(low_ref, recv, start, mixt, qt, vt_ref):
    recv_ref, start_ref = recv.get(), start.get()
    flip_tiles(recv_ref, slice(0, 128), qt.ref)
    qt.send()
    flip_tiles(recv_ref, slice(256, 384), vt_ref)
    for i in range(TILES):
        low = jnp.maximum(low_ref[i] - TILES, 0)
        mixt.ref[i] = forward_tiles(
            i, low, i + 1, 0, recv_ref, slice(128, 256), start_ref, qt.ref[i], vt_ref, jnp.zeros((128, TILE), F32)
        )
        mixt.send((i,))


def fwd_halo_body(low_ref, halo, start, qt, part, gd, mixt, stats, vt_ref):
    halo_ref, start_ref = halo.get(), start.get()
    flip_tiles(halo_ref, slice(128, 256), vt_ref)
    qt_ref, part_ref, gd_ref = qt.get(), part.get(), gd.get()
    for i in range(TILES):
        mixt.ref[i] = forward_tiles(
            i, low_ref[i], TILES, -PLANE, halo_ref, slice(0, 128), start_ref, qt_ref[i], vt_ref, part_ref[i]
        )
        mixt.send((i,))
        for b in (2 * i, 2 * i + 1):
            mix = mixt.ref[i, :, (b % 2) * TOK : (b % 2 + 1) * TOK]
            dn = gd_ref[b, 0:128, :].astype(F32) * gd_ref[b, 128:256, :].astype(F32)
            mean = jnp.sum(mix, axis=0, keepdims=True) * (1.0 / 128.0)
            centred = mix - mean
            rows = (
                mean,
                jnp.sum(centred * centred, axis=0, keepdims=True),
                jnp.sum(dn, axis=0, keepdims=True),
                jnp.sum(dn * centred, axis=0, keepdims=True),
            )
            for k, row in enumerate(rows):
                stats.ref[0, 8 * k + b : 8 * k + b + 1, :] = row
    for d in range(HEADS):
        stats.send((0,), (d,))


def finish(mixt_ref, gd_ref, stats_ref, gate_out, dmix_ref):
    means = [stats_ref[h, 0:8, :] for h in range(HEADS)]
    mean = sum(means) * (1.0 / HEADS)
    square = sum(stats_ref[h, 8:16, :] for h in range(HEADS))
    square = square + 128.0 * sum((m - mean) * (m - mean) for m in means)
    inverse = lax.rsqrt(square * (1.0 / 1024.0) + EPS)
    dmean = sum(stats_ref[h, 16:24, :] for h in range(HEADS)) * (1.0 / 1024.0)
    cross = sum(stats_ref[h, 24:32, :] + (means[h] - mean) * stats_ref[h, 16:24, :] for h in range(HEADS))
    dcross = cross * inverse * (1.0 / 1024.0)
    for b in range(HEADS):
        cols = slice((b % 2) * TOK, (b % 2 + 1) * TOK)
        one = slice(b, b + 1)
        inv = inverse[one, :]
        normed = (mixt_ref[b // 2, :, cols] - mean[one, :]) * inv
        gate = gd_ref[b, 0:128, :].astype(F32)
        dgated = gd_ref[b, 128:256, :].astype(F32)
        gate_out[b, 0:128, :] = (normed * gate).astype(BF16)
        gate_out[b, 128:256, :] = (normed * dgated).astype(BF16)
        dmix_ref[b // 2, :, cols] = (inv * (dgated * gate - dmean[one, :] - normed * dcross[one, :])).astype(BF16)


def backward_tiles(i, low, high, first, keys_ref, key_rows, value_rows, start_ref, qt, q, dmt, kt_ref, dk_ref, dv_ref, total):
    def step(j, acc):
        s = dot(tile_of(keys_ref, j, key_rows), qt) * SCALE
        mask = tile_mask(start_ref, i, first + j * TILE)
        sig = sigmoid(s)
        w = jnp.where(mask, s * sig, 0.0).astype(BF16)
        dw = dot(tile_of(keys_ref, j, value_rows), dmt)
        ds = jnp.where(mask, dw * (sig * (1.0 + s * (1.0 - sig))) * SCALE, 0.0).astype(BF16)
        dv_ref[j] += dot(w, dmt, NT)
        dk_ref[j] += dot(ds, q)
        return acc + dot(kt_ref[j], ds)

    return lax.fori_loop(low, high, step, total)


def middle_body(
    low_ref, who_ref, mixt, gd, stats, halo, recv, start, qt, near, mate, sent, dmix, dqt, back, own, far1, far2, far3, kt_ref, dk_ref, dv_ref, all_ref
):
    finish(mixt.get(), gd.get(), stats.get(), sent.ref, dmix.ref)
    sent.send((), (slice(None), slice(0, 256)))
    dmix.send()
    halo_ref, recv_ref, start_ref, qt_ref = halo.get(), recv.get(), start.get(), qt.get()
    flip_tiles(halo_ref, slice(0, 128), kt_ref)
    dk_ref[...] = jnp.zeros_like(dk_ref)
    dv_ref[...] = jnp.zeros_like(dv_ref)
    for i in range(TILES):
        dqt.ref[i] = backward_tiles(
            i, low_ref[i], TILES, -PLANE, halo_ref, slice(0, 128), slice(128, 256), start_ref, qt_ref[i],
            tile_of(recv_ref, i, slice(0, 128)), dmix.ref[i], kt_ref, dk_ref, dv_ref, jnp.zeros((128, TILE), F32),
        )
    dqt.send()
    for j in range(TILES):
        back.ref[2 * j : 2 * j + 2, 0:128, :] = dk_ref[j].astype(BF16).reshape(2, 128, 128)
        back.ref[2 * j : 2 * j + 2, 128:256, :] = dv_ref[j].astype(BF16).reshape(2, 128, 128)
    back.send()
    near_ref, mate_ref = near.get(), mate.get()
    total = jnp.zeros((128, 1024), F32)
    for n in range(4):
        first = 2 * jnp.bitwise_and(who_ref[2] + n, 3)
        total = total + dot(sent.ref[first + who_ref[3], 0:128, :], near_ref[n])
        total = total + dot(sent.ref[first + 1 - who_ref[3], 0:128, :], mate_ref[n])
    all_ref[...] = total
    for n, made in enumerate((own, far1, far2, far3)):
        block = jnp.bitwise_and(who_ref[0] + n, 3)
        made.ref[...] = all_ref[pl.ds(pl.multiple_of(32 * block, 32), 32), :].astype(made.ref.dtype)
        made.send()


def replica_sum_body(own, got1, got2, got3, out, total_ref, moved_ref):
    total = own.get()[...]
    for got in (got1, got2, got3):
        total = total + got.get()[...].astype(F32)
    total_ref[...] = total
    for j in range(8):
        for b in range(8):
            moved_ref[j, 4 * b : 4 * b + 4, :] = total_ref[4 * j : 4 * j + 4, 128 * b : 128 * b + 128]
    out.ref[...] = moved_ref[...].astype(BF16)
    out.send()


def bwd_own_body(low_ref, recv, start, qt, dmix, part, out, dk, dv, kt_ref):
    recv_ref, start_ref = recv.get(), start.get()
    flip_tiles(recv_ref, slice(128, 256), kt_ref)
    dk.ref[...] = jnp.zeros_like(dk.ref)
    dv.ref[...] = jnp.zeros_like(dv.ref)
    qt_ref, dmix_ref, part_ref = qt.get(), dmix.get(), part.get()
    for i in range(TILES - 1, -1, -1):
        low = jnp.maximum(low_ref[i] - TILES, 0)
        dqt = backward_tiles(
            i, low, i + 1, 0, recv_ref, slice(128, 256), slice(256, 384), start_ref, qt_ref[i],
            tile_of(recv_ref, i, slice(0, 128)), dmix_ref[i], kt_ref, dk.ref, dv.ref, part_ref[i],
        )
        out.ref[2 * i : 2 * i + 2] = dqt.T.astype(BF16).reshape(2, 128, 128)
        blocks = slice(2 * i, 2 * i + 2)
        out.send((blocks,), (blocks, slice(256, 384)))
        dk.send((i,))
        dv.send((i,))


def add_body(dk, dv, back, out):
    next_ref, dk_ref, dv_ref = back.get(), dk.get(), dv.get()
    for b in range(HEADS):
        rows = slice((b % 2) * TOK, (b % 2 + 1) * TOK)
        out.ref[b, 0:128, :] = (dk_ref[b // 2, rows, :] + next_ref[b, 0:128, :].astype(F32)).astype(BF16)
        out.ref[b, 128:256, :] = (dv_ref[b // 2, rows, :] + next_ref[b, 128:256, :].astype(F32)).astype(BF16)
    out.send((), (slice(None), slice(384, 640)))


def final_body(recv, w, out, dq, dk, dv, gg):
    recv_ref = recv.get()
    for n, made in enumerate((dq, dk, dv)):
        for h in range(HEADS):
            made.ref[:, h * TOK : (h + 1) * TOK] = recv_ref[h, 256 + 128 * n : 384 + 128 * n, :]
        made.send()
    for h in range(HEADS):
        gg.ref[:, h * TOK : (h + 1) * TOK] = flip(recv_ref[h, 128:256, :])
    gg.send()
    w_ref = w.get()
    total = dot(flip(recv_ref[0, 0:128, :]), w_ref[0:TOK, :])
    for h in range(1, HEADS):
        total = total + dot(flip(recv_ref[h, 0:128, :]), w_ref[h * TOK : (h + 1) * TOK, :])
    out.ref[...] = total.astype(BF16)
    out.send()


def weight_body(recv, wg):
    recv_ref = recv.get()
    share = recv_ref[0].astype(F32)
    for n in range(1, HEADS):
        share = share + recv_ref[n].astype(F32)
    for b in range(8):
        wg.ref[:, 128 * b : 128 * b + 128] = share[4 * b : 4 * b + 4, :]
    wg.send()


def plane_exchange(blocks):
    return lax.all_to_all(blocks, PLANE_AXES, 0, 0, tiled=True)


def shards(sizes, queries, keys, values, gates, cotangent, segment, w_out):
    dp, planes = sizes
    q, k, v, gate, cot, seg = (a[0] for a in (queries, keys, values, gates, cotangent, segment))
    rows = shape((TOK, 1024), BF16)
    head = shape((TILES, 128, TILE), F32)
    head16 = shape((TILES, 128, TILE), BF16)
    share = shape((4, 1024), F32)
    grad = shape((TILES, TILE, 128), F32)
    vt = pltpu.VMEM((TILES, 128, TILE), BF16)
    acc = pltpu.VMEM((TILES, TILE, 128), F32)

    (packed,) = call(pack_body, "hhh", [shape((8, 384, 128), BF16)], 1 << 16)(q, k, v)
    recv = plane_exchange(packed)

    replica, plane = lax.axis_index("dp"), lax.axis_index("z")
    who = jnp.stack([replica, plane, lax.axis_index("x"), lax.axis_index("c")]).astype(jnp.int32)
    place = plane * PLANE
    users = jnp.arange(USERS, dtype=jnp.int32)[:, None]
    first = jnp.sum((seg[None, :] < users).astype(jnp.int32), axis=1)
    mine = lax.dynamic_slice_in_dim(seg, place, PLANE)
    start = jnp.sum(jnp.where(mine[None, :] == users, first[:, None], 0), axis=0) - place
    low = (start[::TILE] + PLANE) // TILE
    start = start.reshape(8, 128)
    (gd,) = call(dgated_body, "hhh", [shape((8, 256, 128), BF16)], 1 << 28)(cot, gate, w_out)

    low, cot_later = lax.optimization_barrier((low, cot))
    along = [lax.ppermute(cot_later, "x", [(i, (i - n) % 4) for i in range(4)]) for n in (1, 2, 3)]
    pair, gd, start, low, who = lax.optimization_barrier((recv[:, 128:384], gd, start, low, who))
    halo = lax.ppermute(pair, "z", [(i, i + 1) for i in range(planes - 1)])
    gd_recv = plane_exchange(gd)
    part, qt = call(fwd_own_body, "shh", [head, head16], 1 << 29, [vt])(low, recv, start)
    part, *along = lax.optimization_barrier((part, *along))
    near = jnp.stack([cot, *along])
    halo, gd_recv, near, part = lax.optimization_barrier((halo, gd_recv, near, part))
    mate = lax.ppermute(near, "c", [(0, 1), (1, 0)])
    mixt, stats = call(fwd_halo_body, "shhhhh", [head, shape((8, 32, 128), F32)], 1 << 28, [vt], TIGHT, kept={1: (1, 32, 128)})(
        low, halo, start, qt, part, gd_recv
    )
    stats, near, mate = lax.optimization_barrier((stats, near, mate))
    stats = plane_exchange(stats)

    only_q = {6: ((slice(None), slice(0, 128)), (8, 128, 128))}
    far = shape((32, 1024), BF16)
    sent, dmix, dqt, back, own, *fars = call(
        middle_body, "sshhhhhhhhh",
        [shape((8, 640, 128), BF16), head16, head, shape((8, 256, 128), BF16), shape((32, 1024), F32), far, far, far],
        1 << 29, [vt, acc, acc, pltpu.VMEM((128, 1024), F32)], kept={0: (8, 256, 128)}, held=only_q,
    )(low, who, mixt, gd_recv, stats, halo, recv, start, qt, near, mate)
    back = lax.ppermute(back, "z", [(i, i - 1) for i in range(1, planes)])
    fars = [lax.ppermute(x, "dp", [(i, (i + n + 1) % dp) for i in range(dp)]) for n, x in enumerate(fars)]
    moved = shape((8, 32, 128), BF16)
    (moved,) = call(replica_sum_body, "hhhh", [moved], 1 << 16, [pltpu.VMEM((32, 1024), F32), pltpu.VMEM((8, 32, 128), F32)])(own, *fars)
    route = []
    for d in range(dp):
        for z in range(planes):
            for r in range(8):
                route.append(((d * planes + z) * 8 + r, (r // 2 * planes + (r % 2) * 4 + d) * 8 + z))

    sent, dk, dv = call(
        bwd_own_body, "shhhhha", [shape((8, 640, 128), BF16), grad, grad], 1 << 30, [vt], kept={0: (8, 128, 128)}
    )(low, recv, start, qt, dmix, dqt, sent)
    (sent,) = call(add_body, "hhha", [shape((8, 640, 128), BF16)], 1 << 20, (), TIGHT, kept={0: (8, 256, 128)})(dk, dv, back, sent)
    sent, moved = lax.optimization_barrier((sent, moved))
    moved = lax.ppermute(moved, ("dp", "z", "x", "c"), route)
    got = plane_exchange(sent)
    moved, got = lax.optimization_barrier((moved, got))
    shares = plane_exchange(moved)
    out, dq, dk, dv, gg = call(final_body, "hh", [rows] * 5, 1 << 28, (), ROOM)(got, w_out)
    (weight_grad,) = call(weight_body, "h", [share], 1 << 16, (), ROOM)(shares)
    return out[None], dq[None], dk[None], dv[None], gg[None], weight_grad


def solution(mesh):
    dp, seq = mesh.shape["dp"], mesh.shape["seq"]
    planes = seq // 8
    grid = Mesh(mesh.devices.reshape(dp, planes, 4, 2), ("dp", "z", "x", "c"))
    tokens = P("dp", ("z", "x", "c"), None)
    return jax.shard_map(
        functools.partial(shards, (dp, planes)),
        mesh=grid,
        in_specs=(tokens,) * 5 + (P("dp", None), P()),
        out_specs=(tokens,) * 5 + (P(("dp", "z", "x", "c"), None),),
        check_vma=False,
    )
```
